32 devices in a mesh: grp: 2 (over y), pos: 4 (over z), read: 2 (over x), head: 2 (over core).
Axes of the slice: x: 2, y: 2, z: 4, core: 2. Of those that a mesh axis runs over, the one named last changes fastest.
Arguments:
- latents: bfloat16 [32, 128, 512], P(('grp', 'pos')), parts along dimension 0, may hold values from -6 to 6
- read_tokens: bfloat16 [32, 8, 512, 512], P(('grp', 'pos'), 'read'), parts along dimension 0, may hold values from -166.1 to 166.1
- band_start: int32 [32, 8], P(('grp', 'pos'), 'read'), parts along dimension 0, may hold values from 0 to 511
- coverage: int32 [32, 8], P(('grp', 'pos'), 'read'), parts along dimension 0, may hold values from 1 to 512, as said below
- present: int32 [32, 8], P(('grp', 'pos'), 'read'), parts along dimension 0, may hold values from 0 to 1, as said below
- pattern: int32 [32, 16], P(('grp', 'pos')), parts along dimension 0, may hold values from 0 to 1, as said below
- cross_query: bfloat16 [512, 512], P(None, 'head'), may hold values from -0.25 to 0.25
- cross_key: bfloat16 [512, 512], P(None, 'head'), may hold values from -0.25 to 0.25
- cross_value: bfloat16 [512, 512], P(None, 'head'), may hold values from -0.25 to 0.25
- cross_out: bfloat16 [512, 512], P('head'), may hold values from -0.25 to 0.25
- self_query: bfloat16 [512, 512], P(None, 'head'), may hold values from -3.1 to 3.1
- self_key: bfloat16 [512, 512], P(None, 'head'), may hold values from -0.25 to 0.25
- self_value: bfloat16 [512, 512], P(None, 'head'), may hold values from -0.25 to 0.25
- self_out: bfloat16 [512, 512], P('head'), may hold values from -0.25 to 0.25
Outputs:
- latents_out: bfloat16 [32, 128, 512], P(('grp', 'pos'), 'read', 'head'), parts along dimension 0
The draws below stay inside these ranges and needn't reach their ends.
There are 2 independent parts, one for each index of `grp`. The reference program is written for one: setup_inputs(seed, part) draws one part's arguments, and reference() takes and returns one part's arrays. A program takes and returns all parts, laid end to end along the dimension named above; an argument that names none is the same for every part. Nothing has to cross between parts.
Inputs may be any that keep to these rules, and one draw needn't show every extreme that they name: band_start + coverage <= 512 everywhere. Read 0 is present in every segment. pattern[s, s] = 1; pattern[s, t] may be 1 only where the distance of s and t is a power of two.
All inputs are finite; a program needn't handle non-finite values.
Results may differ from the reference program's by a relative error of at most 0.015.
The reference program's roundings to bfloat16 on the way count: a program that leaves them out, or rounds other values in their place, can miss the bound.
Values may be sent and summed in bfloat16 or wider, within the bound.
No kernel may reach another device: no remote copies, remote signals or barrier semaphores. Data moves between devices by JAX's collectives and lax.ppermute only.
A program may use at most 64 MiB of HBM per device.

```python
import math
import jax
import jax.numpy as jnp
from jax import lax

D = 512
HEADS = 8
HD = 64
LAT = 128
SEGLEN = 512
SEGS = 16
READS = 8


def band_pair(key):
    base_key = jax.random.fold_in(key, 101)
    start_key, length_key = jax.random.split(base_key)
    starts = jax.random.randint(start_key, (SEGS, READS), 0, SEGLEN // 2, dtype=jnp.int32)
    starts = starts.at[0, 0].set(0).at[0, 1].set(SEGLEN - 1)
    room_left = SEGLEN - starts
    coins = jax.random.randint(length_key, (SEGS, READS), 0, 1 << 20, dtype=jnp.int32)
    lengths = room_left - coins % ((room_left + 1) // 2)
    lengths = lengths.at[0, 0].set(SEGLEN)
    return (starts, lengths)


def draw_band_start(key, part):
    return band_pair(key)[0]


def draw_coverage(key, part):
    return band_pair(key)[1]


def draw_present(key, part):
    coins = jax.random.randint(jax.random.fold_in(key, 202), (SEGS, READS), 0, 4, dtype=jnp.int32)
    flags = (coins > 0).astype(jnp.int32)
    return flags.at[:, 0].set(1)


def draw_pattern(key, part):
    row_index = jnp.arange(SEGS, dtype=jnp.int32)[:, None]
    column_index = jnp.arange(SEGS, dtype=jnp.int32)[None, :]
    distance = jnp.abs(column_index - row_index)
    power_two = (distance > 0) & (jnp.bitwise_and(distance, distance - 1) == 0)
    coins = jax.random.randint(jax.random.fold_in(key, 303), (SEGS, SEGS), 0, 2, dtype=jnp.int32)
    return jnp.where(distance == 0, 1, jnp.where(power_two, coins, 0)).astype(jnp.int32)


def draw_read_tokens(key, part):
    first_key = jax.random.fold_in(jax.random.fold_in(key, 404), 0)
    full_shape = (SEGS, READS, SEGLEN, D)
    base_value = jnp.clip(jax.random.normal(first_key, full_shape, jnp.float32), -6.0, 6.0)
    return base_value.astype(jnp.bfloat16)


def draw_self_query(key, part):
    first_key = jax.random.fold_in(jax.random.fold_in(key, 505), 0)
    base_value = jnp.clip(jax.random.normal(first_key, (D, D), jnp.float32), -6.0, 6.0)
    return jnp.clip(base_value / math.sqrt(D), -3.05, 3.05).astype(jnp.bfloat16)


def levels(own_key, extent, shards, least, top_value):
    def one(dim, shards_of):
        heights = jax.random.uniform(jax.random.fold_in(jax.random.fold_in(own_key, 6), dim), (shards_of,), jnp.float32, least / len(shards), top_value / len(shards))
        return jnp.repeat(jnp.exp(heights), extent[dim] // shards_of).reshape((-1,) + (1,) * (len(extent) - dim - 1))

    factor_of = one(*shards[0])
    for cut in shards[1:]:
        factor_of = factor_of * one(*cut)
    return factor_of


def normal_values(stream_key, shape, deviation, most, shards=(), kind=jnp.bfloat16):
    factor_of = levels(stream_key, shape, shards, -0.22, 0.18) if shards else 1.0
    array = jax.random.normal(stream_key, shape, jnp.float32) * deviation * factor_of
    return jnp.minimum(jnp.maximum(array, -most), most).astype(kind)


def setup_inputs(seed: int = 0, part: int = 0) -> dict:
    splits = jax.random.split(jax.random.key(seed), 15)
    part_keys = jax.random.split(jax.random.fold_in(splits[14], part), 15)
    return {
        "latents": normal_values(part_keys[0], (SEGS, LAT, D), 1.0, 6.0, ((0, 4),)),
        "read_tokens": draw_read_tokens(jax.random.fold_in(jax.random.fold_in(splits[14], part), 71), part),
        "band_start": draw_band_start(jax.random.fold_in(jax.random.fold_in(splits[14], part), 71), part),
        "coverage": draw_coverage(jax.random.fold_in(jax.random.fold_in(splits[14], part), 71), part),
        "present": draw_present(jax.random.fold_in(jax.random.fold_in(splits[14], part), 71), part),
        "pattern": draw_pattern(jax.random.fold_in(jax.random.fold_in(splits[14], part), 71), part),
        "cross_query": normal_values(splits[6], (D, D), D ** -0.5, 0.25, ((1, 2),)),
        "cross_key": normal_values(splits[7], (D, D), D ** -0.5, 0.25, ((1, 2),)),
        "cross_value": normal_values(splits[8], (D, D), D ** -0.5, 0.25, ((1, 2),)),
        "cross_out": normal_values(splits[9], (D, D), D ** -0.5, 0.25, ((0, 2),)),
        "self_query": draw_self_query(jax.random.fold_in(splits[14], 71), part),
        "self_key": normal_values(splits[11], (D, D), D ** -0.5, 0.25, ((1, 2),)),
        "self_value": normal_values(splits[12], (D, D), D ** -0.5, 0.25, ((1, 2),)),
        "self_out": normal_values(splits[13], (D, D), D ** -0.5, 0.25, ((0, 2),)),
    }


EPSILON = 1e-06
NEGATIVE_FILL = -1e+30

def rms_rows(values):
    return values * lax.rsqrt(lax.optimization_barrier(jnp.mean(values * values, axis=-1, keepdims=True)) + EPSILON)

def rounded(values):
    return lax.optimization_barrier(values.astype(jnp.bfloat16))

def project(input_rows, weight):
    flat_rows = input_rows.reshape(-1, input_rows.shape[-1])
    product = jnp.dot(flat_rows, weight, preferred_element_type=jnp.float32)
    return product.reshape(input_rows.shape[:-1] + (weight.shape[1],))

def attend(segment_query, key_rows, value_rows, live_mask):
    scores = jnp.einsum('qhd,khd->qhk', segment_query.astype(jnp.float32), key_rows.astype(jnp.float32))
    scores = jnp.where(live_mask[None, None, :], scores, NEGATIVE_FILL)
    row_max = lax.optimization_barrier(jnp.max(scores, axis=-1, keepdims=True))
    weights = jnp.where(live_mask[None, None, :], jnp.exp(scores - row_max), 0.0)
    row_total = lax.optimization_barrier(jnp.sum(weights, axis=-1))
    mixed = jnp.einsum('qhk,khd->qhd', rounded(weights).astype(jnp.float32), value_rows.astype(jnp.float32))
    return (mixed / row_total[..., None]).astype(jnp.bfloat16)

def reference(latents, read_tokens, band_start, coverage, present, pattern, cross_query, cross_key, cross_value, cross_out, self_query, self_key, self_value, self_out):
    score_scale = HD ** (-0.5)
    latent_float = latents.astype(jnp.float32)
    normed = rounded(rms_rows(latent_float))
    query_rows = rounded(project(normed, cross_query) * score_scale).reshape(SEGS, LAT, HEADS, HD)
    positions = jnp.arange(SEGLEN, dtype=jnp.int32)

    def cross_segment(segment_item):
        segment_query, tokens, starts, lengths, flags = segment_item
        key_rows = rounded(project(tokens, cross_key)).reshape(READS * SEGLEN, HEADS, HD)
        value_rows = rounded(project(tokens, cross_value)).reshape(READS * SEGLEN, HEADS, HD)
        live_mask = (positions[None, :] >= starts[:, None]) & (positions[None, :] < (starts + lengths)[:, None]) & (flags[:, None] > 0)
        return attend(segment_query, key_rows, value_rows, live_mask.reshape(-1)).reshape(LAT, D)
    attended = lax.map(cross_segment, (query_rows, read_tokens, band_start, coverage, present))
    hidden_state = latent_float + project(attended, cross_out)
    second_normed = rounded(rms_rows(hidden_state))
    self_rows = rounded(project(second_normed, self_query) * score_scale).reshape(SEGS, LAT, HEADS, HD)
    self_keys = rounded(project(second_normed, self_key)).reshape(SEGS * LAT, HEADS, HD)
    self_values = rounded(project(second_normed, self_value)).reshape(SEGS * LAT, HEADS, HD)

    def self_segment(segment_item):
        segment_query, partner_row = segment_item
        live_mask = jnp.repeat(partner_row > 0, LAT)
        return attend(segment_query, self_keys, self_values, live_mask).reshape(LAT, D)
    self_mixed = lax.map(self_segment, (self_rows, pattern))
    return (hidden_state + project(self_mixed, self_out)).astype(jnp.bfloat16)
```

```python
import functools

import jax
import jax.numpy as jnp
from jax import lax
from jax.experimental import pallas as pl
from jax.experimental.pallas import tpu as pltpu
from jax.sharding import PartitionSpec as P

HD = 64
EPSILON = 1e-06
NEG = -1e30
CHUNK = 256
STATS = 128
ROWS = 16
F32 = jnp.float32
BF16 = jnp.bfloat16


def nt_dot(left, right):
    return lax.dot_general(left, right, (((1,), (1,)), ((), ())), preferred_element_type=F32)


def mm(left, right):
    return jnp.dot(left, right, preferred_element_type=F32)


def rms_rows(values):
    return values * lax.rsqrt(jnp.mean(values * values, axis=-1, keepdims=True) + EPSILON)


def spread_queries(query, heads, target):
    rows, width = query.shape
    column_head = lax.broadcasted_iota(jnp.int32, (rows, width), 1) // HD
    for head in range(heads):
        target[head * rows : (head + 1) * rows, :] = jnp.where(
            column_head == head, query.astype(F32), 0.0
        ).astype(BF16)


def tile_fold(values, combine):
    folded = values[:, :128]
    for tile in range(1, values.shape[1] // 128):
        folded = combine(folded, values[:, tile * 128 : (tile + 1) * 128])
    return folded


def attend(chunks, chunk_scores, value_of, scratch):
    score_buf, max_buf, total_buf, acc = scratch
    max_buf[...] = jnp.full(max_buf.shape, NEG, F32)
    total_buf[...] = jnp.zeros(total_buf.shape, F32)
    acc[...] = jnp.zeros(acc.shape, F32)

    def first(chunk, carry):
        scores = chunk_scores(chunk)
        score_buf[chunk] = scores
        max_buf[...] = jnp.maximum(max_buf[...], tile_fold(scores, jnp.maximum))
        return carry

    lax.fori_loop(0, chunks, first, 0)
    row_max = jnp.max(max_buf[...], axis=1, keepdims=True)

    def second(chunk, carry):
        weights = jnp.exp(score_buf[chunk] - row_max)
        total_buf[...] += tile_fold(weights, jnp.add)
        acc[...] += mm(weights.astype(BF16), value_of(chunk))
        return carry

    lax.fori_loop(0, chunks, second, 0)
    return row_max, jnp.sum(total_buf[...], axis=1, keepdims=True)


def emit(segment, row_max, row_total, acc, heads, full, stat_full, own_ref, own_stat_ref, sends):
    readers = len(sends) + 1
    rows, width = full.shape
    part = rows // readers
    lane = lax.broadcasted_iota(jnp.int32, (rows, 128), 1)
    for tile in range(width // 128):
        low, high = 2 * tile, 2 * tile + 1
        cols = slice(tile * 128, (tile + 1) * 128)
        full[:, cols] = jnp.where(
            lane < HD,
            acc[low * rows : (low + 1) * rows, cols],
            acc[high * rows : (high + 1) * rows, cols],
        )
    stats = jnp.zeros((rows, STATS), F32)
    place = 0
    for source in (row_max, row_total):
        for head in range(heads):
            left = source[head * rows : (head + 1) * rows]
            for step in range(3):
                piece = left.astype(BF16).astype(F32)
                stats = jnp.where(lane == place, piece, stats)
                left = left - piece
                place += 1
    stat_full[...] = stats
    reader = lax.axis_index("read")
    for step in range(readers):
        first = pl.multiple_of(lax.rem(reader + step, readers) * part, part)
        if step == 0:
            own_ref[segment] = full[pl.ds(first, part), :]
            own_stat_ref[segment] = stat_full[pl.ds(first, part), :].astype(BF16)
        else:
            sends[step - 1][segment, :, :width] = full[pl.ds(first, part), :].astype(BF16)
            sends[step - 1][segment, :, width:] = stat_full[pl.ds(first, part), :].astype(BF16)


def cross_kernel(
    readers, start_ref, cov_ref, present_ref, lat_ref, tok_ref, wq_ref, wk_ref, wv_ref, *rest
):
    own_ref, own_stat_ref = rest[:2]
    sends = rest[2 : 1 + readers]
    (token_buf, query_buf, spread, score_buf, value_buf, max_buf, total_buf, acc, full, stat_full,
     sems) = rest[1 + readers :]
    segs, lat_rows, width = lat_ref.shape
    reads = tok_ref.shape[1]
    local = wq_ref.shape[1]
    heads = local // HD

    def span(segment, read):
        start = start_ref[segment, read]
        length = cov_ref[segment, read]
        first = (start // ROWS) * ROWS
        last = ((start + length + ROWS - 1) // ROWS) * ROWS
        live = present_ref[segment, read] > 0
        return start - first, jnp.where(live, length, 0), first, jnp.where(live, last - first, 0)

    for segment in range(segs):
        offset = jnp.int32(0)
        for read in range(reads):
            lead, length, first, rows = span(segment, read)

            @pl.when(rows > 0)
            def _(segment=segment, read=read, offset=offset, first=first, rows=rows):
                pltpu.make_async_copy(
                    tok_ref.at[segment, read, pl.ds(pl.multiple_of(first, ROWS), rows), :],
                    token_buf.at[segment, pl.ds(pl.multiple_of(offset, ROWS), rows), :],
                    sems.at[segment],
                ).start()

            offset = offset + rows
        blocks = (((offset + CHUNK - 1) // CHUNK) * CHUNK - offset) // ROWS

        def clear(step, carry, segment=segment, offset=offset):
            token_buf[segment, pl.ds(pl.multiple_of(offset + step * ROWS, ROWS), ROWS), :] = (
                jnp.zeros((ROWS, width), BF16)
            )
            return carry

        lax.fori_loop(0, blocks, clear, 0)

    for segment in range(segs):
        normed = rms_rows(lat_ref[segment].astype(F32)).astype(BF16)
        query_buf[segment] = (mm(normed, wq_ref[...]) * (HD ** (-0.5))).astype(BF16)

    def one_segment(segment, carry):
        spread_queries(query_buf[segment], heads, spread)
        offset = jnp.int32(0)
        bounds = []
        for read in range(reads):
            lead, length, first, rows = span(segment, read)
            bounds.append((offset + lead, offset + lead + length))
            offset = offset + rows

        @pl.when(offset > 0)
        def _():
            landed = token_buf.at[segment, pl.ds(0, offset), :]
            pltpu.make_async_copy(landed, landed, sems.at[segment]).wait()

        def chunk_scores(chunk):
            base = pl.multiple_of(chunk * CHUNK, CHUNK)
            tokens = token_buf[segment, pl.ds(base, CHUNK), :]
            keys = mm(tokens, wk_ref[...]).astype(BF16)
            value_buf[pl.ds(base, CHUNK), :] = mm(tokens, wv_ref[...]).astype(BF16)
            place = base + lax.broadcasted_iota(jnp.int32, (1, CHUNK), 1)
            live = jnp.zeros((1, CHUNK), jnp.bool_)
            for low, high in bounds:
                live = live | ((place >= low) & (place < high))
            return jnp.where(live, nt_dot(spread[...], keys), NEG)

        def value_of(chunk):
            return value_buf[pl.ds(pl.multiple_of(chunk * CHUNK, CHUNK), CHUNK), :]

        chunks = (offset + CHUNK - 1) // CHUNK
        row_max, row_total = attend(
            chunks, chunk_scores, value_of, (score_buf, max_buf, total_buf, acc)
        )
        emit(
            segment, row_max, row_total, acc, heads, full, stat_full, own_ref, own_stat_ref, sends
        )
        return carry

    lax.fori_loop(0, segs, one_segment, 0)


def combine_kernel(own_ref, stat_ref, *rest):
    received, out_ref = rest[:-1], rest[-1]
    width = own_ref.shape[1]
    heads = width // HD
    lane = lax.broadcasted_iota(jnp.int32, (STATS, width), 0)
    head = lax.broadcasted_iota(jnp.int32, (STATS, width), 1) // HD
    pick_max = ((lane // 3) == head).astype(F32).astype(BF16)
    pick_total = ((lane // 3) == head + heads).astype(F32).astype(BF16)
    parts = [(own_ref[...], stat_ref[...])]
    for ref in received:
        parts.append((ref[:, :width].astype(F32), ref[:, width:]))
    maxima = [mm(stat, pick_max) for _, stat in parts]
    totals = [mm(stat, pick_total) for _, stat in parts]
    joint = functools.reduce(jnp.maximum, maxima)
    factors = [jnp.exp(value - joint) for value in maxima]
    total = sum(value * factor for value, factor in zip(totals, factors))
    mixed = sum(part[0] * factor for part, factor in zip(parts, factors))
    out_ref[...] = (mixed / total).astype(BF16)


def hidden_kernel(
    lat_ref, own_ref, other_ref, wo_ref, wp_ref, wq_ref, hid_ref, norm_ref, query_ref
):
    segs, lat_rows, width = lat_ref.shape
    part = own_ref.shape[0] // segs
    first = pl.multiple_of(lax.axis_index("read") * part, part)
    delta = mm(own_ref[...], wo_ref[...]) + mm(other_ref[...], wp_ref[...])
    for segment in range(segs):
        rows = slice(segment * part, (segment + 1) * part)
        hid_ref[rows, :] = lat_ref[segment, pl.ds(first, part), :].astype(F32) + delta[rows]
    normed = rms_rows(hid_ref[...]).astype(BF16)
    norm_ref[...] = normed
    query_ref[...] = (mm(normed, wq_ref[...]) * (HD ** (-0.5))).astype(BF16)


def self_kernel(readers, steps, offsets, pattern_ref, wk_ref, wv_ref, *rest):
    queries = rest[:readers]
    count = 1 + 2 * len(steps)
    blocks = rest[readers : readers + count]
    rest = rest[readers + count :]
    own_ref, own_stat_ref = rest[:2]
    sends = rest[2 : 1 + readers]
    (query_buf, spread, key_all, value_all, key_buf, value_buf, score_buf, max_buf, total_buf, acc,
     full, stat_full) = rest[1 + readers :]
    segs = own_ref.shape[0]
    part = own_ref.shape[1]
    local = wk_ref.shape[1]
    heads = local // HD
    seg_total = pattern_ref.shape[1]
    reader = lax.axis_index("read")
    core = lax.axis_index("head")
    group = lax.axis_index("pos")
    size = segs * part

    key_buf[...] = jnp.zeros(key_buf.shape, BF16)
    value_buf[...] = jnp.zeros(value_buf.shape, BF16)
    for index, block in enumerate(blocks):
        if index == 0:
            slot = 0
        else:
            pair = (index - 1) // 2
            slot = 1 + 2 * pair + (core if index % 2 == 1 else 1 - core)
        place = pl.ds(pl.multiple_of(slot * size, size), size)
        key_all[place, :] = mm(block[...], wk_ref[...]).astype(BF16)
        value_all[place, :] = mm(block[...], wv_ref[...]).astype(BF16)
    for step in range(readers):
        first = pl.multiple_of(lax.rem(reader + readers - step, readers) * part, part)
        for segment in range(segs):
            query_buf[segment, pl.ds(first, part), :] = queries[step][
                segment * part : (segment + 1) * part, :
            ]

    for segment in range(segs):
        spread_queries(query_buf[segment], heads, spread)
        live = jnp.int32(0)
        for offset in offsets:
            block_step = (segment + offset) // segs
            inner = (segment + offset) % segs
            if block_step == 0:
                slot = 0
            else:
                slot = 1 + 2 * steps.index(abs(block_step)) + (1 if block_step > 0 else 0)
            target = group * segs + segment + offset
            inside = (target >= 0) & (target < seg_total)
            flag = pattern_ref[segment, jnp.clip(target, 0, seg_total - 1)]
            chosen = inside & (flag > 0)
            source = (slot * segs + inner) * part

            @pl.when(chosen)
            def _(live=live, source=source):
                place = pl.ds(pl.multiple_of(live * part, part), part)
                key_buf[place, :] = key_all[source : source + part, :]
                value_buf[place, :] = value_all[source : source + part, :]

            live = live + chosen.astype(jnp.int32)

        def chunk_scores(chunk, live=live):
            base = pl.multiple_of(chunk * CHUNK, CHUNK)
            keys = key_buf[pl.ds(base, CHUNK), :]
            place = base + lax.broadcasted_iota(jnp.int32, (1, CHUNK), 1)
            return jnp.where(place < live * part, nt_dot(spread[...], keys), NEG)

        def value_of(chunk):
            return value_buf[pl.ds(pl.multiple_of(chunk * CHUNK, CHUNK), CHUNK), :]

        chunks = (live * part + CHUNK - 1) // CHUNK
        row_max, row_total = attend(
            chunks, chunk_scores, value_of, (score_buf, max_buf, total_buf, acc)
        )
        emit(
            segment, row_max, row_total, acc, heads, full, stat_full, own_ref, own_stat_ref, sends
        )


def out_kernel(hid_ref, own_ref, other_ref, wo_ref, wp_ref, out_ref):
    segs, part, share = out_ref.shape
    cols = pl.ds(pl.multiple_of(lax.axis_index("head") * share, 128), share)
    result = (
        hid_ref[:, cols] + mm(own_ref[...], wo_ref[:, cols]) + mm(other_ref[...], wp_ref[:, cols])
    )
    for segment in range(segs):
        out_ref[segment] = result[segment * part : (segment + 1) * part].astype(BF16)


def cost(flops, moved, exps=0):
    return pl.CostEstimate(flops=int(flops), bytes_accessed=int(moved), transcendentals=int(exps))


def vmem():
    return pl.BlockSpec(memory_space=pltpu.VMEM)


def smem():
    return pl.BlockSpec(memory_space=pltpu.SMEM)


def call(kernel, inputs, outputs, specs=None, scratch=(), estimate=None, limit=None, name=None):
    return pl.pallas_call(
        kernel,
        out_shape=[jax.ShapeDtypeStruct(shape, kind) for shape, kind in outputs],
        in_specs=specs or [vmem() for _ in inputs],
        out_specs=[vmem() for _ in outputs],
        scratch_shapes=list(scratch),
        cost_estimate=estimate,
        compiler_params=pltpu.CompilerParams(vmem_limit_bytes=limit),
        name=name,
    )(*inputs)


def swap_cores(value):
    return lax.ppermute(value, "head", [(0, 1), (1, 0)])


def to_reader(value, step):
    readers = lax.axis_size("read")
    return lax.ppermute(value, "read", [(i, (i + step) % readers) for i in range(readers)])


def both_ways(value, step):
    count = lax.axis_size("pos")
    moves = []
    for place in range(count):
        if place + step < count:
            moves.append((2 * place, 2 * (place + step)))
        if place - step >= 0:
            moves.append((2 * place + 1, 2 * (place - step) + 1))
    return lax.ppermute(value, ("pos", "head"), moves)


def per_device(
    latents, read_tokens, band_start, coverage, present, pattern, cross_query, cross_key,
    cross_value, cross_out, self_query, self_key, self_value, self_out,
):
    segs, lat_rows, width = latents.shape
    reads, length = read_tokens.shape[1:3]
    local = cross_query.shape[1]
    heads = local // HD
    readers = lax.axis_size("read")
    part = lat_rows // readers
    size = segs * part
    seg_total = pattern.shape[1]
    share = width // lax.axis_size("head")
    spread_rows = heads * lat_rows

    offsets = [0]
    distance = 1
    while distance < seg_total:
        offsets += [distance, -distance]
        distance *= 2
    steps = sorted(
        {abs((seg + off) // segs) for off in offsets for seg in range(segs)} - {0}
    )

    cross_out_other = swap_cores(cross_out)
    self_out_other = swap_cores(self_out)

    part_outputs = [((segs, part, local), F32), ((segs, part, STATS), BF16)] + [
        ((segs, part, local + STATS), BF16)
    ] * (readers - 1)
    work = [
        pltpu.VMEM((spread_rows, 128), F32),
        pltpu.VMEM((spread_rows, 128), F32),
        pltpu.VMEM((spread_rows, local), F32),
        pltpu.VMEM((lat_rows, local), F32),
        pltpu.VMEM((lat_rows, STATS), F32),
    ]
    most = reads * length
    produced = call(
        functools.partial(cross_kernel, readers),
        (band_start, coverage, present, latents, read_tokens, cross_query, cross_key, cross_value),
        part_outputs,
        specs=[smem()] * 3
        + [vmem(), pl.BlockSpec(memory_space=pl.ANY), vmem(), vmem(), vmem()],
        scratch=[
            pltpu.VMEM((segs, most, width), BF16),
            pltpu.VMEM((segs, lat_rows, local), BF16),
            pltpu.VMEM((spread_rows, local), BF16),
            pltpu.VMEM((most // CHUNK, spread_rows, CHUNK), F32),
            pltpu.VMEM((most, local), BF16),
        ]
        + work
        + [pltpu.SemaphoreType.DMA((segs,))],
        estimate=cost(
            2 * segs * most * local * (2 * width + 2 * spread_rows),
            2 * segs * most * width,
            segs * most * spread_rows,
        ),
        limit=48 << 20,
        name="cross",
    )

    def combine(parts, name):
        own, own_stat, sends = parts[0], parts[1], parts[2:]
        received = [to_reader(value, step + 1) for step, value in enumerate(sends)]
        inputs = [own.reshape(size, local), own_stat.reshape(size, STATS)] + [
            value.reshape(size, local + STATS) for value in received
        ]
        return call(
            combine_kernel, inputs, [((size, local), BF16)], name=name,
            estimate=cost(8 * size * STATS * local, 8 * size * local),
        )[0]

    attended = combine(produced, "join_reads")
    attended_other = swap_cores(attended)
    hidden, normed, query = call(
        hidden_kernel,
        (latents, attended, attended_other, cross_out, cross_out_other, self_query),
        [((size, width), F32), ((size, width), BF16), ((size, local), BF16)],
        name="hidden",
        estimate=cost(2 * size * width * (width + local), 8 * size * width),
    )
    queries = [query] + [to_reader(query, step) for step in range(1, readers)]
    blocks = [normed]
    direct = {0: normed}
    for step in steps:
        half = step // 2
        source = direct[half] if half and half * 2 == step and half in direct else normed
        direct[step] = both_ways(source, step - half if half in direct and half else step)
    for step in steps:
        blocks += [direct[step], swap_cores(direct[step])]
    keys_most = -(-len(offsets) * part // CHUNK) * CHUNK
    produced = call(
        functools.partial(self_kernel, readers, tuple(steps), tuple(offsets)),
        (pattern, self_key, self_value, *queries, *blocks),
        part_outputs,
        specs=[smem()] + [vmem()] * (2 + len(queries) + len(blocks)),
        scratch=[
            pltpu.VMEM((segs, lat_rows, local), BF16),
            pltpu.VMEM((spread_rows, local), BF16),
            pltpu.VMEM((len(blocks) * size, local), BF16),
            pltpu.VMEM((len(blocks) * size, local), BF16),
            pltpu.VMEM((keys_most, local), BF16),
            pltpu.VMEM((keys_most, local), BF16),
            pltpu.VMEM((keys_most // CHUNK, spread_rows, CHUNK), F32),
        ]
        + work,
        estimate=cost(4 * segs * keys_most * local * spread_rows, 4 * len(blocks) * size * width),
        limit=48 << 20,
        name="within",
    )
    mixed = combine(produced, "join_keys")
    mixed_other = swap_cores(mixed)
    return call(
        out_kernel,
        (hidden, mixed, mixed_other, self_out, self_out_other),
        [((segs, part, share), BF16)],
        name="out",
        estimate=cost(2 * size * width * share, 8 * size * width),
    )[0]


def solution(mesh):
    placed = (
        P(("grp", "pos"), None, None),
        P(("grp", "pos"), "read", None, None),
        P(("grp", "pos"), "read"),
        P(("grp", "pos"), "read"),
        P(("grp", "pos"), "read"),
        P(("grp", "pos"), None),
        P(None, "head"),
        P(None, "head"),
        P(None, "head"),
        P("head", None),
        P(None, "head"),
        P(None, "head"),
        P(None, "head"),
        P("head", None),
    )
    return jax.shard_map(
        per_device,
        mesh=mesh,
        in_specs=placed,
        out_specs=P(("grp", "pos"), "read", "head"),
        check_vma=False,
    )
```

```python
import functools

import jax
import jax.numpy as jnp
from jax import lax
from jax.experimental import pallas as pl
from jax.experimental.pallas import tpu as pltpu
from jax.sharding import PartitionSpec as P

HD = 64
EPSILON = 1e-06
NEG = -1e30
CHUNK = 256
STATS = 128
ROWS = 16
F32 = jnp.float32
BF16 = jnp.bfloat16


def nt_dot(left, right):
    return lax.dot_general(left, right, (((1,), (1,)), ((), ())), preferred_element_type=F32)


def mm(left, right):
    return jnp.dot(left, right, preferred_element_type=F32)


def rms_rows(values):
    return values * lax.rsqrt(jnp.mean(values * values, axis=-1, keepdims=True) + EPSILON)


def spread_queries(query, heads, target):
    rows, width = query.shape
    column_head = lax.broadcasted_iota(jnp.int32, (rows, width), 1) // HD
    for head in range(heads):
        target[head * rows : (head + 1) * rows, :] = jnp.where(
            column_head == head, query.astype(F32), 0.0
        ).astype(BF16)


def tile_fold(values, combine):
    folded = values[:, :128]
    for tile in range(1, values.shape[1] // 128):
        folded = combine(folded, values[:, tile * 128 : (tile + 1) * 128])
    return folded


def attend(chunks, chunk_scores, value_of, scratch):
    score_buf, max_buf, total_buf, acc = scratch
    max_buf[...] = jnp.full(max_buf.shape, NEG, F32)
    total_buf[...] = jnp.zeros(total_buf.shape, F32)
    acc[...] = jnp.zeros(acc.shape, F32)

    def first(chunk, carry):
        scores = chunk_scores(chunk)
        score_buf[chunk] = scores
        max_buf[...] = jnp.maximum(max_buf[...], tile_fold(scores, jnp.maximum))
        return carry

    lax.fori_loop(0, chunks, first, 0)
    row_max = jnp.max(max_buf[...], axis=1, keepdims=True)

    def second(chunk, carry):
        weights = jnp.exp(score_buf[chunk] - row_max)
        total_buf[...] += tile_fold(weights, jnp.add)
        acc[...] += mm(weights.astype(BF16), value_of(chunk))
        return carry

    lax.fori_loop(0, chunks, second, 0)
    return row_max, jnp.sum(total_buf[...], axis=1, keepdims=True)


def emit(segment, row_max, row_total, acc, heads, full, stat_full, own_ref, own_stat_ref, sends):
    readers = len(sends) + 1
    rows, width = full.shape
    part = rows // readers
    lane = lax.broadcasted_iota(jnp.int32, (rows, 128), 1)
    for tile in range(width // 128):
        low, high = 2 * tile, 2 * tile + 1
        cols = slice(tile * 128, (tile + 1) * 128)
        full[:, cols] = jnp.where(
            lane < HD,
            acc[low * rows : (low + 1) * rows, cols],
            acc[high * rows : (high + 1) * rows, cols],
        )
    stats = jnp.zeros((rows, STATS), F32)
    place = 0
    for source in (row_max, row_total):
        for head in range(heads):
            left = source[head * rows : (head + 1) * rows]
            for step in range(3):
                piece = left.astype(BF16).astype(F32)
                stats = jnp.where(lane == place, piece, stats)
                left = left - piece
                place += 1
    stat_full[...] = stats
    reader = lax.axis_index("read")
    for step in range(readers):
        first = pl.multiple_of(lax.rem(reader + step, readers) * part, part)
        if step == 0:
            own_ref[segment] = full[pl.ds(first, part), :]
            own_stat_ref[segment] = stat_full[pl.ds(first, part), :].astype(BF16)
        else:
            sends[step - 1][segment, :, :width] = full[pl.ds(first, part), :].astype(BF16)
            sends[step - 1][segment, :, width:] = stat_full[pl.ds(first, part), :].astype(BF16)


def cross_kernel(
    readers, start_hbm, cov_hbm, present_hbm, lat_hbm, tok_ref, wq_hbm, wk_hbm, wv_hbm, *rest
):
    own_ref, own_stat_ref = rest[:2]
    sends = rest[2 : 1 + readers]
    (start_ref, cov_ref, present_ref, lat_ref, wq_ref, wk_ref, wv_ref, token_buf, query_buf, spread,
     score_buf, value_buf, max_buf, total_buf, acc, full, stat_full, load_sems, sems) = rest[
        1 + readers :
    ]
    loads = [
        pltpu.make_async_copy(source, target, load_sems.at[index])
        for index, (source, target) in enumerate(
            (
                (start_hbm, start_ref),
                (cov_hbm, cov_ref),
                (present_hbm, present_ref),
                (lat_hbm, lat_ref),
                (wq_hbm, wq_ref),
                (wk_hbm, wk_ref),
                (wv_hbm, wv_ref),
            )
        )
    ]
    for load in loads:
        load.start()
    for load in loads[:3]:
        load.wait()
    segs, lat_rows, width = lat_ref.shape
    reads = tok_ref.shape[1]
    local = wq_ref.shape[1]
    heads = local // HD

    def span(segment, read):
        start = start_ref[segment, read]
        length = cov_ref[segment, read]
        first = (start // ROWS) * ROWS
        last = ((start + length + ROWS - 1) // ROWS) * ROWS
        live = present_ref[segment, read] > 0
        return start - first, jnp.where(live, length, 0), first, jnp.where(live, last - first, 0)

    for segment in range(segs):
        offset = jnp.int32(0)
        for read in range(reads):
            lead, length, first, rows = span(segment, read)

            @pl.when(rows > 0)
            def _(segment=segment, read=read, offset=offset, first=first, rows=rows):
                pltpu.make_async_copy(
                    tok_ref.at[segment, read, pl.ds(pl.multiple_of(first, ROWS), rows), :],
                    token_buf.at[segment, pl.ds(pl.multiple_of(offset, ROWS), rows), :],
                    sems.at[segment],
                ).start()

            offset = offset + rows
        blocks = (((offset + CHUNK - 1) // CHUNK) * CHUNK - offset) // ROWS

        def clear(step, carry, segment=segment, offset=offset):
            token_buf[segment, pl.ds(pl.multiple_of(offset + step * ROWS, ROWS), ROWS), :] = (
                jnp.zeros((ROWS, width), BF16)
            )
            return carry

        lax.fori_loop(0, blocks, clear, 0)

    for load in loads[3:]:
        load.wait()
    for segment in range(segs):
        normed = rms_rows(lat_ref[segment].astype(F32)).astype(BF16)
        query_buf[segment] = (mm(normed, wq_ref[...]) * (HD ** (-0.5))).astype(BF16)

    def one_segment(segment, carry):
        spread_queries(query_buf[segment], heads, spread)
        offset = jnp.int32(0)
        bounds = []
        for read in range(reads):
            lead, length, first, rows = span(segment, read)
            bounds.append((offset + lead, offset + lead + length))
            offset = offset + rows

        @pl.when(offset > 0)
        def _():
            landed = token_buf.at[segment, pl.ds(0, offset), :]
            pltpu.make_async_copy(landed, landed, sems.at[segment]).wait()

        def chunk_scores(chunk):
            base = pl.multiple_of(chunk * CHUNK, CHUNK)
            tokens = token_buf[segment, pl.ds(base, CHUNK), :]
            keys = mm(tokens, wk_ref[...]).astype(BF16)
            value_buf[pl.ds(base, CHUNK), :] = mm(tokens, wv_ref[...]).astype(BF16)
            place = base + lax.broadcasted_iota(jnp.int32, (1, CHUNK), 1)
            live = jnp.zeros((1, CHUNK), jnp.bool_)
            for low, high in bounds:
                live = live | ((place >= low) & (place < high))
            return jnp.where(live, nt_dot(spread[...], keys), NEG)

        def value_of(chunk):
            return value_buf[pl.ds(pl.multiple_of(chunk * CHUNK, CHUNK), CHUNK), :]

        chunks = (offset + CHUNK - 1) // CHUNK
        row_max, row_total = attend(
            chunks, chunk_scores, value_of, (score_buf, max_buf, total_buf, acc)
        )
        emit(
            segment, row_max, row_total, acc, heads, full, stat_full, own_ref, own_stat_ref, sends
        )
        return carry

    lax.fori_loop(0, segs, one_segment, 0)


def combine_kernel(own_ref, stat_ref, *rest):
    received, out_ref = rest[:-1], rest[-1]
    width = own_ref.shape[1]
    heads = width // HD
    lane = lax.broadcasted_iota(jnp.int32, (STATS, width), 0)
    head = lax.broadcasted_iota(jnp.int32, (STATS, width), 1) // HD
    pick_max = ((lane // 3) == head).astype(F32).astype(BF16)
    pick_total = ((lane // 3) == head + heads).astype(F32).astype(BF16)
    parts = [(own_ref[...], stat_ref[...])]
    for ref in received:
        parts.append((ref[:, :width].astype(F32), ref[:, width:]))
    maxima = [mm(stat, pick_max) for _, stat in parts]
    totals = [mm(stat, pick_total) for _, stat in parts]
    joint = functools.reduce(jnp.maximum, maxima)
    factors = [jnp.exp(value - joint) for value in maxima]
    total = sum(value * factor for value, factor in zip(totals, factors))
    mixed = sum(part[0] * factor for part, factor in zip(parts, factors))
    out_ref[...] = (mixed / total).astype(BF16)


def hidden_kernel(
    lat_ref, own_ref, other_ref, wo_ref, wp_ref, wq_ref, hid_ref, norm_ref, query_ref
):
    segs, lat_rows, width = lat_ref.shape
    part = own_ref.shape[0] // segs
    first = pl.multiple_of(lax.axis_index("read") * part, part)
    delta = mm(own_ref[...], wo_ref[...]) + mm(other_ref[...], wp_ref[...])
    for segment in range(segs):
        rows = slice(segment * part, (segment + 1) * part)
        hid_ref[rows, :] = lat_ref[segment, pl.ds(first, part), :].astype(F32) + delta[rows]
    normed = rms_rows(hid_ref[...]).astype(BF16)
    norm_ref[...] = normed
    query_ref[...] = (mm(normed, wq_ref[...]) * (HD ** (-0.5))).astype(BF16)


def self_kernel(readers, steps, offsets, pattern_ref, wk_ref, wv_ref, *rest):
    queries = rest[:readers]
    count = 1 + 2 * len(steps)
    blocks = rest[readers : readers + count]
    rest = rest[readers + count :]
    own_ref, own_stat_ref = rest[:2]
    sends = rest[2 : 1 + readers]
    (query_buf, spread, key_all, value_all, key_buf, value_buf, score_buf, max_buf, total_buf, acc,
     full, stat_full) = rest[1 + readers :]
    segs = own_ref.shape[0]
    part = own_ref.shape[1]
    local = wk_ref.shape[1]
    heads = local // HD
    seg_total = pattern_ref.shape[1]
    reader = lax.axis_index("read")
    core = lax.axis_index("head")
    group = lax.axis_index("pos")
    size = segs * part

    key_buf[...] = jnp.zeros(key_buf.shape, BF16)
    value_buf[...] = jnp.zeros(value_buf.shape, BF16)
    for index, block in enumerate(blocks):
        if index == 0:
            slot = 0
        else:
            pair = (index - 1) // 2
            slot = 1 + 2 * pair + (core if index % 2 == 1 else 1 - core)
        place = pl.ds(pl.multiple_of(slot * size, size), size)
        key_all[place, :] = mm(block[...], wk_ref[...]).astype(BF16)
        value_all[place, :] = mm(block[...], wv_ref[...]).astype(BF16)
    for step in range(readers):
        first = pl.multiple_of(lax.rem(reader + readers - step, readers) * part, part)
        for segment in range(segs):
            query_buf[segment, pl.ds(first, part), :] = queries[step][
                segment * part : (segment + 1) * part, :
            ]

    for segment in range(segs):
        spread_queries(query_buf[segment], heads, spread)
        live = jnp.int32(0)
        for offset in offsets:
            block_step = (segment + offset) // segs
            inner = (segment + offset) % segs
            if block_step == 0:
                slot = 0
            else:
                slot = 1 + 2 * steps.index(abs(block_step)) + (1 if block_step > 0 else 0)
            target = group * segs + segment + offset
            inside = (target >= 0) & (target < seg_total)
            flag = pattern_ref[segment, jnp.clip(target, 0, seg_total - 1)]
            chosen = inside & (flag > 0)
            source = (slot * segs + inner) * part

            @pl.when(chosen)
            def _(live=live, source=source):
                place = pl.ds(pl.multiple_of(live * part, part), part)
                key_buf[place, :] = key_all[source : source + part, :]
                value_buf[place, :] = value_all[source : source + part, :]

            live = live + chosen.astype(jnp.int32)

        def chunk_scores(chunk, live=live):
            base = pl.multiple_of(chunk * CHUNK, CHUNK)
            keys = key_buf[pl.ds(base, CHUNK), :]
            place = base + lax.broadcasted_iota(jnp.int32, (1, CHUNK), 1)
            return jnp.where(place < live * part, nt_dot(spread[...], keys), NEG)

        def value_of(chunk):
            return value_buf[pl.ds(pl.multiple_of(chunk * CHUNK, CHUNK), CHUNK), :]

        chunks = (live * part + CHUNK - 1) // CHUNK
        row_max, row_total = attend(
            chunks, chunk_scores, value_of, (score_buf, max_buf, total_buf, acc)
        )
        emit(
            segment, row_max, row_total, acc, heads, full, stat_full, own_ref, own_stat_ref, sends
        )


def out_kernel(hid_ref, own_ref, other_ref, wo_ref, wp_ref, out_ref):
    segs, part, share = out_ref.shape
    cols = pl.ds(pl.multiple_of(lax.axis_index("head") * share, 128), share)
    result = (
        hid_ref[:, cols] + mm(own_ref[...], wo_ref[:, cols]) + mm(other_ref[...], wp_ref[:, cols])
    )
    for segment in range(segs):
        out_ref[segment] = result[segment * part : (segment + 1) * part].astype(BF16)


def cost(flops, moved, exps=0):
    return pl.CostEstimate(flops=int(flops), bytes_accessed=int(moved), transcendentals=int(exps))


def vmem():
    return pl.BlockSpec(memory_space=pltpu.VMEM)


def smem():
    return pl.BlockSpec(memory_space=pltpu.SMEM)


def call(kernel, inputs, outputs, specs=None, scratch=(), estimate=None, limit=8 << 20, name=None):
    return pl.pallas_call(
        kernel,
        out_shape=[jax.ShapeDtypeStruct(shape, kind) for shape, kind in outputs],
        in_specs=specs or [vmem() for _ in inputs],
        out_specs=[vmem() for _ in outputs],
        scratch_shapes=list(scratch),
        cost_estimate=estimate,
        compiler_params=pltpu.CompilerParams(vmem_limit_bytes=limit),
        name=name,
    )(*inputs)


def swap_cores(value):
    return lax.ppermute(value, "head", [(0, 1), (1, 0)])


def to_reader(value, step):
    readers = lax.axis_size("read")
    return lax.ppermute(value, "read", [(i, (i + step) % readers) for i in range(readers)])


def both_ways(value, step):
    count = lax.axis_size("pos")
    moves = []
    for place in range(count):
        if place + step < count:
            moves.append((2 * place, 2 * (place + step)))
        if place - step >= 0:
            moves.append((2 * place + 1, 2 * (place - step) + 1))
    return lax.ppermute(value, ("pos", "head"), moves)


def per_device(
    latents, read_tokens, band_start, coverage, present, pattern, cross_query, cross_key,
    cross_value, cross_out, self_query, self_key, self_value, self_out,
):
    segs, lat_rows, width = latents.shape
    reads, length = read_tokens.shape[1:3]
    local = cross_query.shape[1]
    heads = local // HD
    readers = lax.axis_size("read")
    part = lat_rows // readers
    size = segs * part
    seg_total = pattern.shape[1]
    share = width // lax.axis_size("head")
    spread_rows = heads * lat_rows

    offsets = [0]
    distance = 1
    while distance < seg_total:
        offsets += [distance, -distance]
        distance *= 2
    steps = sorted(
        {abs((seg + off) // segs) for off in offsets for seg in range(segs)} - {0}
    )

    cross_out_other = swap_cores(cross_out)
    self_out_other = swap_cores(self_out)

    part_outputs = [((segs, part, local), F32), ((segs, part, STATS), BF16)] + [
        ((segs, part, local + STATS), BF16)
    ] * (readers - 1)
    work = [
        pltpu.VMEM((spread_rows, 128), F32),
        pltpu.VMEM((spread_rows, 128), F32),
        pltpu.VMEM((spread_rows, local), F32),
        pltpu.VMEM((lat_rows, local), F32),
        pltpu.VMEM((lat_rows, STATS), F32),
    ]
    most = reads * length
    produced = call(
        functools.partial(cross_kernel, readers),
        (band_start, coverage, present, latents, read_tokens, cross_query, cross_key, cross_value),
        part_outputs,
        specs=[pl.BlockSpec(memory_space=pltpu.HBM)] * 8,
        scratch=[
            pltpu.SMEM(band_start.shape, jnp.int32),
            pltpu.SMEM(coverage.shape, jnp.int32),
            pltpu.SMEM(present.shape, jnp.int32),
            pltpu.VMEM(latents.shape, BF16),
            pltpu.VMEM(cross_query.shape, BF16),
            pltpu.VMEM(cross_key.shape, BF16),
            pltpu.VMEM(cross_value.shape, BF16),
            pltpu.VMEM((segs, most, width), BF16),
            pltpu.VMEM((segs, lat_rows, local), BF16),
            pltpu.VMEM((spread_rows, local), BF16),
            pltpu.VMEM((most // CHUNK, spread_rows, CHUNK), F32),
            pltpu.VMEM((most, local), BF16),
        ]
        + work
        + [pltpu.SemaphoreType.DMA((7,)), pltpu.SemaphoreType.DMA((segs,))],
        estimate=cost(
            2 * segs * most * local * (2 * width + 2 * spread_rows),
            2 * segs * most * width,
            segs * most * spread_rows,
        ),
        limit=60 * 1024 * 1024,
        name="cross",
    )

    def combine(parts, name):
        own, own_stat, sends = parts[0], parts[1], parts[2:]
        received = [to_reader(value, step + 1) for step, value in enumerate(sends)]
        inputs = [own.reshape(size, local), own_stat.reshape(size, STATS)] + [
            value.reshape(size, local + STATS) for value in received
        ]
        return call(
            combine_kernel, inputs, [((size, local), BF16)], name=name,
            estimate=cost(8 * size * STATS * local, 8 * size * local),
        )[0]

    attended = combine(produced, "join_reads")
    attended_other = swap_cores(attended)
    hidden, normed, query = call(
        hidden_kernel,
        (latents, attended, attended_other, cross_out, cross_out_other, self_query),
        [((size, width), F32), ((size, width), BF16), ((size, local), BF16)],
        name="hidden",
        estimate=cost(2 * size * width * (width + local), 8 * size * width),
    )
    queries = [query] + [to_reader(query, step) for step in range(1, readers)]
    blocks = [normed]
    direct = {0: normed}
    for step in steps:
        half = step // 2
        source = direct[half] if half and half * 2 == step and half in direct else normed
        direct[step] = both_ways(source, step - half if half in direct and half else step)
    for step in steps:
        blocks += [direct[step], swap_cores(direct[step])]
    keys_most = -(-len(offsets) * part // CHUNK) * CHUNK
    produced = call(
        functools.partial(self_kernel, readers, tuple(steps), tuple(offsets)),
        (pattern, self_key, self_value, *queries, *blocks),
        part_outputs,
        specs=[smem()] + [vmem()] * (2 + len(queries) + len(blocks)),
        scratch=[
            pltpu.VMEM((segs, lat_rows, local), BF16),
            pltpu.VMEM((spread_rows, local), BF16),
            pltpu.VMEM((len(blocks) * size, local), BF16),
            pltpu.VMEM((len(blocks) * size, local), BF16),
            pltpu.VMEM((keys_most, local), BF16),
            pltpu.VMEM((keys_most, local), BF16),
            pltpu.VMEM((keys_most // CHUNK, spread_rows, CHUNK), F32),
        ]
        + work,
        estimate=cost(4 * segs * keys_most * local * spread_rows, 4 * len(blocks) * size * width),
        limit=16 << 20,
        name="within",
    )
    mixed = combine(produced, "join_keys")
    mixed_other = swap_cores(mixed)
    return call(
        out_kernel,
        (hidden, mixed, mixed_other, self_out, self_out_other),
        [((segs, part, share), BF16)],
        name="out",
        estimate=cost(2 * size * width * share, 8 * size * width),
    )[0]


def solution(mesh):
    placed = (
        P(("grp", "pos"), None, None),
        P(("grp", "pos"), "read", None, None),
        P(("grp", "pos"), "read"),
        P(("grp", "pos"), "read"),
        P(("grp", "pos"), "read"),
        P(("grp", "pos"), None),
        P(None, "head"),
        P(None, "head"),
        P(None, "head"),
        P("head", None),
        P(None, "head"),
        P(None, "head"),
        P(None, "head"),
        P("head", None),
    )
    return jax.shard_map(
        per_device,
        mesh=mesh,
        in_specs=placed,
        out_specs=P(("grp", "pos"), "read", "head"),
        check_vma=False,
    )
```

```python
import functools

import jax
import jax.numpy as jnp
from jax import lax
from jax.experimental import pallas as pl
from jax.experimental.pallas import tpu as pltpu
from jax.sharding import PartitionSpec as P

HD = 64
EPSILON = 1e-06
NEG = -1e30
CHUNK = 256
STATS = 128
ROWS = 16
F32 = jnp.float32
BF16 = jnp.bfloat16


def nt_dot(left, right):
    return lax.dot_general(left, right, (((1,), (1,)), ((), ())), preferred_element_type=F32)


def mm(left, right):
    return jnp.dot(left, right, preferred_element_type=F32)


def rms_rows(values):
    return values * lax.rsqrt(jnp.mean(values * values, axis=-1, keepdims=True) + EPSILON)


def spread_queries(query, heads, target):
    rows, width = query.shape
    column_head = lax.broadcasted_iota(jnp.int32, (rows, width), 1) // HD
    for head in range(heads):
        target[head * rows : (head + 1) * rows, :] = jnp.where(
            column_head == head, query.astype(F32), 0.0
        ).astype(BF16)


def tile_fold(values, combine):
    folded = values[:, :128]
    for tile in range(1, values.shape[1] // 128):
        folded = combine(folded, values[:, tile * 128 : (tile + 1) * 128])
    return folded


def attend(chunks, chunk_scores, value_of, scratch):
    score_buf, max_buf, total_buf, acc = scratch
    max_buf[...] = jnp.full(max_buf.shape, NEG, F32)
    total_buf[...] = jnp.zeros(total_buf.shape, F32)
    acc[...] = jnp.zeros(acc.shape, F32)

    def first(chunk, carry):
        scores = chunk_scores(chunk)
        score_buf[chunk] = scores
        max_buf[...] = jnp.maximum(max_buf[...], tile_fold(scores, jnp.maximum))
        return carry

    lax.fori_loop(0, chunks, first, 0)
    row_max = jnp.max(max_buf[...], axis=1, keepdims=True)

    def second(chunk, carry):
        weights = jnp.exp(score_buf[chunk] - row_max)
        total_buf[...] += tile_fold(weights, jnp.add)
        acc[...] += mm(weights.astype(BF16), value_of(chunk))
        return carry

    lax.fori_loop(0, chunks, second, 0)
    return row_max, jnp.sum(total_buf[...], axis=1, keepdims=True)


def emit(segment, row_max, row_total, acc, heads, full, stat_full, own_ref, own_stat_ref, sends):
    readers = len(sends) + 1
    rows, width = full.shape
    part = rows // readers
    lane = lax.broadcasted_iota(jnp.int32, (rows, 128), 1)
    filled = row_total > 0
    divisor = jnp.where(filled, row_total, 1.0)
    level = jnp.where(filled, row_max + jnp.log(divisor), NEG)
    for tile in range(width // 128):
        low = slice(2 * tile * rows, (2 * tile + 1) * rows)
        high = slice((2 * tile + 1) * rows, (2 * tile + 2) * rows)
        cols = slice(tile * 128, (tile + 1) * 128)
        full[:, cols] = jnp.where(lane < HD, acc[low, cols], acc[high, cols]) / jnp.where(
            lane < HD, divisor[low], divisor[high]
        )
    stats = jnp.zeros((rows, STATS), F32)
    for head in range(heads):
        left = level[head * rows : (head + 1) * rows]
        for step in range(3):
            piece = left.astype(BF16).astype(F32)
            stats = jnp.where(lane == 3 * head + step, piece, stats)
            left = left - piece
    stat_full[...] = stats
    reader = lax.axis_index("read")
    for step in range(readers):
        first = pl.multiple_of(lax.rem(reader + step, readers) * part, part)
        if step == 0:
            own_ref[segment] = full[pl.ds(first, part), :]
            own_stat_ref[segment] = stat_full[pl.ds(first, part), :].astype(BF16)
        else:
            sends[step - 1][segment, :, :width] = full[pl.ds(first, part), :].astype(BF16)
            sends[step - 1][segment, :, width:] = stat_full[pl.ds(first, part), :].astype(BF16)


def cross_kernel(
    readers, start_hbm, cov_hbm, present_hbm, lat_hbm, tok_ref, wq_hbm, wk_hbm, wv_hbm, *rest
):
    own_ref, own_stat_ref = rest[:2]
    sends = rest[2 : 1 + readers]
    (start_ref, cov_ref, present_ref, seg_of, low_of, high_of, lat_ref, wq_ref, wk_ref, wv_ref,
     token_buf, spread, key_buf, score_buf, value_buf, max_buf, total_buf, acc, full, stat_full,
     load_sems, sems) = rest[1 + readers :]
    loads = [
        pltpu.make_async_copy(source, target, load_sems.at[index])
        for index, (source, target) in enumerate(
            (
                (start_hbm, start_ref),
                (cov_hbm, cov_ref),
                (present_hbm, present_ref),
                (lat_hbm, lat_ref),
                (wq_hbm, wq_ref),
                (wk_hbm, wk_ref),
                (wv_hbm, wv_ref),
            )
        )
    ]
    for load in loads:
        load.start()
    for load in loads[:3]:
        load.wait()
    segs, lat_rows, width = lat_ref.shape
    reads = tok_ref.shape[1]
    local = wq_ref.shape[1]
    heads = local // HD

    used = jnp.int32(0)
    for segment in range(segs):
        offset = used * CHUNK
        for read in range(reads):
            start = start_ref[segment, read]
            length = cov_ref[segment, read]
            live = present_ref[segment, read] > 0
            first = (start // ROWS) * ROWS
            last = ((start + length + ROWS - 1) // ROWS) * ROWS
            rows = jnp.where(live, last - first, 0)
            low_of[segment, read] = offset + start - first
            high_of[segment, read] = offset + jnp.where(live, start - first + length, 0)

            @pl.when(live)
            def _(segment=segment, read=read, offset=offset, first=first, rows=rows):
                pltpu.make_async_copy(
                    tok_ref.at[segment, read, pl.ds(pl.multiple_of(first, ROWS), rows), :],
                    token_buf.at[pl.ds(pl.multiple_of(offset, ROWS), rows), :],
                    sems.at[segment],
                ).start()

            offset = offset + rows
        low_of[segment, reads] = offset - used * CHUNK
        chunks = (offset - used * CHUNK + CHUNK - 1) // CHUNK

        def clear(step, carry, offset=offset):
            token_buf[pl.ds(pl.multiple_of(offset + step * ROWS, ROWS), ROWS), :] = jnp.zeros(
                (ROWS, width), BF16
            )
            return carry

        lax.fori_loop(0, ((used + chunks) * CHUNK - offset) // ROWS, clear, 0)

        def note(step, carry, segment=segment, used=used):
            seg_of[used + step] = segment
            return carry

        lax.fori_loop(0, chunks, note, 0)
        used = used + chunks
    for step in range(3):
        seg_of[used + step] = segs
    for read in range(reads):
        low_of[segs, read] = 0
        high_of[segs, read] = 0

    max_buf[...] = jnp.full(max_buf.shape, NEG, F32)
    total_buf[...] = jnp.zeros(total_buf.shape, F32)
    acc[...] = jnp.zeros(acc.shape, F32)
    for load in loads[3:]:
        load.wait()
    for segment in range(segs):
        normed = rms_rows(lat_ref[segment].astype(F32)).astype(BF16)
        query = (mm(normed, wq_ref[...]) * (HD ** (-0.5))).astype(BF16)
        spread_queries(query, heads, spread.at[segment])

    def landed(segment):
        size = pl.multiple_of(low_of[segment, reads], ROWS)
        whole = token_buf.at[pl.ds(0, size), :]
        pltpu.make_async_copy(whole, whole, sems.at[segment]).wait()

    def projected(pair):
        place = pl.ds(pl.multiple_of(pair * 2 * CHUNK, 2 * CHUNK), 2 * CHUNK)
        tokens = token_buf[place, :]
        key_buf[lax.rem(pair, 2)] = mm(tokens, wk_ref[...]).astype(BF16)
        value_buf[place, :] = mm(tokens, wv_ref[...]).astype(BF16)

    def arrive(chunk, before):
        upcoming = seg_of[chunk]

        @pl.when((upcoming != before) & (upcoming < segs))
        def _():
            landed(upcoming)

    pairs = (used + 1) // 2

    @pl.when(used > 0)
    def _():
        arrive(0, -1)
        arrive(1, seg_of[0])
        projected(jnp.int32(0))

    def first_pass(pair, carry):
        chunk = 2 * pair
        arrive(chunk + 2, seg_of[chunk + 1])
        arrive(chunk + 3, seg_of[chunk + 2])
        keys = key_buf[lax.rem(pair, 2)]
        segments = [seg_of[chunk], seg_of[chunk + 1]]
        for half in range(2):
            segment = segments[half]
            place = (chunk + half) * CHUNK + lax.broadcasted_iota(jnp.int32, (1, CHUNK), 1)
            live = jnp.zeros((1, CHUNK), jnp.bool_)
            for read in range(reads):
                live = live | (
                    (place >= low_of[segment, read]) & (place < high_of[segment, read])
                )
            for block in range(2):
                size = acc.shape[1] // 2
                rows = slice(block * size, (block + 1) * size)
                scores = nt_dot(
                    spread[segment, rows], keys[half * CHUNK : (half + 1) * CHUNK]
                )
                scores = jnp.where(live, scores, NEG)
                score_buf[chunk + half, rows] = scores
                max_buf[segment, rows] = jnp.maximum(
                    max_buf[segment, rows], tile_fold(scores, jnp.maximum)
                )
        projected(pair + 1)
        return carry

    lax.fori_loop(0, pairs, first_pass, 0)
    for segment in range(segs):
        row_max = jnp.max(max_buf[segment], axis=1, keepdims=True)
        max_buf[segment] = jnp.broadcast_to(row_max, max_buf.shape[1:])

    def second_pass(pair, carry):
        for half in range(2):
            chunk = 2 * pair + half
            segment = seg_of[chunk]
            value = value_buf[pl.ds(pl.multiple_of(chunk * CHUNK, CHUNK), CHUNK), :]
            for block in range(2):
                rows = slice(block * acc.shape[1] // 2, (block + 1) * acc.shape[1] // 2)
                weights = jnp.exp(
                    score_buf[chunk, rows] - jnp.tile(max_buf[segment, rows], (1, CHUNK // 128))
                )
                total_buf[segment, rows] += tile_fold(weights, jnp.add)
                acc[segment, rows] += mm(weights.astype(BF16), value)
        return carry

    lax.fori_loop(0, pairs, second_pass, 0)

    def finish(segment, carry):
        row_total = jnp.sum(total_buf[segment], axis=1, keepdims=True)
        row_total = jnp.broadcast_to(row_total, total_buf.shape[1:])
        emit(
            segment, max_buf[segment], row_total, acc.at[segment], heads, full, stat_full,
            own_ref, own_stat_ref, sends,
        )
        return carry

    lax.fori_loop(0, segs, finish, 0)


def combine_kernel(own_ref, stat_ref, *rest):
    received, out_ref = rest[:-1], rest[-1]
    width = own_ref.shape[1]
    lane = lax.broadcasted_iota(jnp.int32, (STATS, width), 0)
    head = lax.broadcasted_iota(jnp.int32, (STATS, width), 1) // HD
    pick = ((lane // 3) == head).astype(F32).astype(BF16)
    parts = [(own_ref[...], stat_ref[...])]
    for ref in received:
        parts.append((ref[:, :width].astype(F32), ref[:, width:]))
    levels = [mm(stat, pick) for _, stat in parts]
    joint = functools.reduce(jnp.maximum, levels)
    factors = [jnp.exp(level - joint) for level in levels]
    mixed = sum(part[0] * factor for part, factor in zip(parts, factors))
    out_ref[...] = (mixed / sum(factors)).astype(BF16)


def hidden_kernel(
    lat_ref, own_ref, other_ref, wo_ref, wp_ref, wq_ref, hid_ref, norm_ref, query_ref
):
    segs, lat_rows, width = lat_ref.shape
    part = own_ref.shape[0] // segs
    first = pl.multiple_of(lax.axis_index("read") * part, part)
    delta = mm(own_ref[...], wo_ref[...]) + mm(other_ref[...], wp_ref[...])
    for segment in range(segs):
        rows = slice(segment * part, (segment + 1) * part)
        hid_ref[rows, :] = lat_ref[segment, pl.ds(first, part), :].astype(F32) + delta[rows]
    normed = rms_rows(hid_ref[...]).astype(BF16)
    norm_ref[...] = normed
    query_ref[...] = (mm(normed, wq_ref[...]) * (HD ** (-0.5))).astype(BF16)


def self_kernel(readers, steps, offsets, pattern_ref, wk_ref, wv_ref, *rest):
    queries = rest[:readers]
    count = 1 + 2 * len(steps)
    blocks = rest[readers : readers + count]
    rest = rest[readers + count :]
    own_ref, own_stat_ref = rest[:2]
    sends = rest[2 : 1 + readers]
    (query_buf, spread, key_all, value_all, key_buf, value_buf, score_buf, max_buf, total_buf, acc,
     full, stat_full) = rest[1 + readers :]
    segs = own_ref.shape[0]
    part = own_ref.shape[1]
    local = wk_ref.shape[1]
    heads = local // HD
    seg_total = pattern_ref.shape[1]
    reader = lax.axis_index("read")
    core = lax.axis_index("head")
    group = lax.axis_index("pos")
    size = segs * part

    key_buf[...] = jnp.zeros(key_buf.shape, BF16)
    value_buf[...] = jnp.zeros(value_buf.shape, BF16)
    for index, block in enumerate(blocks):
        if index == 0:
            slot = 0
        else:
            pair = (index - 1) // 2
            slot = 1 + 2 * pair + (core if index % 2 == 1 else 1 - core)
        place = pl.ds(pl.multiple_of(slot * size, size), size)
        key_all[place, :] = mm(block[...], wk_ref[...]).astype(BF16)
        value_all[place, :] = mm(block[...], wv_ref[...]).astype(BF16)
    for step in range(readers):
        first = pl.multiple_of(lax.rem(reader + readers - step, readers) * part, part)
        for segment in range(segs):
            query_buf[segment, pl.ds(first, part), :] = queries[step][
                segment * part : (segment + 1) * part, :
            ]

    for segment in range(segs):
        spread_queries(query_buf[segment], heads, spread)
        live = jnp.int32(0)
        for offset in offsets:
            block_step = (segment + offset) // segs
            inner = (segment + offset) % segs
            if block_step == 0:
                slot = 0
            else:
                slot = 1 + 2 * steps.index(abs(block_step)) + (1 if block_step > 0 else 0)
            target = group * segs + segment + offset
            inside = (target >= 0) & (target < seg_total)
            flag = pattern_ref[segment, jnp.clip(target, 0, seg_total - 1)]
            chosen = inside & (flag > 0)
            source = (slot * segs + inner) * part

            @pl.when(chosen)
            def _(live=live, source=source):
                place = pl.ds(pl.multiple_of(live * part, part), part)
                key_buf[place, :] = key_all[source : source + part, :]
                value_buf[place, :] = value_all[source : source + part, :]

            live = live + chosen.astype(jnp.int32)

        def chunk_scores(chunk, live=live):
            base = pl.multiple_of(chunk * CHUNK, CHUNK)
            keys = key_buf[pl.ds(base, CHUNK), :]
            place = base + lax.broadcasted_iota(jnp.int32, (1, CHUNK), 1)
            return jnp.where(place < live * part, nt_dot(spread[...], keys), NEG)

        def value_of(chunk):
            return value_buf[pl.ds(pl.multiple_of(chunk * CHUNK, CHUNK), CHUNK), :]

        chunks = (live * part + CHUNK - 1) // CHUNK
        row_max, row_total = attend(
            chunks, chunk_scores, value_of, (score_buf, max_buf, total_buf, acc)
        )
        wide = (heads * full.shape[0], 128)
        row_max, row_total = jnp.broadcast_to(row_max, wide), jnp.broadcast_to(row_total, wide)
        emit(
            segment, row_max, row_total, acc, heads, full, stat_full, own_ref, own_stat_ref, sends
        )


def out_kernel(hid_ref, own_ref, other_ref, wo_ref, wp_ref, out_ref):
    segs, part, share = out_ref.shape
    cols = pl.ds(pl.multiple_of(lax.axis_index("head") * share, 128), share)
    result = (
        hid_ref[:, cols] + mm(own_ref[...], wo_ref[:, cols]) + mm(other_ref[...], wp_ref[:, cols])
    )
    for segment in range(segs):
        out_ref[segment] = result[segment * part : (segment + 1) * part].astype(BF16)


def cost(flops, moved, exps=0):
    return pl.CostEstimate(flops=int(flops), bytes_accessed=int(moved), transcendentals=int(exps))


def vmem():
    return pl.BlockSpec(memory_space=pltpu.VMEM)


def smem():
    return pl.BlockSpec(memory_space=pltpu.SMEM)


def call(kernel, inputs, outputs, specs=None, scratch=(), estimate=None, limit=8 << 20, name=None):
    return pl.pallas_call(
        kernel,
        out_shape=[jax.ShapeDtypeStruct(shape, kind) for shape, kind in outputs],
        in_specs=specs or [vmem() for _ in inputs],
        out_specs=[vmem() for _ in outputs],
        scratch_shapes=list(scratch),
        cost_estimate=estimate,
        compiler_params=pltpu.CompilerParams(vmem_limit_bytes=limit),
        name=name,
    )(*inputs)


def swap_cores(value):
    return lax.ppermute(value, "head", [(0, 1), (1, 0)])


def to_reader(value, step):
    readers = lax.axis_size("read")
    return lax.ppermute(value, "read", [(i, (i + step) % readers) for i in range(readers)])


def both_ways(value, step):
    count = lax.axis_size("pos")
    moves = []
    for place in range(count):
        if place + step < count:
            moves.append((2 * place, 2 * (place + step)))
        if place - step >= 0:
            moves.append((2 * place + 1, 2 * (place - step) + 1))
    return lax.ppermute(value, ("pos", "head"), moves)


def per_device(
    latents, read_tokens, band_start, coverage, present, pattern, cross_query, cross_key,
    cross_value, cross_out, self_query, self_key, self_value, self_out,
):
    segs, lat_rows, width = latents.shape
    reads, length = read_tokens.shape[1:3]
    local = cross_query.shape[1]
    heads = local // HD
    readers = lax.axis_size("read")
    part = lat_rows // readers
    size = segs * part
    seg_total = pattern.shape[1]
    share = width // lax.axis_size("head")
    spread_rows = heads * lat_rows

    offsets = [0]
    distance = 1
    while distance < seg_total:
        offsets += [distance, -distance]
        distance *= 2
    steps = sorted(
        {abs((seg + off) // segs) for off in offsets for seg in range(segs)} - {0}
    )

    cross_out_other = swap_cores(cross_out)
    self_out_other = swap_cores(self_out)

    part_outputs = [((segs, part, local), F32), ((segs, part, STATS), BF16)] + [
        ((segs, part, local + STATS), BF16)
    ] * (readers - 1)
    work = [
        pltpu.VMEM((spread_rows, 128), F32),
        pltpu.VMEM((spread_rows, 128), F32),
        pltpu.VMEM((spread_rows, local), F32),
        pltpu.VMEM((lat_rows, local), F32),
        pltpu.VMEM((lat_rows, STATS), F32),
    ]
    most = reads * length
    tiles = -(-most // CHUNK)
    spare = (segs * tiles + 1) // 2 * 2 + 2
    produced = call(
        functools.partial(cross_kernel, readers),
        (band_start, coverage, present, latents, read_tokens, cross_query, cross_key, cross_value),
        part_outputs,
        specs=[pl.BlockSpec(memory_space=pltpu.HBM)] * 8,
        scratch=[
            pltpu.SMEM(band_start.shape, jnp.int32),
            pltpu.SMEM(coverage.shape, jnp.int32),
            pltpu.SMEM(present.shape, jnp.int32),
            pltpu.SMEM((segs * tiles + 3,), jnp.int32),
            pltpu.SMEM((segs + 1, reads + 1), jnp.int32),
            pltpu.SMEM((segs + 1, reads), jnp.int32),
            pltpu.VMEM(latents.shape, BF16),
            pltpu.VMEM(cross_query.shape, BF16),
            pltpu.VMEM(cross_key.shape, BF16),
            pltpu.VMEM(cross_value.shape, BF16),
            pltpu.VMEM((spare * CHUNK, width), BF16),
            pltpu.VMEM((segs + 1, spread_rows, local), BF16),
            pltpu.VMEM((2, 2 * CHUNK, local), BF16),
            pltpu.VMEM((segs * tiles + 1, spread_rows, CHUNK), F32),
            pltpu.VMEM((spare * CHUNK, local), BF16),
            pltpu.VMEM((segs + 1, spread_rows, 128), F32),
            pltpu.VMEM((segs + 1, spread_rows, 128), F32),
            pltpu.VMEM((segs + 1, spread_rows, local), F32),
        ]
        + work[3:]
        + [pltpu.SemaphoreType.DMA((7,)), pltpu.SemaphoreType.DMA((segs,))],
        estimate=cost(
            2 * segs * most * local * (2 * width + 2 * spread_rows),
            2 * segs * most * width,
            segs * most * spread_rows,
        ),
        limit=60 * 1024 * 1024,
        name="cross",
    )

    def combine(parts, name):
        own, own_stat, sends = parts[0], parts[1], parts[2:]
        received = [to_reader(value, step + 1) for step, value in enumerate(sends)]
        inputs = [own.reshape(size, local), own_stat.reshape(size, STATS)] + [
            value.reshape(size, local + STATS) for value in received
        ]
        return call(
            combine_kernel, inputs, [((size, local), BF16)], name=name,
            estimate=cost(8 * size * STATS * local, 8 * size * local),
        )[0]

    attended = combine(produced, "join_reads")
    attended_other = swap_cores(attended)
    hidden, normed, query = call(
        hidden_kernel,
        (latents, attended, attended_other, cross_out, cross_out_other, self_query),
        [((size, width), F32), ((size, width), BF16), ((size, local), BF16)],
        name="hidden",
        estimate=cost(2 * size * width * (width + local), 8 * size * width),
    )
    queries = [query] + [to_reader(query, step) for step in range(1, readers)]
    blocks = [normed]
    direct = {0: normed}
    for step in steps:
        half = step // 2
        source = direct[half] if half and half * 2 == step and half in direct else normed
        direct[step] = both_ways(source, step - half if half in direct and half else step)
    for step in steps:
        blocks += [direct[step], swap_cores(direct[step])]
    keys_most = -(-len(offsets) * part // CHUNK) * CHUNK
    produced = call(
        functools.partial(self_kernel, readers, tuple(steps), tuple(offsets)),
        (pattern, self_key, self_value, *queries, *blocks),
        part_outputs,
        specs=[smem()] + [vmem()] * (2 + len(queries) + len(blocks)),
        scratch=[
            pltpu.VMEM((segs, lat_rows, local), BF16),
            pltpu.VMEM((spread_rows, local), BF16),
            pltpu.VMEM((len(blocks) * size, local), BF16),
            pltpu.VMEM((len(blocks) * size, local), BF16),
            pltpu.VMEM((keys_most, local), BF16),
            pltpu.VMEM((keys_most, local), BF16),
            pltpu.VMEM((keys_most // CHUNK, spread_rows, CHUNK), F32),
        ]
        + work,
        estimate=cost(4 * segs * keys_most * local * spread_rows, 4 * len(blocks) * size * width),
        limit=16 << 20,
        name="within",
    )
    mixed = combine(produced, "join_keys")
    mixed_other = swap_cores(mixed)
    return call(
        out_kernel,
        (hidden, mixed, mixed_other, self_out, self_out_other),
        [((segs, part, share), BF16)],
        name="out",
        estimate=cost(2 * size * width * share, 8 * size * width),
    )[0]


def solution(mesh):
    placed = (
        P(("grp", "pos"), None, None),
        P(("grp", "pos"), "read", None, None),
        P(("grp", "pos"), "read"),
        P(("grp", "pos"), "read"),
        P(("grp", "pos"), "read"),
        P(("grp", "pos"), None),
        P(None, "head"),
        P(None, "head"),
        P(None, "head"),
        P("head", None),
        P(None, "head"),
        P(None, "head"),
        P(None, "head"),
        P("head", None),
    )
    return jax.shard_map(
        per_device,
        mesh=mesh,
        in_specs=placed,
        out_specs=P(("grp", "pos"), "read", "head"),
        check_vma=False,
    )
```

```python
import functools

import jax
import jax.numpy as jnp
from jax import lax
from jax.experimental import pallas as pl
from jax.experimental.pallas import tpu as pltpu
from jax.sharding import PartitionSpec as P


HD = 64
EPSILON = 1e-06
NEG = -1e30
CHUNK = 256
STATS = 128
ROWS = 16
F32 = jnp.float32
BF16 = jnp.bfloat16


def nt_dot(left, right):
    return lax.dot_general(left, right, (((1,), (1,)), ((), ())), preferred_element_type=F32)


def mm(left, right):
    return jnp.dot(left, right, preferred_element_type=F32)


def rms_rows(values):
    return values * lax.rsqrt(jnp.mean(values * values, axis=-1, keepdims=True) + EPSILON)


def spread_queries(query, heads, target):
    rows, width = query.shape
    lane = lax.broadcasted_iota(jnp.int32, (rows, 128), 1)
    for head in range(heads):
        inside = (lane >= HD) if head % 2 else (lane < HD)
        for tile in range(width // 128):
            cols = slice(tile * 128, (tile + 1) * 128)
            kept = jnp.zeros((rows, 128), BF16)
            if tile == head // 2:
                kept = jnp.where(inside, query[:, cols].astype(F32), 0.0).astype(BF16)
            target[head * rows : (head + 1) * rows, cols] = kept


def tile_fold(values, combine):
    folded = values[:, :128]
    for tile in range(1, values.shape[1] // 128):
        folded = combine(folded, values[:, tile * 128 : (tile + 1) * 128])
    return folded


def emit(segment, row_max, row_total, acc, heads, full, stat_full, own_ref, own_stat_ref, sends):
    readers = len(sends) + 1
    rows, width = full.shape
    part = rows // readers
    lane = lax.broadcasted_iota(jnp.int32, (rows, 128), 1)
    group = STATS // heads

    def compact(values):
        packed = values[:rows]
        for head in range(1, heads):
            packed = jnp.where(lane < head * group, packed, values[head * rows : (head + 1) * rows])
        return packed

    divisor = jnp.where(row_total > 0, row_total, 1.0)
    packed_total = compact(row_total)
    level = jnp.where(
        packed_total > 0, compact(row_max) + jnp.log(jnp.where(packed_total > 0, packed_total, 1.0)),
        NEG,
    )
    for tile in range(width // 128):
        low = slice(2 * tile * rows, (2 * tile + 1) * rows)
        high = slice((2 * tile + 1) * rows, (2 * tile + 2) * rows)
        cols = slice(tile * 128, (tile + 1) * 128)
        full[:, cols] = jnp.where(lane < HD, acc[low, cols], acc[high, cols]) / jnp.where(
            lane < HD, divisor[low], divisor[high]
        )
    stats = jnp.zeros((rows, STATS), F32)
    for step in range(3):
        piece = level.astype(BF16).astype(F32)
        stats = jnp.where(lax.rem(lane, group) == step, piece, stats)
        level = level - piece
    stat_full[...] = stats
    reader = lax.axis_index("read")
    for step in range(readers):
        first = pl.multiple_of(lax.rem(reader + step, readers) * part, part)
        if step == 0:
            own_ref[segment] = full[pl.ds(first, part), :]
            own_stat_ref[segment] = stat_full[pl.ds(first, part), :].astype(BF16)
        else:
            sends[step - 1][segment, :, :width] = full[pl.ds(first, part), :].astype(BF16)
            sends[step - 1][segment, :, width:] = stat_full[pl.ds(first, part), :].astype(BF16)


def cross_kernel(
    readers, start_hbm, cov_hbm, present_hbm, lat_hbm, tok_ref, wq_hbm, wk_hbm, wv_hbm, *rest
):
    own_ref, own_stat_ref = rest[:2]
    sends = rest[2 : 1 + readers]
    (start_ref, cov_ref, present_ref, seg_of, low_of, high_of, lat_ref, wq_ref, wk_ref, wv_ref,
     token_buf, spread, key_buf, score_buf, value_buf, max_buf, total_buf, acc, full, stat_full,
     load_sems, sems) = rest[1 + readers :]
    loads = [
        pltpu.make_async_copy(source, target, load_sems.at[index])
        for index, (source, target) in enumerate(
            (
                (start_hbm, start_ref),
                (cov_hbm, cov_ref),
                (present_hbm, present_ref),
                (lat_hbm, lat_ref),
                (wq_hbm, wq_ref),
                (wk_hbm, wk_ref),
                (wv_hbm, wv_ref),
            )
        )
    ]
    for load in loads:
        load.start()
    for load in loads[:3]:
        load.wait()
    segs, lat_rows, width = lat_ref.shape
    reads = tok_ref.shape[1]
    local = wq_ref.shape[1]
    heads = local // HD

    used = jnp.int32(0)
    for segment in range(segs):
        offset = used * CHUNK
        for read in range(reads):
            start = start_ref[segment, read]
            length = cov_ref[segment, read]
            live = present_ref[segment, read] > 0
            first = (start // ROWS) * ROWS
            last = ((start + length + ROWS - 1) // ROWS) * ROWS
            rows = jnp.where(live, last - first, 0)
            low_of[segment, read] = offset + start - first
            high_of[segment, read] = offset + jnp.where(live, start - first + length, 0)

            @pl.when(live)
            def _(segment=segment, read=read, offset=offset, first=first, rows=rows):
                pltpu.make_async_copy(
                    tok_ref.at[segment, read, pl.ds(pl.multiple_of(first, ROWS), rows), :],
                    token_buf.at[pl.ds(pl.multiple_of(offset, ROWS), rows), :],
                    sems.at[segment],
                ).start()

            offset = offset + rows
        low_of[segment, reads] = offset - used * CHUNK
        chunks = (offset - used * CHUNK + CHUNK - 1) // CHUNK

        def clear(step, carry, offset=offset):
            token_buf[pl.ds(pl.multiple_of(offset + step * ROWS, ROWS), ROWS), :] = jnp.zeros(
                (ROWS, width), BF16
            )
            return carry

        lax.fori_loop(0, ((used + chunks) * CHUNK - offset) // ROWS, clear, 0)

        def note(step, carry, segment=segment, used=used):
            seg_of[used + step] = segment
            return carry

        lax.fori_loop(0, chunks, note, 0)
        used = used + chunks
    for step in range(3):
        seg_of[used + step] = segs
    for read in range(reads):
        low_of[segs, read] = 0
        high_of[segs, read] = 0

    max_buf[...] = jnp.full(max_buf.shape, NEG, F32)
    total_buf[...] = jnp.zeros(total_buf.shape, F32)
    acc[...] = jnp.zeros(acc.shape, F32)
    for load in loads[3:]:
        load.wait()
    normed = rms_rows(lat_ref[...].reshape(segs * lat_rows, width).astype(F32)).astype(BF16)
    query = (mm(normed, wq_ref[...]) * (HD ** (-0.5))).astype(BF16)
    for segment in range(segs):
        spread_queries(
            query[segment * lat_rows : (segment + 1) * lat_rows], heads, spread.at[segment]
        )

    def landed(segment):
        size = pl.multiple_of(low_of[segment, reads], ROWS)
        whole = token_buf.at[pl.ds(0, size), :]
        pltpu.make_async_copy(whole, whole, sems.at[segment]).wait()

    def projected(pair):
        place = pl.ds(pl.multiple_of(pair * 2 * CHUNK, 2 * CHUNK), 2 * CHUNK)
        tokens = token_buf[place, :]
        key_buf[lax.rem(pair, 2)] = mm(tokens, wk_ref[...]).astype(BF16)
        value_buf[place, :] = mm(tokens, wv_ref[...]).astype(BF16)

    def arrive(chunk, before):
        upcoming = seg_of[chunk]

        @pl.when((upcoming != before) & (upcoming < segs))
        def _():
            landed(upcoming)

    pairs = (used + 1) // 2

    @pl.when(used > 0)
    def _():
        arrive(0, -1)
        arrive(1, seg_of[0])
        projected(jnp.int32(0))

    def first_pass(pair, carry):
        chunk = 2 * pair
        arrive(chunk + 2, seg_of[chunk + 1])
        arrive(chunk + 3, seg_of[chunk + 2])
        keys = key_buf[lax.rem(pair, 2)]
        segments = [seg_of[chunk], seg_of[chunk + 1]]
        for half in range(2):
            segment = segments[half]
            place = (chunk + half) * CHUNK + lax.broadcasted_iota(jnp.int32, (1, CHUNK), 1)
            live = jnp.zeros((1, CHUNK), jnp.bool_)
            for read in range(reads):
                live = live | (
                    (place >= low_of[segment, read]) & (place < high_of[segment, read])
                )
            for block in range(2):
                size = acc.shape[1] // 2
                rows = slice(block * size, (block + 1) * size)
                scores = nt_dot(
                    spread[segment, rows], keys[half * CHUNK : (half + 1) * CHUNK]
                )
                scores = jnp.where(live, scores, NEG)
                score_buf[chunk + half, rows] = scores
                max_buf[segment, rows] = jnp.maximum(
                    max_buf[segment, rows], tile_fold(scores, jnp.maximum)
                )
        projected(pair + 1)
        return carry

    lax.fori_loop(0, pairs, first_pass, 0)
    for segment in range(segs):
        row_max = jnp.max(max_buf[segment], axis=1, keepdims=True)
        max_buf[segment] = jnp.broadcast_to(row_max, max_buf.shape[1:])

    def second_pass(pair, carry):
        for half in range(2):
            chunk = 2 * pair + half
            segment = seg_of[chunk]
            value = value_buf[pl.ds(pl.multiple_of(chunk * CHUNK, CHUNK), CHUNK), :]
            for block in range(2):
                rows = slice(block * acc.shape[1] // 2, (block + 1) * acc.shape[1] // 2)
                weights = jnp.exp(
                    score_buf[chunk, rows] - jnp.tile(max_buf[segment, rows], (1, CHUNK // 128))
                )
                total_buf[segment, rows] += tile_fold(weights, jnp.add)
                acc[segment, rows] += mm(weights.astype(BF16), value)
        return carry

    lax.fori_loop(0, pairs, second_pass, 0)

    def finish(segment, carry):
        row_total = jnp.sum(total_buf[segment], axis=1, keepdims=True)
        row_total = jnp.broadcast_to(row_total, total_buf.shape[1:])
        emit(
            segment, max_buf[segment], row_total, acc.at[segment], heads, full, stat_full,
            own_ref, own_stat_ref, sends,
        )
        return carry

    lax.fori_loop(0, segs, finish, 0)


def row_levels(stats, width):
    group = STATS // (width // HD)
    lane = lax.broadcasted_iota(jnp.int32, (STATS, width), 0)
    head = lax.broadcasted_iota(jnp.int32, (STATS, width), 1) // HD
    pick = ((lane // group == head) & (lax.rem(lane, group) < 3)).astype(F32).astype(BF16)
    return mm(stats, pick)


def own_kernel(own_ref, stat_ref, kept_ref, level_ref):
    kept_ref[...] = own_ref[...]
    level_ref[...] = row_levels(stat_ref[...], own_ref.shape[1])


def combine_kernel(own_ref, level_ref, *rest):
    received, out_ref = rest[:-1], rest[-1]
    width = own_ref.shape[1]
    parts = [own_ref[...]] + [ref[:, :width].astype(F32) for ref in received]
    levels = [level_ref[...]] + [row_levels(ref[:, width:], width) for ref in received]
    joint = functools.reduce(jnp.maximum, levels)
    factors = [jnp.exp(level - joint) for level in levels]
    mixed = sum(part * factor for part, factor in zip(parts, factors))
    out_ref[...] = (mixed / sum(factors)).astype(BF16)


def hidden_kernel(
    lat_ref, own_ref, other_ref, wo_ref, wp_ref, wq_ref, hid_ref, norm_ref, query_ref
):
    segs, _, _ = lat_ref.shape
    part = own_ref.shape[0] // segs
    first = pl.multiple_of(lax.axis_index("read") * part, part)
    delta = mm(own_ref[...], wo_ref[...]) + mm(other_ref[...], wp_ref[...])
    for segment in range(segs):
        rows = slice(segment * part, (segment + 1) * part)
        hid_ref[rows, :] = lat_ref[segment, pl.ds(first, part), :].astype(F32) + delta[rows]
    normed = rms_rows(hid_ref[...]).astype(BF16)
    norm_ref[...] = normed
    query_ref[...] = (mm(normed, wq_ref[...]) * (HD ** (-0.5))).astype(BF16)


def project_blocks(blocks, slots, wk_ref, wv_ref, key_all, value_all):
    for block, slot in zip(blocks, slots):
        size = block.shape[0]
        place = pl.ds(pl.multiple_of(slot * size, size), size)
        key_all[place, :] = mm(block[...], wk_ref[...]).astype(BF16)
        value_all[place, :] = mm(block[...], wv_ref[...]).astype(BF16)


def collect(segment, segs, part, slot_of, offsets, pattern_ref, sources, targets):
    seg_total = pattern_ref.shape[1]
    home = lax.axis_index("pos") * segs + segment
    live = jnp.int32(0)
    for offset in offsets:
        block_step, inner = divmod(segment + offset, segs)
        if block_step not in slot_of:
            continue
        inside = (home + offset >= 0) & (home + offset < seg_total)
        flag = pattern_ref[segment, jnp.clip(home + offset, 0, seg_total - 1)]
        chosen = inside & (flag > 0)
        source = (slot_of[block_step] * segs + inner) * part

        @pl.when(chosen)
        def _(live=live, source=source):
            place = pl.ds(pl.multiple_of(live * part, part), part)
            for whole, packed in zip(sources, targets):
                packed[place, :] = whole[source : source + part, :]

        live = live + chosen.astype(jnp.int32)
    return live


def near_kernel(readers, offsets, pattern_ref, wk_ref, wv_ref, *rest):
    queries = rest[:readers]
    own, ahead, behind = rest[readers : readers + 3]
    spread, max_out, total_out, acc = rest[readers + 3 : readers + 7]
    query_buf, key_all, value_all, key_buf, value_buf, score_buf = rest[readers + 7 :]
    segs, spread_rows, local = spread.shape
    lat_rows = query_buf.shape[1]
    part = lat_rows // readers
    heads = local // HD
    reader = lax.axis_index("read")
    core = lax.axis_index("head")

    key_buf[...] = jnp.zeros(key_buf.shape, BF16)
    value_buf[...] = jnp.zeros(value_buf.shape, BF16)
    project_blocks(
        (own, ahead, behind), (0, 1 + core, 2 - core), wk_ref, wv_ref, key_all, value_all
    )
    for step in range(readers):
        first = pl.multiple_of(lax.rem(reader + readers - step, readers) * part, part)
        for segment in range(segs):
            query_buf[segment, pl.ds(first, part), :] = queries[step][
                segment * part : (segment + 1) * part, :
            ]

    for segment in range(segs):
        spread_queries(query_buf[segment], heads, spread.at[segment])
        live = collect(
            segment, segs, part, {0: 0, -1: 1, 1: 2}, offsets, pattern_ref,
            (key_all, value_all), (key_buf, value_buf),
        )
        max_out[segment] = jnp.full(max_out.shape[1:], NEG, F32)
        total_out[segment] = jnp.zeros(total_out.shape[1:], F32)
        acc[segment] = jnp.zeros(acc.shape[1:], F32)

        def first_pass(chunk, carry, segment=segment, live=live):
            base = pl.multiple_of(chunk * CHUNK, CHUNK)
            place = base + lax.broadcasted_iota(jnp.int32, (1, CHUNK), 1)
            scores = nt_dot(spread[segment], key_buf[pl.ds(base, CHUNK), :])
            scores = jnp.where(place < live * part, scores, NEG)
            score_buf[chunk] = scores
            max_out[segment] = jnp.maximum(max_out[segment], tile_fold(scores, jnp.maximum))
            return carry

        chunks = (live * part + CHUNK - 1) // CHUNK
        lax.fori_loop(0, chunks, first_pass, 0)
        row_max = jnp.max(max_out[segment], axis=1, keepdims=True)
        max_out[segment] = jnp.broadcast_to(row_max, max_out.shape[1:])

        def second_pass(chunk, carry, segment=segment):
            value = value_buf[pl.ds(pl.multiple_of(chunk * CHUNK, CHUNK), CHUNK), :]
            for block in range(2):
                rows = slice(block * spread_rows // 2, (block + 1) * spread_rows // 2)
                weights = jnp.exp(
                    score_buf[chunk, rows] - jnp.tile(max_out[segment, rows], (1, CHUNK // 128))
                )
                total_out[segment, rows] += tile_fold(weights, jnp.add)
                acc[segment, rows] += mm(weights.astype(BF16), value)
            return carry

        lax.fori_loop(0, chunks, second_pass, 0)


def far_kernel(readers, steps, offsets, pattern_ref, wk_ref, wv_ref, *rest):
    spread, max_in, total_in, acc_in = rest[:4]
    blocks = rest[4 : 4 + 2 * len(steps)]
    rest = rest[4 + 2 * len(steps) :]
    own_ref, own_stat_ref = rest[:2]
    sends = rest[2 : 1 + readers]
    key_all, value_all, key_buf, value_buf, max_buf, total_buf, acc, full, stat_full = rest[
        1 + readers :
    ]
    segs, _, local = spread.shape
    heads = local // HD
    part = own_ref.shape[1]
    core = lax.axis_index("head")
    many = key_buf.shape[0]

    key_buf[...] = jnp.zeros(key_buf.shape, BF16)
    value_buf[...] = jnp.zeros(value_buf.shape, BF16)
    slots, slot_of = [], {}
    for index, step in enumerate(steps):
        slots += [2 * index + core, 2 * index + 1 - core]
        slot_of[-step], slot_of[step] = 2 * index, 2 * index + 1
    project_blocks(blocks, slots, wk_ref, wv_ref, key_all, value_all)

    for segment in range(segs):
        live = collect(
            segment, segs, part, slot_of, offsets, pattern_ref,
            (key_all, value_all), (key_buf, value_buf),
        )
        place = lax.broadcasted_iota(jnp.int32, (1, many), 1)
        scores = nt_dot(spread[segment], key_buf[...])
        scores = jnp.where(place < live * part, scores, NEG)
        before = max_in[segment]
        top = jnp.max(tile_fold(scores, jnp.maximum), axis=1, keepdims=True)
        max_buf[...] = jnp.maximum(before, jnp.broadcast_to(top, before.shape))
        factor = jnp.exp(before - max_buf[...])
        weights = jnp.exp(scores - jnp.tile(max_buf[...], (1, many // 128)))
        total_buf[...] = total_in[segment] * factor + tile_fold(weights, jnp.add)
        acc[...] = acc_in[segment] * jnp.tile(factor, (1, local // 128)) + mm(
            weights.astype(BF16), value_buf[...]
        )
        row_total = jnp.sum(total_buf[...], axis=1, keepdims=True)
        emit(
            segment, max_buf[...], jnp.broadcast_to(row_total, total_buf.shape), acc, heads, full,
            stat_full, own_ref, own_stat_ref, sends,
        )


def out_kernel(hid_ref, own_ref, other_ref, wo_ref, wp_ref, out_ref):
    segs, part, share = out_ref.shape
    cols = pl.ds(pl.multiple_of(lax.axis_index("head") * share, 128), share)
    result = (
        hid_ref[:, cols] + mm(own_ref[...], wo_ref[:, cols]) + mm(other_ref[...], wp_ref[:, cols])
    )
    for segment in range(segs):
        out_ref[segment] = result[segment * part : (segment + 1) * part].astype(BF16)


def cost(flops, moved, exps=0):
    return pl.CostEstimate(flops=int(flops), bytes_accessed=int(moved), transcendentals=int(exps))


def vmem():
    return pl.BlockSpec(memory_space=pltpu.VMEM)


def smem():
    return pl.BlockSpec(memory_space=pltpu.SMEM)


def call(kernel, inputs, outputs, specs=None, scratch=(), estimate=None, limit=8 << 20):
    return pl.pallas_call(
        kernel,
        out_shape=[jax.ShapeDtypeStruct(shape, kind) for shape, kind in outputs],
        in_specs=specs or [vmem() for _ in inputs],
        out_specs=[vmem() for _ in outputs],
        scratch_shapes=list(scratch),
        cost_estimate=estimate,
        compiler_params=pltpu.CompilerParams(vmem_limit_bytes=limit),
    )(*inputs)


def swap_cores(value):
    return lax.ppermute(value, "head", [(0, 1), (1, 0)])


def to_reader(value, step):
    readers = lax.axis_size("read")
    return lax.ppermute(value, "read", [(i, (i + step) % readers) for i in range(readers)])


def both_ways(value, step):
    count = lax.axis_size("pos")
    moves = []
    for place in range(count):
        if place + step < count:
            moves.append((2 * place, 2 * (place + step)))
        if place - step >= 0:
            moves.append((2 * place + 1, 2 * (place - step) + 1))
    return lax.ppermute(value, ("pos", "head"), moves)


def layer(
    latents, read_tokens, band_start, coverage, present, pattern, cross_query, cross_key,
    cross_value, cross_out, self_query, self_key, self_value, self_out,
):
    segs, lat_rows, width = latents.shape
    reads, length = read_tokens.shape[1:3]
    local = cross_query.shape[1]
    heads = local // HD
    readers = lax.axis_size("read")
    part = lat_rows // readers
    size = segs * part
    seg_total = pattern.shape[1]
    share = width // lax.axis_size("head")
    spread_rows = heads * lat_rows

    offsets = [0]
    distance = 1
    while distance < seg_total:
        offsets += [distance, -distance]
        distance *= 2
    steps = sorted(
        {abs((seg + off) // segs) for off in offsets for seg in range(segs)} - {0}
    )

    cross_out_other = swap_cores(cross_out)
    self_out_other = swap_cores(self_out)

    part_outputs = [((segs, part, local), F32), ((segs, part, STATS), BF16)] + [
        ((segs, part, local + STATS), BF16)
    ] * (readers - 1)
    work = [pltpu.VMEM((lat_rows, local), F32), pltpu.VMEM((lat_rows, STATS), F32)]
    most = reads * length
    tiles = -(-most // CHUNK)
    spare = (segs * tiles + 1) // 2 * 2 + 2
    produced = call(
        functools.partial(cross_kernel, readers),
        (band_start, coverage, present, latents, read_tokens, cross_query, cross_key, cross_value),
        part_outputs,
        specs=[pl.BlockSpec(memory_space=pltpu.HBM)] * 8,
        scratch=[
            pltpu.SMEM(band_start.shape, jnp.int32),
            pltpu.SMEM(coverage.shape, jnp.int32),
            pltpu.SMEM(present.shape, jnp.int32),
            pltpu.SMEM((segs * tiles + 3,), jnp.int32),
            pltpu.SMEM((segs + 1, reads + 1), jnp.int32),
            pltpu.SMEM((segs + 1, reads), jnp.int32),
            pltpu.VMEM(latents.shape, BF16),
            pltpu.VMEM(cross_query.shape, BF16),
            pltpu.VMEM(cross_key.shape, BF16),
            pltpu.VMEM(cross_value.shape, BF16),
            pltpu.VMEM((spare * CHUNK, width), BF16),
            pltpu.VMEM((segs + 1, spread_rows, local), BF16),
            pltpu.VMEM((2, 2 * CHUNK, local), BF16),
            pltpu.VMEM((segs * tiles + 1, spread_rows, CHUNK), F32),
            pltpu.VMEM((spare * CHUNK, local), BF16),
            pltpu.VMEM((segs + 1, spread_rows, 128), F32),
            pltpu.VMEM((segs + 1, spread_rows, 128), F32),
            pltpu.VMEM((segs + 1, spread_rows, local), F32),
        ]
        + work
        + [pltpu.SemaphoreType.DMA((7,)), pltpu.SemaphoreType.DMA((segs,))],
        estimate=cost(
            2 * segs * most * local * (2 * width + 2 * spread_rows),
            2 * segs * most * width,
            segs * most * spread_rows,
        ),
        limit=60 * 1024 * 1024,
    )

    def combine(parts):
        own, own_stat, sends = parts[0], parts[1], parts[2:]
        received = [to_reader(value, step + 1) for step, value in enumerate(sends)]
        kept, level = call(
            own_kernel,
            (own.reshape(size, local), own_stat.reshape(size, STATS)),
            [((size, local), F32), ((size, local), F32)],
            estimate=cost(2 * size * STATS * local, 12 * size * local),
        )
        return call(
            combine_kernel,
            [kept, level] + [value.reshape(size, local + STATS) for value in received],
            [((size, local), BF16)],
            estimate=cost(8 * size * STATS * local, 8 * size * local),
        )[0]

    attended = combine(produced)
    attended_other = swap_cores(attended)
    hidden, normed, query = call(
        hidden_kernel,
        (latents, attended, attended_other, cross_out, cross_out_other, self_query),
        [((size, width), F32), ((size, width), BF16), ((size, local), BF16)],
        estimate=cost(2 * size * width * (width + local), 8 * size * width),
    )
    queries = [query] + [to_reader(query, step) for step in range(1, readers)]
    direct, pair = {}, {}
    for step in steps:
        half = step // 2
        if half in direct and 2 * half == step:
            direct[step] = both_ways(direct[half], half)
        else:
            direct[step] = both_ways(normed, step)
        pair[step] = (direct[step], swap_cores(direct[step]))
    state = [
        ((segs, spread_rows, local), BF16),
        ((segs, spread_rows, 128), F32),
        ((segs, spread_rows, 128), F32),
        ((segs, spread_rows, local), F32),
    ]

    def reach(test):
        return max(
            sum(test(abs((segment + offset) // segs)) for offset in offsets)
            for segment in range(segs)
        )

    near_keys = -(-reach(lambda step: step <= 1) * part // CHUNK) * CHUNK
    far_keys = -(-reach(lambda step: step > 1) * part // 128) * 128
    carried = call(
        functools.partial(near_kernel, readers, tuple(offsets)),
        (pattern, self_key, self_value, *queries, normed, *pair[1]),
        state,
        specs=[smem()] + [vmem()] * (5 + len(queries)),
        scratch=[
            pltpu.VMEM((segs, lat_rows, local), BF16),
            pltpu.VMEM((3 * size, local), BF16),
            pltpu.VMEM((3 * size, local), BF16),
            pltpu.VMEM((near_keys, local), BF16),
            pltpu.VMEM((near_keys, local), BF16),
            pltpu.VMEM((near_keys // CHUNK, spread_rows, CHUNK), F32),
        ],
        estimate=cost(4 * segs * near_keys * local * spread_rows, 8 * segs * spread_rows * local),
        limit=16 << 20,
    )
    far = [step for step in steps if step > 1]
    far_blocks = [block for step in far for block in pair[step]]
    produced = call(
        functools.partial(far_kernel, readers, tuple(far), tuple(offsets)),
        (pattern, self_key, self_value, *carried, *far_blocks),
        part_outputs,
        specs=[smem()] + [vmem()] * (6 + len(far_blocks)),
        scratch=[
            pltpu.VMEM((len(far_blocks) * size, local), BF16),
            pltpu.VMEM((len(far_blocks) * size, local), BF16),
            pltpu.VMEM((far_keys, local), BF16),
            pltpu.VMEM((far_keys, local), BF16),
            pltpu.VMEM((spread_rows, 128), F32),
            pltpu.VMEM((spread_rows, 128), F32),
            pltpu.VMEM((spread_rows, local), F32),
        ]
        + work,
        estimate=cost(
            4 * segs * far_keys * local * spread_rows, 8 * segs * spread_rows * local
        ),
        limit=16 << 20,
    )
    mixed = combine(produced)
    mixed_other = swap_cores(mixed)
    return call(
        out_kernel,
        (hidden, mixed, mixed_other, self_out, self_out_other),
        [((segs, part, share), BF16)],
        estimate=cost(2 * size * width * share, 8 * size * width),
    )[0]


def solution(mesh):
    placed = (
        P(("grp", "pos"), None, None),
        P(("grp", "pos"), "read", None, None),
        P(("grp", "pos"), "read"),
        P(("grp", "pos"), "read"),
        P(("grp", "pos"), "read"),
        P(("grp", "pos"), None),
        P(None, "head"),
        P(None, "head"),
        P(None, "head"),
        P("head", None),
        P(None, "head"),
        P(None, "head"),
        P(None, "head"),
        P("head", None),
    )
    return jax.shard_map(
        layer,
        mesh=mesh,
        in_specs=placed,
        out_specs=P(("grp", "pos"), "read", "head"),
        check_vma=False,
    )
```

```python
import functools

import jax
import jax.numpy as jnp
from jax import lax
from jax.experimental import pallas as pl
from jax.experimental.pallas import tpu as pltpu
from jax.sharding import PartitionSpec as P


HD = 64
EPSILON = 1e-06
NEG = -1e30
CHUNK = 256
STATS = 128
ROWS = 16
F32 = jnp.float32
BF16 = jnp.bfloat16


def nt_dot(left, right):
    return lax.dot_general(left, right, (((1,), (1,)), ((), ())), preferred_element_type=F32)


def mm(left, right):
    return jnp.dot(left, right, preferred_element_type=F32)


def rms_rows(values):
    return values * lax.rsqrt(jnp.mean(values * values, axis=-1, keepdims=True) + EPSILON)


def spread_queries(query, heads, target):
    rows, width = query.shape
    lane = lax.broadcasted_iota(jnp.int32, (rows, 128), 1)
    for head in range(heads):
        inside = (lane >= HD) if head % 2 else (lane < HD)
        for tile in range(width // 128):
            cols = slice(tile * 128, (tile + 1) * 128)
            kept = jnp.zeros((rows, 128), BF16)
            if tile == head // 2:
                kept = jnp.where(inside, query[:, cols].astype(F32), 0.0).astype(BF16)
            target[head * rows : (head + 1) * rows, cols] = kept


def tile_fold(values, combine):
    folded = values[:, :128]
    for tile in range(1, values.shape[1] // 128):
        folded = combine(folded, values[:, tile * 128 : (tile + 1) * 128])
    return folded


def emit(segment, row_max, row_total, acc, heads, full, stat_full, own_ref, own_stat_ref, sends):
    readers = len(sends) + 1
    rows, width = full.shape
    part = rows // readers
    lane = lax.broadcasted_iota(jnp.int32, (rows, 128), 1)
    group = STATS // heads

    def compact(values):
        packed = values[:rows]
        for head in range(1, heads):
            packed = jnp.where(lane < head * group, packed, values[head * rows : (head + 1) * rows])
        return packed

    divisor = jnp.where(row_total > 0, row_total, 1.0)
    packed_total = compact(row_total)
    level = jnp.where(
        packed_total > 0, compact(row_max) + jnp.log(jnp.where(packed_total > 0, packed_total, 1.0)),
        NEG,
    )
    for tile in range(width // 128):
        low = slice(2 * tile * rows, (2 * tile + 1) * rows)
        high = slice((2 * tile + 1) * rows, (2 * tile + 2) * rows)
        cols = slice(tile * 128, (tile + 1) * 128)
        full[:, cols] = jnp.where(lane < HD, acc[low, cols], acc[high, cols]) / jnp.where(
            lane < HD, divisor[low], divisor[high]
        )
    stats = jnp.zeros((rows, STATS), F32)
    for step in range(3):
        piece = level.astype(BF16).astype(F32)
        stats = jnp.where(lax.rem(lane, group) == step, piece, stats)
        level = level - piece
    stat_full[...] = stats
    reader = lax.axis_index("read")
    for step in range(readers):
        first = pl.multiple_of(lax.rem(reader + step, readers) * part, part)
        if step == 0:
            own_ref[segment] = full[pl.ds(first, part), :]
            own_stat_ref[segment] = stat_full[pl.ds(first, part), :].astype(BF16)
        else:
            sends[step - 1][segment, :, :width] = full[pl.ds(first, part), :].astype(BF16)
            sends[step - 1][segment, :, width:] = stat_full[pl.ds(first, part), :].astype(BF16)


def cross_kernel(
    readers, start_hbm, cov_hbm, present_hbm, lat_hbm, tok_ref, wq_hbm, wk_hbm, wv_hbm, *rest
):
    own_ref, own_stat_ref = rest[:2]
    sends = rest[2 : 1 + readers]
    (start_ref, cov_ref, present_ref, seg_of, low_of, high_of, lat_ref, wq_ref, wk_ref, wv_ref,
     token_buf, spread, key_buf, score_buf, value_buf, max_buf, total_buf, acc, full, stat_full,
     load_sems, sems) = rest[1 + readers :]
    loads = [
        pltpu.make_async_copy(source, target, load_sems.at[index])
        for index, (source, target) in enumerate(
            (
                (start_hbm, start_ref),
                (cov_hbm, cov_ref),
                (present_hbm, present_ref),
                (lat_hbm, lat_ref),
                (wq_hbm, wq_ref),
                (wk_hbm, wk_ref),
                (wv_hbm, wv_ref),
            )
        )
    ]
    for load in loads:
        load.start()
    for load in loads[:3]:
        load.wait()
    segs, lat_rows, width = lat_ref.shape
    reads = tok_ref.shape[1]
    local = wq_ref.shape[1]
    heads = local // HD

    used = jnp.int32(0)
    for segment in range(segs):
        offset = used * CHUNK
        for read in range(reads):
            start = start_ref[segment, read]
            length = cov_ref[segment, read]
            live = present_ref[segment, read] > 0
            first = (start // ROWS) * ROWS
            last = ((start + length + ROWS - 1) // ROWS) * ROWS
            rows = jnp.where(live, last - first, 0)
            low_of[segment, read] = offset + start - first
            high_of[segment, read] = offset + jnp.where(live, start - first + length, 0)

            @pl.when(live)
            def _(segment=segment, read=read, offset=offset, first=first, rows=rows):
                pltpu.make_async_copy(
                    tok_ref.at[segment, read, pl.ds(pl.multiple_of(first, ROWS), rows), :],
                    token_buf.at[pl.ds(pl.multiple_of(offset, ROWS), rows), :],
                    sems.at[segment],
                ).start()

            offset = offset + rows
        low_of[segment, reads] = offset - used * CHUNK
        chunks = (offset - used * CHUNK + CHUNK - 1) // CHUNK

        def clear(step, carry, offset=offset):
            token_buf[pl.ds(pl.multiple_of(offset + step * ROWS, ROWS), ROWS), :] = jnp.zeros(
                (ROWS, width), BF16
            )
            return carry

        lax.fori_loop(0, ((used + chunks) * CHUNK - offset) // ROWS, clear, 0)

        def note(step, carry, segment=segment, used=used):
            seg_of[used + step] = segment
            return carry

        lax.fori_loop(0, chunks, note, 0)
        used = used + chunks
    for step in range(3):
        seg_of[used + step] = segs
    for read in range(reads):
        low_of[segs, read] = 0
        high_of[segs, read] = 0

    max_buf[...] = jnp.full(max_buf.shape, NEG, F32)
    total_buf[...] = jnp.zeros(total_buf.shape, F32)
    acc[...] = jnp.zeros(acc.shape, F32)
    for load in loads[3:]:
        load.wait()
    normed = rms_rows(lat_ref[...].reshape(segs * lat_rows, width).astype(F32)).astype(BF16)
    query = (mm(normed, wq_ref[...]) * (HD ** (-0.5))).astype(BF16)
    for segment in range(segs):
        spread_queries(
            query[segment * lat_rows : (segment + 1) * lat_rows], heads, spread.at[segment]
        )

    def landed(segment):
        size = pl.multiple_of(low_of[segment, reads], ROWS)
        whole = token_buf.at[pl.ds(0, size), :]
        pltpu.make_async_copy(whole, whole, sems.at[segment]).wait()

    def projected(pair):
        place = pl.ds(pl.multiple_of(pair * 2 * CHUNK, 2 * CHUNK), 2 * CHUNK)
        tokens = token_buf[place, :]
        key_buf[lax.rem(pair, 2)] = mm(tokens, wk_ref[...]).astype(BF16)
        value_buf[place, :] = mm(tokens, wv_ref[...]).astype(BF16)

    def arrive(chunk, before):
        upcoming = seg_of[chunk]

        @pl.when((upcoming != before) & (upcoming < segs))
        def _():
            landed(upcoming)

    pairs = (used + 1) // 2

    @pl.when(used > 0)
    def _():
        arrive(0, -1)
        arrive(1, seg_of[0])
        projected(jnp.int32(0))

    def first_pass(pair, carry):
        chunk = 2 * pair
        arrive(chunk + 2, seg_of[chunk + 1])
        arrive(chunk + 3, seg_of[chunk + 2])
        keys = key_buf[lax.rem(pair, 2)]
        segments = [seg_of[chunk], seg_of[chunk + 1]]
        for half in range(2):
            segment = segments[half]
            place = (chunk + half) * CHUNK + lax.broadcasted_iota(jnp.int32, (1, CHUNK), 1)
            live = jnp.zeros((1, CHUNK), jnp.bool_)
            for read in range(reads):
                live = live | (
                    (place >= low_of[segment, read]) & (place < high_of[segment, read])
                )
            for block in range(2):
                size = acc.shape[1] // 2
                rows = slice(block * size, (block + 1) * size)
                scores = nt_dot(
                    spread[segment, rows], keys[half * CHUNK : (half + 1) * CHUNK]
                )
                scores = jnp.where(live, scores, NEG)
                score_buf[chunk + half, rows] = scores
                max_buf[segment, rows] = jnp.maximum(
                    max_buf[segment, rows], tile_fold(scores, jnp.maximum)
                )
        projected(pair + 1)
        return carry

    lax.fori_loop(0, pairs, first_pass, 0)
    for segment in range(segs):
        row_max = jnp.max(max_buf[segment], axis=1, keepdims=True)
        max_buf[segment] = jnp.broadcast_to(row_max, max_buf.shape[1:])

    def second_pass(pair, carry):
        for half in range(2):
            chunk = 2 * pair + half
            segment = seg_of[chunk]
            value = value_buf[pl.ds(pl.multiple_of(chunk * CHUNK, CHUNK), CHUNK), :]
            for block in range(2):
                rows = slice(block * acc.shape[1] // 2, (block + 1) * acc.shape[1] // 2)
                weights = jnp.exp(
                    score_buf[chunk, rows] - jnp.tile(max_buf[segment, rows], (1, CHUNK // 128))
                )
                total_buf[segment, rows] += tile_fold(weights, jnp.add)
                acc[segment, rows] += mm(weights.astype(BF16), value)
        return carry

    lax.fori_loop(0, pairs, second_pass, 0)

    def finish(segment, carry):
        row_total = jnp.sum(total_buf[segment], axis=1, keepdims=True)
        row_total = jnp.broadcast_to(row_total, total_buf.shape[1:])
        emit(
            segment, max_buf[segment], row_total, acc.at[segment], heads, full, stat_full,
            own_ref, own_stat_ref, sends,
        )
        return carry

    lax.fori_loop(0, segs, finish, 0)


def row_levels(stats, width):
    group = STATS // (width // HD)
    lane = lax.broadcasted_iota(jnp.int32, (STATS, width), 0)
    head = lax.broadcasted_iota(jnp.int32, (STATS, width), 1) // HD
    pick = ((lane // group == head) & (lax.rem(lane, group) < 3)).astype(F32).astype(BF16)
    return mm(stats, pick)


def own_kernel(own_ref, stat_ref, kept_ref, level_ref):
    kept_ref[...] = own_ref[...]
    level_ref[...] = row_levels(stat_ref[...], own_ref.shape[1])


def combine_kernel(own_ref, level_ref, *rest):
    received, out_ref = rest[:-1], rest[-1]
    width = own_ref.shape[1]
    parts = [own_ref[...]] + [ref[:, :width].astype(F32) for ref in received]
    levels = [level_ref[...]] + [row_levels(ref[:, width:], width) for ref in received]
    joint = functools.reduce(jnp.maximum, levels)
    factors = [jnp.exp(level - joint) for level in levels]
    mixed = sum(part * factor for part, factor in zip(parts, factors))
    out_ref[...] = (mixed / sum(factors)).astype(BF16)


def hidden_kernel(
    lat_ref, own_ref, other_ref, wo_ref, wp_ref, wq_ref, hid_ref, norm_ref, query_ref
):
    segs, _, _ = lat_ref.shape
    part = own_ref.shape[0] // segs
    first = pl.multiple_of(lax.axis_index("read") * part, part)
    delta = mm(own_ref[...], wo_ref[...]) + mm(other_ref[...], wp_ref[...])
    for segment in range(segs):
        rows = slice(segment * part, (segment + 1) * part)
        hid_ref[rows, :] = lat_ref[segment, pl.ds(first, part), :].astype(F32) + delta[rows]
    normed = rms_rows(hid_ref[...]).astype(BF16)
    norm_ref[...] = normed
    query_ref[...] = (mm(normed, wq_ref[...]) * (HD ** (-0.5))).astype(BF16)


def project_blocks(blocks, slots, wk_ref, wv_ref, key_all, value_all):
    for block, slot in zip(blocks, slots):
        size = block.shape[0]
        place = pl.ds(pl.multiple_of(slot * size, size), size)
        key_all[place, :] = mm(block[...], wk_ref[...]).astype(BF16)
        value_all[place, :] = mm(block[...], wv_ref[...]).astype(BF16)


def collect(segment, segs, part, slot_of, offsets, pattern_ref, sources, targets):
    seg_total = pattern_ref.shape[1]
    home = lax.axis_index("pos") * segs + segment
    live = jnp.int32(0)
    for offset in offsets:
        block_step, inner = divmod(segment + offset, segs)
        if block_step not in slot_of:
            continue
        inside = (home + offset >= 0) & (home + offset < seg_total)
        flag = pattern_ref[segment, jnp.clip(home + offset, 0, seg_total - 1)]
        chosen = inside & (flag > 0)
        source = (slot_of[block_step] * segs + inner) * part

        @pl.when(chosen)
        def _(live=live, source=source):
            place = pl.ds(pl.multiple_of(live * part, part), part)
            for whole, packed in zip(sources, targets):
                packed[place, :] = whole[source : source + part, :]

        live = live + chosen.astype(jnp.int32)
    return live


def near_kernel(readers, offsets, pattern_ref, wk_ref, wv_ref, *rest):
    queries = rest[:readers]
    own, ahead, behind = rest[readers : readers + 3]
    spread, max_out, total_out, acc = rest[readers + 3 : readers + 7]
    query_buf, key_all, value_all, key_buf, value_buf, score_buf = rest[readers + 7 :]
    segs, spread_rows, local = spread.shape
    lat_rows = query_buf.shape[1]
    part = lat_rows // readers
    heads = local // HD
    reader = lax.axis_index("read")
    core = lax.axis_index("head")

    key_buf[...] = jnp.zeros(key_buf.shape, BF16)
    value_buf[...] = jnp.zeros(value_buf.shape, BF16)
    project_blocks(
        (own, ahead, behind), (0, 1 + core, 2 - core), wk_ref, wv_ref, key_all, value_all
    )
    for step in range(readers):
        first = pl.multiple_of(lax.rem(reader + readers - step, readers) * part, part)
        for segment in range(segs):
            query_buf[segment, pl.ds(first, part), :] = queries[step][
                segment * part : (segment + 1) * part, :
            ]

    for segment in range(segs):
        spread_queries(query_buf[segment], heads, spread.at[segment])
        live = collect(
            segment, segs, part, {0: 0, -1: 1, 1: 2}, offsets, pattern_ref,
            (key_all, value_all), (key_buf, value_buf),
        )
        max_out[segment] = jnp.full(max_out.shape[1:], NEG, F32)
        total_out[segment] = jnp.zeros(total_out.shape[1:], F32)
        acc[segment] = jnp.zeros(acc.shape[1:], F32)

        def first_pass(chunk, carry, segment=segment, live=live):
            base = pl.multiple_of(chunk * CHUNK, CHUNK)
            place = base + lax.broadcasted_iota(jnp.int32, (1, CHUNK), 1)
            scores = nt_dot(spread[segment], key_buf[pl.ds(base, CHUNK), :])
            scores = jnp.where(place < live * part, scores, NEG)
            score_buf[chunk] = scores
            max_out[segment] = jnp.maximum(max_out[segment], tile_fold(scores, jnp.maximum))
            return carry

        chunks = (live * part + CHUNK - 1) // CHUNK
        lax.fori_loop(0, chunks, first_pass, 0)
        row_max = jnp.max(max_out[segment], axis=1, keepdims=True)
        max_out[segment] = jnp.broadcast_to(row_max, max_out.shape[1:])

        def second_pass(chunk, carry, segment=segment):
            value = value_buf[pl.ds(pl.multiple_of(chunk * CHUNK, CHUNK), CHUNK), :]
            for block in range(2):
                rows = slice(block * spread_rows // 2, (block + 1) * spread_rows // 2)
                weights = jnp.exp(
                    score_buf[chunk, rows] - jnp.tile(max_out[segment, rows], (1, CHUNK // 128))
                )
                total_out[segment, rows] += tile_fold(weights, jnp.add)
                acc[segment, rows] += mm(weights.astype(BF16), value)
            return carry

        lax.fori_loop(0, chunks, second_pass, 0)


def far_kernel(readers, steps, offsets, pattern_ref, wk_ref, wv_ref, *rest):
    spread, max_in, total_in, acc_in = rest[:4]
    blocks = rest[4 : 4 + 2 * len(steps)]
    rest = rest[4 + 2 * len(steps) :]
    own_ref, own_stat_ref = rest[:2]
    sends = rest[2 : 1 + readers]
    key_all, value_all, key_buf, value_buf, max_buf, total_buf, acc, full, stat_full = rest[
        1 + readers :
    ]
    segs, _, local = spread.shape
    heads = local // HD
    part = own_ref.shape[1]
    core = lax.axis_index("head")
    many = key_buf.shape[0]

    key_buf[...] = jnp.zeros(key_buf.shape, BF16)
    value_buf[...] = jnp.zeros(value_buf.shape, BF16)
    slots, slot_of = [], {}
    for index, step in enumerate(steps):
        slots += [2 * index + core, 2 * index + 1 - core]
        slot_of[-step], slot_of[step] = 2 * index, 2 * index + 1
    project_blocks(blocks, slots, wk_ref, wv_ref, key_all, value_all)

    for segment in range(segs):
        live = collect(
            segment, segs, part, slot_of, offsets, pattern_ref,
            (key_all, value_all), (key_buf, value_buf),
        )
        place = lax.broadcasted_iota(jnp.int32, (1, many), 1)
        scores = nt_dot(spread[segment], key_buf[...])
        scores = jnp.where(place < live * part, scores, NEG)
        before = max_in[segment]
        top = jnp.max(tile_fold(scores, jnp.maximum), axis=1, keepdims=True)
        max_buf[...] = jnp.maximum(before, jnp.broadcast_to(top, before.shape))
        factor = jnp.exp(before - max_buf[...])
        weights = jnp.exp(scores - jnp.tile(max_buf[...], (1, many // 128)))
        total_buf[...] = total_in[segment] * factor + tile_fold(weights, jnp.add)
        acc[...] = acc_in[segment] * jnp.tile(factor, (1, local // 128)) + mm(
            weights.astype(BF16), value_buf[...]
        )
        row_total = jnp.sum(total_buf[...], axis=1, keepdims=True)
        emit(
            segment, max_buf[...], jnp.broadcast_to(row_total, total_buf.shape), acc, heads, full,
            stat_full, own_ref, own_stat_ref, sends,
        )


def out_kernel(hid_ref, own_ref, other_ref, wo_ref, wp_ref, out_ref):
    segs, part, share = out_ref.shape
    cols = pl.ds(pl.multiple_of(lax.axis_index("head") * share, 128), share)
    result = (
        hid_ref[:, cols] + mm(own_ref[...], wo_ref[:, cols]) + mm(other_ref[...], wp_ref[:, cols])
    )
    for segment in range(segs):
        out_ref[segment] = result[segment * part : (segment + 1) * part].astype(BF16)


def cost(flops, moved, exps=0):
    return pl.CostEstimate(flops=int(flops), bytes_accessed=int(moved), transcendentals=int(exps))


def vmem():
    return pl.BlockSpec(memory_space=pltpu.VMEM)


def smem():
    return pl.BlockSpec(memory_space=pltpu.SMEM)


def call(kernel, inputs, outputs, specs=None, scratch=(), estimate=None, limit=8 << 20):
    return pl.pallas_call(
        kernel,
        out_shape=[jax.ShapeDtypeStruct(shape, kind) for shape, kind in outputs],
        in_specs=specs or [vmem() for _ in inputs],
        out_specs=[vmem() for _ in outputs],
        scratch_shapes=list(scratch),
        cost_estimate=estimate,
        compiler_params=pltpu.CompilerParams(vmem_limit_bytes=limit),
    )(*inputs)


def swap_cores(value):
    return lax.ppermute(value, "head", [(0, 1), (1, 0)])


def to_reader(value, step):
    readers = lax.axis_size("read")
    return lax.ppermute(value, "read", [(i, (i + step) % readers) for i in range(readers)])


def both_ways(value, step):
    count = lax.axis_size("pos")
    ring = [2 * place for place in range(count)]
    ring += [2 * place + 1 for place in reversed(range(count))]
    moves = [(ring[i], ring[(i + step) % len(ring)]) for i in range(len(ring))]
    return lax.ppermute(value, ("pos", "head"), moves)


def layer(
    latents, read_tokens, band_start, coverage, present, pattern, cross_query, cross_key,
    cross_value, cross_out, self_query, self_key, self_value, self_out,
):
    segs, lat_rows, width = latents.shape
    reads, length = read_tokens.shape[1:3]
    local = cross_query.shape[1]
    heads = local // HD
    readers = lax.axis_size("read")
    part = lat_rows // readers
    size = segs * part
    seg_total = pattern.shape[1]
    share = width // lax.axis_size("head")
    spread_rows = heads * lat_rows

    offsets = [0]
    distance = 1
    while distance < seg_total:
        offsets += [distance, -distance]
        distance *= 2
    steps = sorted(
        {abs((seg + off) // segs) for off in offsets for seg in range(segs)} - {0}
    )

    cross_out_other = swap_cores(cross_out)
    self_out_other = swap_cores(self_out)

    part_outputs = [((segs, part, local), F32), ((segs, part, STATS), BF16)] + [
        ((segs, part, local + STATS), BF16)
    ] * (readers - 1)
    work = [pltpu.VMEM((lat_rows, local), F32), pltpu.VMEM((lat_rows, STATS), F32)]
    most = reads * length
    tiles = -(-most // CHUNK)
    spare = (segs * tiles + 1) // 2 * 2 + 2
    produced = call(
        functools.partial(cross_kernel, readers),
        (band_start, coverage, present, latents, read_tokens, cross_query, cross_key, cross_value),
        part_outputs,
        specs=[pl.BlockSpec(memory_space=pltpu.HBM)] * 8,
        scratch=[
            pltpu.SMEM(band_start.shape, jnp.int32),
            pltpu.SMEM(coverage.shape, jnp.int32),
            pltpu.SMEM(present.shape, jnp.int32),
            pltpu.SMEM((segs * tiles + 3,), jnp.int32),
            pltpu.SMEM((segs + 1, reads + 1), jnp.int32),
            pltpu.SMEM((segs + 1, reads), jnp.int32),
            pltpu.VMEM(latents.shape, BF16),
            pltpu.VMEM(cross_query.shape, BF16),
            pltpu.VMEM(cross_key.shape, BF16),
            pltpu.VMEM(cross_value.shape, BF16),
            pltpu.VMEM((spare * CHUNK, width), BF16),
            pltpu.VMEM((segs + 1, spread_rows, local), BF16),
            pltpu.VMEM((2, 2 * CHUNK, local), BF16),
            pltpu.VMEM((segs * tiles + 1, spread_rows, CHUNK), F32),
            pltpu.VMEM((spare * CHUNK, local), BF16),
            pltpu.VMEM((segs + 1, spread_rows, 128), F32),
            pltpu.VMEM((segs + 1, spread_rows, 128), F32),
            pltpu.VMEM((segs + 1, spread_rows, local), F32),
        ]
        + work
        + [pltpu.SemaphoreType.DMA((7,)), pltpu.SemaphoreType.DMA((segs,))],
        estimate=cost(
            2 * segs * most * local * (2 * width + 2 * spread_rows),
            2 * segs * most * width,
            segs * most * spread_rows,
        ),
        limit=60 * 1024 * 1024,
    )

    def combine(parts):
        own, own_stat, sends = parts[0], parts[1], parts[2:]
        received = [to_reader(value, step + 1) for step, value in enumerate(sends)]
        kept, level = call(
            own_kernel,
            (own.reshape(size, local), own_stat.reshape(size, STATS)),
            [((size, local), F32), ((size, local), F32)],
            estimate=cost(2 * size * STATS * local, 12 * size * local),
        )
        return call(
            combine_kernel,
            [kept, level] + [value.reshape(size, local + STATS) for value in received],
            [((size, local), BF16)],
            estimate=cost(8 * size * STATS * local, 8 * size * local),
        )[0]

    attended = combine(produced)
    attended_other = swap_cores(attended)
    hidden, normed, query = call(
        hidden_kernel,
        (latents, attended, attended_other, cross_out, cross_out_other, self_query),
        [((size, width), F32), ((size, width), BF16), ((size, local), BF16)],
        estimate=cost(2 * size * width * (width + local), 8 * size * width),
    )
    queries = [query] + [to_reader(query, step) for step in range(1, readers)]
    direct, pair = {}, {}
    for step in steps:
        half = step // 2
        if half in direct and 2 * half == step:
            direct[step] = both_ways(direct[half], half)
        else:
            direct[step] = both_ways(normed, step)
        pair[step] = (direct[step], swap_cores(direct[step]))
    state = [
        ((segs, spread_rows, local), BF16),
        ((segs, spread_rows, 128), F32),
        ((segs, spread_rows, 128), F32),
        ((segs, spread_rows, local), F32),
    ]

    def reach(test):
        return max(
            sum(test(abs((segment + offset) // segs)) for offset in offsets)
            for segment in range(segs)
        )

    near_keys = -(-reach(lambda step: step <= 1) * part // CHUNK) * CHUNK
    far_keys = -(-reach(lambda step: step > 1) * part // 128) * 128
    carried = call(
        functools.partial(near_kernel, readers, tuple(offsets)),
        (pattern, self_key, self_value, *queries, normed, *pair[1]),
        state,
        specs=[smem()] + [vmem()] * (5 + len(queries)),
        scratch=[
            pltpu.VMEM((segs, lat_rows, local), BF16),
            pltpu.VMEM((3 * size, local), BF16),
            pltpu.VMEM((3 * size, local), BF16),
            pltpu.VMEM((near_keys, local), BF16),
            pltpu.VMEM((near_keys, local), BF16),
            pltpu.VMEM((near_keys // CHUNK, spread_rows, CHUNK), F32),
        ],
        estimate=cost(4 * segs * near_keys * local * spread_rows, 8 * segs * spread_rows * local),
        limit=16 << 20,
    )
    far = [step for step in steps if step > 1]
    far_blocks = [block for step in far for block in pair[step]]
    produced = call(
        functools.partial(far_kernel, readers, tuple(far), tuple(offsets)),
        (pattern, self_key, self_value, *carried, *far_blocks),
        part_outputs,
        specs=[smem()] + [vmem()] * (6 + len(far_blocks)),
        scratch=[
            pltpu.VMEM((len(far_blocks) * size, local), BF16),
            pltpu.VMEM((len(far_blocks) * size, local), BF16),
            pltpu.VMEM((far_keys, local), BF16),
            pltpu.VMEM((far_keys, local), BF16),
            pltpu.VMEM((spread_rows, 128), F32),
            pltpu.VMEM((spread_rows, 128), F32),
            pltpu.VMEM((spread_rows, local), F32),
        ]
        + work,
        estimate=cost(
            4 * segs * far_keys * local * spread_rows, 8 * segs * spread_rows * local
        ),
        limit=16 << 20,
    )
    mixed = combine(produced)
    mixed_other = swap_cores(mixed)
    return call(
        out_kernel,
        (hidden, mixed, mixed_other, self_out, self_out_other),
        [((segs, part, share), BF16)],
        estimate=cost(2 * size * width * share, 8 * size * width),
    )[0]


def solution(mesh):
    placed = (
        P(("grp", "pos"), None, None),
        P(("grp", "pos"), "read", None, None),
        P(("grp", "pos"), "read"),
        P(("grp", "pos"), "read"),
        P(("grp", "pos"), "read"),
        P(("grp", "pos"), None),
        P(None, "head"),
        P(None, "head"),
        P(None, "head"),
        P("head", None),
        P(None, "head"),
        P(None, "head"),
        P(None, "head"),
        P("head", None),
    )
    return jax.shard_map(
        layer,
        mesh=mesh,
        in_specs=placed,
        out_specs=P(("grp", "pos"), "read", "head"),
        check_vma=False,
    )
```

```python
import functools

import jax
import jax.numpy as jnp
from jax import lax
from jax.experimental import pallas as pl
from jax.experimental.pallas import tpu as pltpu
from jax.sharding import PartitionSpec as P


HD = 64
EPSILON = 1e-06
NEG = -1e30
CHUNK = 256
STATS = 128
STAT_ROWS = 16
ROWS = 16
F32 = jnp.float32
BF16 = jnp.bfloat16


def nt_dot(left, right):
    return lax.dot_general(left, right, (((1,), (1,)), ((), ())), preferred_element_type=F32)


def mm(left, right):
    return jnp.dot(left, right, preferred_element_type=F32)


def rms_rows(values):
    return values * lax.rsqrt(jnp.mean(values * values, axis=-1, keepdims=True) + EPSILON)


def spread_queries(query, heads, target):
    rows, width = query.shape
    lane = lax.broadcasted_iota(jnp.int32, (rows, 128), 1)
    for head in range(heads):
        inside = (lane >= HD) if head % 2 else (lane < HD)
        for tile in range(width // 128):
            cols = slice(tile * 128, (tile + 1) * 128)
            kept = jnp.zeros((rows, 128), BF16)
            if tile == head // 2:
                kept = jnp.where(inside, query[:, cols].astype(F32), 0.0).astype(BF16)
            target[head * rows : (head + 1) * rows, cols] = kept


def tile_fold(values, combine):
    folded = values[:, :128]
    for tile in range(1, values.shape[1] // 128):
        folded = combine(folded, values[:, tile * 128 : (tile + 1) * 128])
    return folded


def emit(segment, row_max, row_total, acc, heads, full, stat_full, own_ref, own_stat_ref, sends):
    readers = len(sends) + 1
    rows, width = full.shape
    part = rows // readers
    lane = lax.broadcasted_iota(jnp.int32, (rows, 128), 1)
    lane_head = lax.rem(lane, heads)

    def compact(values):
        packed = values[:rows]
        for head in range(1, heads):
            packed = jnp.where(lane_head == head, values[head * rows : (head + 1) * rows], packed)
        return packed

    divisor = jnp.where(row_total > 0, row_total, 1.0)
    packed_total = compact(row_total)
    level = jnp.where(
        packed_total > 0, compact(row_max) + jnp.log(jnp.where(packed_total > 0, packed_total, 1.0)),
        NEG,
    )
    for tile in range(width // 128):
        low = slice(2 * tile * rows, (2 * tile + 1) * rows)
        high = slice((2 * tile + 1) * rows, (2 * tile + 2) * rows)
        cols = slice(tile * 128, (tile + 1) * 128)
        full[:, cols] = jnp.where(lane < HD, acc[low, cols], acc[high, cols]) / jnp.where(
            lane < HD, divisor[low], divisor[high]
        )
    stats = jnp.zeros((rows, STATS), F32)
    for step in range(3):
        piece = level.astype(BF16).astype(F32)
        stats = jnp.where(lane // heads == step, piece, stats)
        level = level - piece
    stat_full[...] = stats
    flipped = stats.T[:STAT_ROWS]
    reader = lax.axis_index("read")
    for step in range(readers):
        first = pl.multiple_of(lax.rem(reader + step, readers) * part, part)
        if step == 0:
            own_ref[segment] = full[pl.ds(first, part), :]
            own_stat_ref[segment] = stat_full[pl.ds(first, part), :].astype(BF16)
        else:
            sends[step - 1][segment, :part, :] = full[pl.ds(first, part), :].astype(BF16)
            turned = pltpu.roll(flipped, lax.rem(rows - first, rows), 1)
            sends[step - 1][segment, part:, :] = jnp.concatenate(
                [turned, jnp.zeros((STAT_ROWS, width - rows), F32)], axis=1
            ).astype(BF16)


def cross_kernel(
    readers, start_hbm, cov_hbm, present_hbm, lat_hbm, tok_ref, wq_hbm, wk_hbm, wv_hbm, *rest
):
    own_ref, own_stat_ref = rest[:2]
    sends = rest[2 : 1 + readers]
    (start_ref, cov_ref, present_ref, seg_of, low_of, high_of, lat_ref, wq_ref, wk_ref, wv_ref,
     token_buf, spread, key_buf, score_buf, value_buf, max_buf, total_buf, acc, full, stat_full,
     load_sems, sems) = rest[1 + readers :]
    loads = [
        pltpu.make_async_copy(source, target, load_sems.at[index])
        for index, (source, target) in enumerate(
            (
                (start_hbm, start_ref),
                (cov_hbm, cov_ref),
                (present_hbm, present_ref),
                (lat_hbm, lat_ref),
                (wq_hbm, wq_ref),
                (wk_hbm, wk_ref),
                (wv_hbm, wv_ref),
            )
        )
    ]
    for load in loads:
        load.start()
    for load in loads[:3]:
        load.wait()
    segs, lat_rows, width = lat_ref.shape
    reads = tok_ref.shape[1]
    local = wq_ref.shape[1]
    heads = local // HD

    used = jnp.int32(0)
    for segment in range(segs):
        offset = used * CHUNK
        for read in range(reads):
            start = start_ref[segment, read]
            length = cov_ref[segment, read]
            live = present_ref[segment, read] > 0
            first = start & -ROWS
            last = (start + length + ROWS - 1) & -ROWS
            rows = pl.multiple_of(jnp.where(live, last - first, 0), ROWS)
            low_of[segment, read] = offset + start - first
            high_of[segment, read] = offset + jnp.where(live, start - first + length, 0)

            @pl.when(live)
            def _(segment=segment, read=read, offset=offset, first=first, rows=rows):
                pltpu.make_async_copy(
                    tok_ref.at[segment, read, pl.ds(pl.multiple_of(first, ROWS), rows), :],
                    token_buf.at[pl.ds(pl.multiple_of(offset, ROWS), rows), :],
                    sems.at[segment],
                ).start()

            offset = offset + rows
        low_of[segment, reads] = offset - used * CHUNK
        chunks = (offset - used * CHUNK + CHUNK - 1) // CHUNK

        def clear(step, carry, offset=offset):
            token_buf[pl.ds(pl.multiple_of(offset + step * ROWS, ROWS), ROWS), :] = jnp.zeros(
                (ROWS, width), BF16
            )
            return carry

        lax.fori_loop(0, ((used + chunks) * CHUNK - offset) // ROWS, clear, 0)

        def note(step, carry, segment=segment, used=used):
            seg_of[used + step] = segment
            return carry

        lax.fori_loop(0, chunks, note, 0)
        used = used + chunks
    for step in range(3):
        seg_of[used + step] = segs
    for read in range(reads):
        low_of[segs, read] = 0
        high_of[segs, read] = 0

    max_buf[:segs] = jnp.full((segs,) + max_buf.shape[1:], NEG, F32)
    total_buf[:segs] = jnp.zeros((segs,) + total_buf.shape[1:], F32)
    acc[:segs] = jnp.zeros((segs,) + acc.shape[1:], F32)
    for load in loads[3:]:
        load.wait()
    normed = rms_rows(lat_ref[...].reshape(segs * lat_rows, width).astype(F32)).astype(BF16)
    query = (mm(normed, wq_ref[...]) * (HD ** (-0.5))).astype(BF16)
    for segment in range(segs):
        spread_queries(
            query[segment * lat_rows : (segment + 1) * lat_rows], heads, spread.at[segment]
        )

    def landed(segment):
        size = pl.multiple_of(low_of[segment, reads], ROWS)
        whole = token_buf.at[pl.ds(0, size), :]
        pltpu.make_async_copy(whole, whole, sems.at[segment]).wait()

    def projected(pair):
        place = pl.ds(pl.multiple_of(pair * 2 * CHUNK, 2 * CHUNK), 2 * CHUNK)
        tokens = token_buf[place, :]
        key_buf[lax.rem(pair, 2)] = mm(tokens, wk_ref[...]).astype(BF16)
        value_buf[place, :] = mm(tokens, wv_ref[...]).astype(BF16)

    def arrive(chunk, before):
        upcoming = seg_of[chunk]

        @pl.when((upcoming != before) & (upcoming < segs))
        def _():
            landed(upcoming)

    pairs = (used + 1) // 2

    @pl.when(used > 0)
    def _():
        arrive(0, -1)
        arrive(1, seg_of[0])
        projected(jnp.int32(0))

    def first_pass(pair, carry):
        chunk = 2 * pair
        arrive(chunk + 2, seg_of[chunk + 1])
        arrive(chunk + 3, seg_of[chunk + 2])
        keys = key_buf[lax.rem(pair, 2)]
        segments = [seg_of[chunk], seg_of[chunk + 1]]
        for half in range(2):
            segment = segments[half]
            place = (chunk + half) * CHUNK + lax.broadcasted_iota(jnp.int32, (1, CHUNK), 1)
            live = jnp.zeros((1, CHUNK), jnp.bool_)
            for read in range(reads):
                live = live | (
                    (place >= low_of[segment, read]) & (place < high_of[segment, read])
                )
            for block in range(2):
                size = acc.shape[1] // 2
                rows = slice(block * size, (block + 1) * size)
                scores = nt_dot(
                    spread[segment, rows], keys[half * CHUNK : (half + 1) * CHUNK]
                )
                scores = jnp.where(live, scores, NEG)
                score_buf[chunk + half, rows] = scores
                max_buf[segment, rows] = jnp.maximum(
                    max_buf[segment, rows], tile_fold(scores, jnp.maximum)
                )
        projected(pair + 1)
        return carry

    lax.fori_loop(0, pairs, first_pass, 0)
    for segment in range(segs):
        row_max = jnp.max(max_buf[segment], axis=1, keepdims=True)
        max_buf[segment] = jnp.broadcast_to(row_max, max_buf.shape[1:])

    def second_pass(pair, carry):
        for half in range(2):
            chunk = 2 * pair + half
            segment = seg_of[chunk]
            value = value_buf[pl.ds(pl.multiple_of(chunk * CHUNK, CHUNK), CHUNK), :]
            for block in range(2):
                rows = slice(block * acc.shape[1] // 2, (block + 1) * acc.shape[1] // 2)
                weights = jnp.exp(
                    score_buf[chunk, rows] - jnp.tile(max_buf[segment, rows], (1, CHUNK // 128))
                )
                total_buf[segment, rows] += tile_fold(weights, jnp.add)
                acc[segment, rows] += mm(weights.astype(BF16), value)
        return carry

    lax.fori_loop(0, pairs, second_pass, 0)

    def finish(segment, carry):
        row_total = jnp.sum(total_buf[segment], axis=1, keepdims=True)
        row_total = jnp.broadcast_to(row_total, total_buf.shape[1:])
        emit(
            segment, max_buf[segment], row_total, acc.at[segment], heads, full, stat_full,
            own_ref, own_stat_ref, sends,
        )
        return carry

    lax.fori_loop(0, segs, finish, 0)


def pick_heads(rows, width):
    heads = width // HD
    place = lax.broadcasted_iota(jnp.int32, (rows, width), 0)
    head = lax.broadcasted_iota(jnp.int32, (rows, width), 1) // HD
    return ((lax.rem(place, heads) == head) & (place < 3 * heads)).astype(F32).astype(BF16)


def own_kernel(own_ref, stat_ref, kept_ref, level_ref):
    kept_ref[...] = own_ref[...]
    level_ref[...] = mm(stat_ref[...], pick_heads(STATS, own_ref.shape[1]))


def combine_kernel(own_ref, level_ref, *rest):
    received, out_ref = rest[:-1], rest[-1]
    width = own_ref.shape[1]
    segs = received[0].shape[0]
    part = own_ref.shape[0] // segs
    pick = pick_heads(STAT_ROWS, width)
    for segment in range(segs):
        rows = slice(segment * part, (segment + 1) * part)
        parts, levels = [own_ref[rows, :]], [level_ref[rows, :]]
        for ref in received:
            parts.append(ref[segment, :part, :].astype(F32))
            stats = ref[segment, part:, :STATS]
            levels.append(
                lax.dot_general(
                    stats, pick, (((0,), (0,)), ((), ())), preferred_element_type=F32
                )[:part]
            )
        joint = functools.reduce(jnp.maximum, levels)
        factors = [jnp.exp(level - joint) for level in levels]
        mixed = sum(value * factor for value, factor in zip(parts, factors))
        out_ref[rows, :] = (mixed / sum(factors)).astype(BF16)


def hidden_kernel(
    lat_ref, own_ref, other_ref, wo_ref, wp_ref, wq_ref, hid_ref, norm_ref, query_ref
):
    segs, _, _ = lat_ref.shape
    part = own_ref.shape[0] // segs
    first = pl.multiple_of(lax.axis_index("read") * part, part)
    delta = mm(own_ref[...], wo_ref[...]) + mm(other_ref[...], wp_ref[...])
    for segment in range(segs):
        rows = slice(segment * part, (segment + 1) * part)
        hid_ref[rows, :] = lat_ref[segment, pl.ds(first, part), :].astype(F32) + delta[rows]
    normed = rms_rows(hid_ref[...]).astype(BF16)
    norm_ref[...] = normed
    query_ref[...] = (mm(normed, wq_ref[...]) * (HD ** (-0.5))).astype(BF16)


def project_blocks(blocks, slots, wk_ref, wv_ref, key_all, value_all):
    for block, slot in zip(blocks, slots):
        size = block.shape[0]
        place = pl.ds(pl.multiple_of(slot * size, size), size)
        key_all[place, :] = mm(block[...], wk_ref[...]).astype(BF16)
        value_all[place, :] = mm(block[...], wv_ref[...]).astype(BF16)


def collect(segment, segs, part, slot_of, offsets, pattern_ref, sources, targets):
    seg_total = pattern_ref.shape[1]
    home = lax.axis_index("pos") * segs + segment
    live = jnp.int32(0)
    for offset in offsets:
        block_step, inner = divmod(segment + offset, segs)
        if block_step not in slot_of:
            continue
        inside = (home + offset >= 0) & (home + offset < seg_total)
        flag = pattern_ref[segment, jnp.clip(home + offset, 0, seg_total - 1)]
        chosen = inside & (flag > 0)
        source = (slot_of[block_step] * segs + inner) * part

        place = pl.ds(pl.multiple_of(live * part, part), part)
        for whole, packed in zip(sources, targets):
            packed[place, :] = whole[source : source + part, :]
        live = live + chosen.astype(jnp.int32)
    return live


def near_kernel(readers, offsets, pattern_ref, wk_ref, wv_ref, *rest):
    queries = rest[:readers]
    own, ahead, behind = rest[readers : readers + 3]
    spread, max_out, total_out, acc = rest[readers + 3 : readers + 7]
    query_buf, key_all, value_all, key_buf, value_buf, score_buf = rest[readers + 7 :]
    segs, spread_rows, local = spread.shape
    lat_rows = query_buf.shape[1]
    part = lat_rows // readers
    heads = local // HD
    reader = lax.axis_index("read")
    core = lax.axis_index("head")

    key_buf[...] = jnp.zeros(key_buf.shape, BF16)
    value_buf[...] = jnp.zeros(value_buf.shape, BF16)
    project_blocks(
        (own, ahead, behind), (0, 1 + core, 2 - core), wk_ref, wv_ref, key_all, value_all
    )
    for step in range(readers):
        first = pl.multiple_of(lax.rem(reader + readers - step, readers) * part, part)
        for segment in range(segs):
            query_buf[segment, pl.ds(first, part), :] = queries[step][
                segment * part : (segment + 1) * part, :
            ]

    for segment in range(segs):
        spread_queries(query_buf[segment], heads, spread.at[segment])
        live = collect(
            segment, segs, part, {0: 0, -1: 1, 1: 2}, offsets, pattern_ref,
            (key_all, value_all), (key_buf, value_buf),
        )
        max_out[segment] = jnp.full(max_out.shape[1:], NEG, F32)
        total_out[segment] = jnp.zeros(total_out.shape[1:], F32)
        acc[segment] = jnp.zeros(acc.shape[1:], F32)

        def first_pass(chunk, carry, segment=segment, live=live):
            base = pl.multiple_of(chunk * CHUNK, CHUNK)
            place = base + lax.broadcasted_iota(jnp.int32, (1, CHUNK), 1)
            scores = nt_dot(spread[segment], key_buf[pl.ds(base, CHUNK), :])
            scores = jnp.where(place < live * part, scores, NEG)
            score_buf[chunk] = scores
            max_out[segment] = jnp.maximum(max_out[segment], tile_fold(scores, jnp.maximum))
            return carry

        chunks = (live * part + CHUNK - 1) // CHUNK
        lax.fori_loop(0, chunks, first_pass, 0)
        row_max = jnp.max(max_out[segment], axis=1, keepdims=True)
        max_out[segment] = jnp.broadcast_to(row_max, max_out.shape[1:])

        def second_pass(chunk, carry, segment=segment):
            value = value_buf[pl.ds(pl.multiple_of(chunk * CHUNK, CHUNK), CHUNK), :]
            for block in range(2):
                rows = slice(block * spread_rows // 2, (block + 1) * spread_rows // 2)
                weights = jnp.exp(
                    score_buf[chunk, rows] - jnp.tile(max_out[segment, rows], (1, CHUNK // 128))
                )
                total_out[segment, rows] += tile_fold(weights, jnp.add)
                acc[segment, rows] += mm(weights.astype(BF16), value)
            return carry

        lax.fori_loop(0, chunks, second_pass, 0)


def far_kernel(readers, steps, offsets, pattern_ref, wk_ref, wv_ref, *rest):
    spread, max_in, total_in, acc_in = rest[:4]
    blocks = rest[4 : 4 + 2 * len(steps)]
    rest = rest[4 + 2 * len(steps) :]
    own_ref, own_stat_ref = rest[:2]
    sends = rest[2 : 1 + readers]
    key_all, value_all, key_buf, value_buf, max_buf, total_buf, acc, full, stat_full = rest[
        1 + readers :
    ]
    segs, _, local = spread.shape
    heads = local // HD
    part = own_ref.shape[1]
    core = lax.axis_index("head")
    many = key_buf.shape[1]

    key_buf[...] = jnp.zeros(key_buf.shape, BF16)
    value_buf[...] = jnp.zeros(value_buf.shape, BF16)
    slots, slot_of = [], {}
    for index, step in enumerate(steps):
        slots += [2 * index + core, 2 * index + 1 - core]
        slot_of[-step], slot_of[step] = 2 * index, 2 * index + 1
    project_blocks(blocks, slots, wk_ref, wv_ref, key_all, value_all)
    counts = [
        collect(
            segment, segs, part, slot_of, offsets, pattern_ref,
            (key_all, value_all), (key_buf.at[segment], value_buf.at[segment]),
        )
        for segment in range(segs)
    ]

    for segment in range(segs):
        place = lax.broadcasted_iota(jnp.int32, (1, many), 1)
        scores = nt_dot(spread[segment], key_buf[segment])
        scores = jnp.where(place < counts[segment] * part, scores, NEG)
        before = max_in[segment]
        top = jnp.max(tile_fold(scores, jnp.maximum), axis=1, keepdims=True)
        peak = jnp.maximum(before, jnp.broadcast_to(top, before.shape))
        max_buf[segment] = peak
        factor = jnp.exp(before - peak)
        weights = jnp.exp(scores - jnp.tile(peak, (1, many // 128)))
        row_total = jnp.sum(
            total_in[segment] * factor + tile_fold(weights, jnp.add), axis=1, keepdims=True
        )
        total_buf[segment] = jnp.broadcast_to(row_total, before.shape)
        acc[segment] = acc_in[segment] * jnp.tile(factor, (1, local // 128)) + mm(
            weights.astype(BF16), value_buf[segment]
        )
    for segment in range(segs):
        emit(
            segment, max_buf[segment], total_buf[segment], acc.at[segment], heads,
            full.at[segment], stat_full.at[segment], own_ref, own_stat_ref, sends,
        )


def out_kernel(hid_ref, own_ref, other_ref, wo_ref, wp_ref, out_ref):
    segs, part, share = out_ref.shape
    cols = pl.ds(pl.multiple_of(lax.axis_index("head") * share, 128), share)
    result = (
        hid_ref[:, cols] + mm(own_ref[...], wo_ref[:, cols]) + mm(other_ref[...], wp_ref[:, cols])
    )
    for segment in range(segs):
        out_ref[segment] = result[segment * part : (segment + 1) * part].astype(BF16)


def cost(flops, moved, exps=0):
    return pl.CostEstimate(flops=int(flops), bytes_accessed=int(moved), transcendentals=int(exps))


def vmem():
    return pl.BlockSpec(memory_space=pltpu.VMEM)


def smem():
    return pl.BlockSpec(memory_space=pltpu.SMEM)


def call(kernel, inputs, outputs, specs=None, scratch=(), estimate=None, limit=8 << 20):
    return pl.pallas_call(
        kernel,
        out_shape=[jax.ShapeDtypeStruct(shape, kind) for shape, kind in outputs],
        in_specs=specs or [vmem() for _ in inputs],
        out_specs=[vmem() for _ in outputs],
        scratch_shapes=list(scratch),
        cost_estimate=estimate,
        compiler_params=pltpu.CompilerParams(vmem_limit_bytes=limit),
    )(*inputs)


def swap_cores(value):
    return lax.ppermute(value, "head", [(0, 1), (1, 0)])


def to_reader(value, step):
    readers = lax.axis_size("read")
    return lax.ppermute(value, "read", [(i, (i + step) % readers) for i in range(readers)])


def both_ways(value, step):
    count = lax.axis_size("pos")
    ring = [2 * place for place in range(count)]
    ring += [2 * place + 1 for place in reversed(range(count))]
    moves = [(ring[i], ring[(i + step) % len(ring)]) for i in range(len(ring))]
    return lax.ppermute(value, ("pos", "head"), moves)


def layer(
    latents, read_tokens, band_start, coverage, present, pattern, cross_query, cross_key,
    cross_value, cross_out, self_query, self_key, self_value, self_out,
):
    segs, lat_rows, width = latents.shape
    reads, length = read_tokens.shape[1:3]
    local = cross_query.shape[1]
    heads = local // HD
    readers = lax.axis_size("read")
    part = lat_rows // readers
    size = segs * part
    seg_total = pattern.shape[1]
    share = width // lax.axis_size("head")
    spread_rows = heads * lat_rows

    offsets = [0]
    distance = 1
    while distance < seg_total:
        offsets += [distance, -distance]
        distance *= 2
    steps = sorted(
        {abs((seg + off) // segs) for off in offsets for seg in range(segs)} - {0}
    )

    cross_out_other = swap_cores(cross_out)
    self_out_other = swap_cores(self_out)

    part_outputs = [((segs, part, local), F32), ((segs, part, STATS), BF16)] + [
        ((segs, part + STAT_ROWS, local), BF16)
    ] * (readers - 1)
    work = [pltpu.VMEM((lat_rows, local), F32), pltpu.VMEM((lat_rows, STATS), F32)]
    most = reads * length
    tiles = -(-most // CHUNK)
    spare = (segs * tiles + 1) // 2 * 2 + 2
    produced = call(
        functools.partial(cross_kernel, readers),
        (band_start, coverage, present, latents, read_tokens, cross_query, cross_key, cross_value),
        part_outputs,
        specs=[pl.BlockSpec(memory_space=pltpu.HBM)] * 8,
        scratch=[
            pltpu.SMEM(band_start.shape, jnp.int32),
            pltpu.SMEM(coverage.shape, jnp.int32),
            pltpu.SMEM(present.shape, jnp.int32),
            pltpu.SMEM((segs * tiles + 3,), jnp.int32),
            pltpu.SMEM((segs + 1, reads + 1), jnp.int32),
            pltpu.SMEM((segs + 1, reads), jnp.int32),
            pltpu.VMEM(latents.shape, BF16),
            pltpu.VMEM(cross_query.shape, BF16),
            pltpu.VMEM(cross_key.shape, BF16),
            pltpu.VMEM(cross_value.shape, BF16),
            pltpu.VMEM((spare * CHUNK, width), BF16),
            pltpu.VMEM((segs + 1, spread_rows, local), BF16),
            pltpu.VMEM((2, 2 * CHUNK, local), BF16),
            pltpu.VMEM((segs * tiles + 1, spread_rows, CHUNK), F32),
            pltpu.VMEM((spare * CHUNK, local), BF16),
            pltpu.VMEM((segs + 1, spread_rows, 128), F32),
            pltpu.VMEM((segs + 1, spread_rows, 128), F32),
            pltpu.VMEM((segs + 1, spread_rows, local), F32),
        ]
        + work
        + [pltpu.SemaphoreType.DMA((7,)), pltpu.SemaphoreType.DMA((segs,))],
        estimate=cost(
            2 * segs * most * local * (2 * width + 2 * spread_rows),
            2 * segs * most * width,
            segs * most * spread_rows,
        ),
        limit=60 * 1024 * 1024,
    )

    def combine(parts):
        own, own_stat, sends = parts[0], parts[1], parts[2:]
        received = [to_reader(value, step + 1) for step, value in enumerate(sends)]
        kept, level = call(
            own_kernel,
            (own.reshape(size, local), own_stat.reshape(size, STATS)),
            [((size, local), F32), ((size, local), F32)],
            estimate=cost(2 * size * STATS * local, 12 * size * local),
        )
        return call(
            combine_kernel,
            [kept, level] + received,
            [((size, local), BF16)],
            estimate=cost(8 * size * STATS * local, 8 * size * local),
        )[0]

    attended = combine(produced)
    attended_other = swap_cores(attended)
    hidden, normed, query = call(
        hidden_kernel,
        (latents, attended, attended_other, cross_out, cross_out_other, self_query),
        [((size, width), F32), ((size, width), BF16), ((size, local), BF16)],
        estimate=cost(2 * size * width * (width + local), 8 * size * width),
    )
    queries = [query] + [to_reader(query, step) for step in range(1, readers)]
    direct, pair = {}, {}
    for step in steps:
        half = step // 2
        if half in direct and 2 * half == step:
            direct[step] = both_ways(direct[half], half)
        else:
            direct[step] = both_ways(normed, step)
        pair[step] = (direct[step], swap_cores(direct[step]))
    state = [
        ((segs, spread_rows, local), BF16),
        ((segs, spread_rows, 128), F32),
        ((segs, spread_rows, 128), F32),
        ((segs, spread_rows, local), F32),
    ]

    def reach(test):
        return max(
            sum(test(abs((segment + offset) // segs)) for offset in offsets)
            for segment in range(segs)
        )

    near_keys = -(-reach(lambda step: step <= 1) * part // CHUNK) * CHUNK
    far_keys = -(-reach(lambda step: step > 1) * part // 128) * 128
    carried = call(
        functools.partial(near_kernel, readers, tuple(offsets)),
        (pattern, self_key, self_value, *queries, normed, *pair[1]),
        state,
        specs=[smem()] + [vmem()] * (5 + len(queries)),
        scratch=[
            pltpu.VMEM((segs, lat_rows, local), BF16),
            pltpu.VMEM((3 * size, local), BF16),
            pltpu.VMEM((3 * size, local), BF16),
            pltpu.VMEM((near_keys, local), BF16),
            pltpu.VMEM((near_keys, local), BF16),
            pltpu.VMEM((near_keys // CHUNK, spread_rows, CHUNK), F32),
        ],
        estimate=cost(4 * segs * near_keys * local * spread_rows, 8 * segs * spread_rows * local),
        limit=16 << 20,
    )
    far = [step for step in steps if step > 1]
    far_blocks = [block for step in far for block in pair[step]]
    produced = call(
        functools.partial(far_kernel, readers, tuple(far), tuple(offsets)),
        (pattern, self_key, self_value, *carried, *far_blocks),
        part_outputs,
        specs=[smem()] + [vmem()] * (6 + len(far_blocks)),
        scratch=[
            pltpu.VMEM((len(far_blocks) * size, local), BF16),
            pltpu.VMEM((len(far_blocks) * size, local), BF16),
            pltpu.VMEM((segs, far_keys, local), BF16),
            pltpu.VMEM((segs, far_keys, local), BF16),
            pltpu.VMEM((segs, spread_rows, 128), F32),
            pltpu.VMEM((segs, spread_rows, 128), F32),
            pltpu.VMEM((segs, spread_rows, local), F32),
            pltpu.VMEM((segs, lat_rows, local), F32),
            pltpu.VMEM((segs, lat_rows, STATS), F32),
        ],
        estimate=cost(
            4 * segs * far_keys * local * spread_rows, 8 * segs * spread_rows * local
        ),
        limit=16 << 20,
    )
    mixed = combine(produced)
    mixed_other = swap_cores(mixed)
    return call(
        out_kernel,
        (hidden, mixed, mixed_other, self_out, self_out_other),
        [((segs, part, share), BF16)],
        estimate=cost(2 * size * width * share, 8 * size * width),
    )[0]


def solution(mesh):
    placed = (
        P(("grp", "pos"), None, None),
        P(("grp", "pos"), "read", None, None),
        P(("grp", "pos"), "read"),
        P(("grp", "pos"), "read"),
        P(("grp", "pos"), "read"),
        P(("grp", "pos"), None),
        P(None, "head"),
        P(None, "head"),
        P(None, "head"),
        P("head", None),
        P(None, "head"),
        P(None, "head"),
        P(None, "head"),
        P("head", None),
    )
    return jax.shard_map(
        layer,
        mesh=mesh,
        in_specs=placed,
        out_specs=P(("grp", "pos"), "read", "head"),
        check_vma=False,
    )
```

```python
import functools

import jax
import jax.numpy as jnp
from jax import lax
from jax.experimental import pallas as pl
from jax.experimental.pallas import tpu as pltpu
from jax.sharding import PartitionSpec as P


HD = 64
EPSILON = 1e-06
NEG = -1e30
CHUNK = 256
STATS = 128
STAT_ROWS = 16
ROWS = 16
F32 = jnp.float32
BF16 = jnp.bfloat16


def nt_dot(left, right):
    return lax.dot_general(left, right, (((1,), (1,)), ((), ())), preferred_element_type=F32)


def mm(left, right):
    return jnp.dot(left, right, preferred_element_type=F32)


def rms_rows(values):
    return values * lax.rsqrt(jnp.mean(values * values, axis=-1, keepdims=True) + EPSILON)


def spread_queries(query, heads, target):
    rows, width = query.shape
    lane = lax.broadcasted_iota(jnp.int32, (rows, 128), 1)
    for head in range(heads):
        inside = (lane >= HD) if head % 2 else (lane < HD)
        for tile in range(width // 128):
            cols = slice(tile * 128, (tile + 1) * 128)
            kept = jnp.zeros((rows, 128), BF16)
            if tile == head // 2:
                kept = jnp.where(inside, query[:, cols].astype(F32), 0.0).astype(BF16)
            target[head * rows : (head + 1) * rows, cols] = kept


def tile_fold(values, combine):
    folded = values[:, :128]
    for tile in range(1, values.shape[1] // 128):
        folded = combine(folded, values[:, tile * 128 : (tile + 1) * 128])
    return folded


def emit(segment, row_max, row_total, acc, heads, full, stat_full, own_ref, own_stat_ref, sends):
    readers = len(sends) + 1
    rows, width = full.shape
    part = rows // readers
    lane = lax.broadcasted_iota(jnp.int32, (rows, 128), 1)
    lane_head = lax.rem(lane, heads)

    def compact(values):
        packed = values[:rows]
        for head in range(1, heads):
            packed = jnp.where(lane_head == head, values[head * rows : (head + 1) * rows], packed)
        return packed

    divisor = jnp.where(row_total > 0, row_total, 1.0)
    packed_total = compact(row_total)
    level = jnp.where(
        packed_total > 0, compact(row_max) + jnp.log(jnp.where(packed_total > 0, packed_total, 1.0)),
        NEG,
    )
    for tile in range(width // 128):
        low = slice(2 * tile * rows, (2 * tile + 1) * rows)
        high = slice((2 * tile + 1) * rows, (2 * tile + 2) * rows)
        cols = slice(tile * 128, (tile + 1) * 128)
        full[:, cols] = jnp.where(lane < HD, acc[low, cols], acc[high, cols]) / jnp.where(
            lane < HD, divisor[low], divisor[high]
        )
    stats = jnp.zeros((rows, STATS), F32)
    for step in range(3):
        piece = level.astype(BF16).astype(F32)
        stats = jnp.where(lane // heads == step, piece, stats)
        level = level - piece
    stat_full[...] = stats
    flipped = stats.T[:STAT_ROWS]
    reader = lax.axis_index("read")
    for step in range(readers):
        first = pl.multiple_of(lax.rem(reader + step, readers) * part, part)
        if step == 0:
            own_ref[segment] = full[pl.ds(first, part), :]
            own_stat_ref[segment] = stat_full[pl.ds(first, part), :].astype(BF16)
        else:
            sends[step - 1][segment, :part, :] = full[pl.ds(first, part), :].astype(BF16)
            turned = pltpu.roll(flipped, lax.rem(rows - first, rows), 1)
            sends[step - 1][segment, part:, :] = jnp.concatenate(
                [turned, jnp.zeros((STAT_ROWS, width - rows), F32)], axis=1
            ).astype(BF16)


def cross_kernel(
    readers, start_hbm, cov_hbm, present_hbm, lat_hbm, tok_ref, wq_hbm, wk_hbm, wv_hbm, *rest
):
    own_ref, own_stat_ref = rest[:2]
    sends = rest[2 : 1 + readers]
    (start_ref, cov_ref, present_ref, seg_of, low_of, high_of, lat_ref, wq_ref, wk_ref, wv_ref,
     token_buf, spread, key_buf, score_buf, value_buf, max_buf, total_buf, acc, full, stat_full,
     load_sems, sems) = rest[1 + readers :]
    loads = [
        pltpu.make_async_copy(source, target, load_sems.at[index])
        for index, (source, target) in enumerate(
            (
                (start_hbm, start_ref),
                (cov_hbm, cov_ref),
                (present_hbm, present_ref),
                (lat_hbm, lat_ref),
                (wq_hbm, wq_ref),
                (wk_hbm, wk_ref),
                (wv_hbm, wv_ref),
            )
        )
    ]
    for load in loads:
        load.start()
    for load in loads[:3]:
        load.wait()
    segs, lat_rows, width = lat_ref.shape
    reads = tok_ref.shape[1]
    local = wq_ref.shape[1]
    heads = local // HD

    used = jnp.int32(0)
    for segment in range(segs):
        offset = used * CHUNK
        for read in range(reads):
            start = start_ref[segment, read]
            length = cov_ref[segment, read]
            live = present_ref[segment, read] > 0
            first = start & -ROWS
            last = (start + length + ROWS - 1) & -ROWS
            rows = pl.multiple_of(jnp.where(live, last - first, 0), ROWS)
            low_of[segment, read] = offset + start - first
            high_of[segment, read] = offset + jnp.where(live, start - first + length, 0)

            @pl.when(live)
            def _(segment=segment, read=read, offset=offset, first=first, rows=rows):
                pltpu.make_async_copy(
                    tok_ref.at[segment, read, pl.ds(pl.multiple_of(first, ROWS), rows), :],
                    token_buf.at[pl.ds(pl.multiple_of(offset, ROWS), rows), :],
                    sems.at[segment],
                ).start()

            offset = offset + rows
        low_of[segment, reads] = offset - used * CHUNK
        chunks = (offset - used * CHUNK + CHUNK - 1) // CHUNK

        def clear(step, carry, offset=offset):
            token_buf[pl.ds(pl.multiple_of(offset + step * ROWS, ROWS), ROWS), :] = jnp.zeros(
                (ROWS, width), BF16
            )
            return carry

        lax.fori_loop(0, ((used + chunks) * CHUNK - offset) // ROWS, clear, 0)

        def note(step, carry, segment=segment, used=used):
            seg_of[used + step] = segment
            return carry

        lax.fori_loop(0, chunks, note, 0)
        used = used + chunks
    for step in range(3):
        seg_of[used + step] = segs
    for read in range(reads):
        low_of[segs, read] = 0
        high_of[segs, read] = 0

    max_buf[:segs] = jnp.full((segs,) + max_buf.shape[1:], NEG, F32)
    total_buf[:segs] = jnp.zeros((segs,) + total_buf.shape[1:], F32)
    acc[:segs] = jnp.zeros((segs,) + acc.shape[1:], F32)
    for load in loads[3:]:
        load.wait()
    normed = rms_rows(lat_ref[...].reshape(segs * lat_rows, width).astype(F32)).astype(BF16)
    query = (mm(normed, wq_ref[...]) * (HD ** (-0.5))).astype(BF16)
    for segment in range(segs):
        spread_queries(
            query[segment * lat_rows : (segment + 1) * lat_rows], heads, spread.at[segment]
        )

    def landed(segment):
        size = pl.multiple_of(low_of[segment, reads], ROWS)
        whole = token_buf.at[pl.ds(0, size), :]
        pltpu.make_async_copy(whole, whole, sems.at[segment]).wait()

    def projected(pair):
        place = pl.ds(pl.multiple_of(pair * 2 * CHUNK, 2 * CHUNK), 2 * CHUNK)
        tokens = token_buf[place, :]
        key_buf[lax.rem(pair, 2)] = mm(tokens, wk_ref[...]).astype(BF16)
        value_buf[place, :] = mm(tokens, wv_ref[...]).astype(BF16)

    def arrive(chunk, before):
        upcoming = seg_of[chunk]

        @pl.when((upcoming != before) & (upcoming < segs))
        def _():
            landed(upcoming)

    pairs = (used + 1) // 2

    @pl.when(used > 0)
    def _():
        arrive(0, -1)
        arrive(1, seg_of[0])
        projected(jnp.int32(0))

    def first_pass(pair, carry):
        chunk = 2 * pair
        arrive(chunk + 2, seg_of[chunk + 1])
        arrive(chunk + 3, seg_of[chunk + 2])
        keys = key_buf[lax.rem(pair, 2)]
        segments = [seg_of[chunk], seg_of[chunk + 1]]
        for half in range(2):
            segment = segments[half]
            place = (chunk + half) * CHUNK + lax.broadcasted_iota(jnp.int32, (1, CHUNK), 1)
            live = jnp.zeros((1, CHUNK), jnp.bool_)
            for read in range(reads):
                live = live | (
                    (place >= low_of[segment, read]) & (place < high_of[segment, read])
                )
            for block in range(2):
                size = acc.shape[1] // 2
                rows = slice(block * size, (block + 1) * size)
                scores = nt_dot(
                    spread[segment, rows], keys[half * CHUNK : (half + 1) * CHUNK]
                )
                scores = jnp.where(live, scores, NEG)
                score_buf[chunk + half, rows] = scores
                max_buf[segment, rows] = jnp.maximum(
                    max_buf[segment, rows], tile_fold(scores, jnp.maximum)
                )
        projected(pair + 1)
        return carry

    lax.fori_loop(0, pairs, first_pass, 0)
    for segment in range(segs):
        row_max = jnp.max(max_buf[segment], axis=1, keepdims=True)
        max_buf[segment] = jnp.broadcast_to(row_max, max_buf.shape[1:])

    def second_pass(pair, carry):
        for half in range(2):
            chunk = 2 * pair + half
            segment = seg_of[chunk]
            value = value_buf[pl.ds(pl.multiple_of(chunk * CHUNK, CHUNK), CHUNK), :]
            for block in range(2):
                rows = slice(block * acc.shape[1] // 2, (block + 1) * acc.shape[1] // 2)
                weights = jnp.exp(
                    score_buf[chunk, rows] - jnp.tile(max_buf[segment, rows], (1, CHUNK // 128))
                )
                total_buf[segment, rows] += tile_fold(weights, jnp.add)
                acc[segment, rows] += mm(weights.astype(BF16), value)
        return carry

    lax.fori_loop(0, pairs, second_pass, 0)

    for segment in range(segs):
        row_total = jnp.sum(total_buf[segment], axis=1, keepdims=True)
        emit(
            segment, max_buf[segment], jnp.broadcast_to(row_total, total_buf.shape[1:]),
            acc.at[segment], heads, full.at[segment], stat_full.at[segment], own_ref,
            own_stat_ref, sends,
        )


def pick_heads(rows, width):
    heads = width // HD
    place = lax.broadcasted_iota(jnp.int32, (rows, width), 0)
    head = lax.broadcasted_iota(jnp.int32, (rows, width), 1) // HD
    return ((lax.rem(place, heads) == head) & (place < 3 * heads)).astype(F32).astype(BF16)


def own_kernel(own_ref, stat_ref, kept_ref, level_ref):
    kept_ref[...] = own_ref[...]
    level_ref[...] = mm(stat_ref[...], pick_heads(STATS, own_ref.shape[1]))


def combine_kernel(own_ref, level_ref, *rest):
    received, out_ref = rest[:-1], rest[-1]
    width = own_ref.shape[1]
    segs = received[0].shape[0]
    part = own_ref.shape[0] // segs
    pick = pick_heads(STAT_ROWS, width)
    for segment in range(segs):
        rows = slice(segment * part, (segment + 1) * part)
        parts, levels = [own_ref[rows, :]], [level_ref[rows, :]]
        for ref in received:
            parts.append(ref[segment, :part, :].astype(F32))
            stats = ref[segment, part:, :STATS]
            levels.append(
                lax.dot_general(
                    stats, pick, (((0,), (0,)), ((), ())), preferred_element_type=F32
                )[:part]
            )
        joint = functools.reduce(jnp.maximum, levels)
        factors = [jnp.exp(level - joint) for level in levels]
        mixed = sum(value * factor for value, factor in zip(parts, factors))
        out_ref[rows, :] = (mixed / sum(factors)).astype(BF16)


def hidden_kernel(
    lat_ref, own_ref, other_ref, wo_ref, wp_ref, wq_ref, hid_ref, norm_ref, query_ref
):
    segs, _, _ = lat_ref.shape
    part = own_ref.shape[0] // segs
    first = pl.multiple_of(lax.axis_index("read") * part, part)
    delta = mm(own_ref[...], wo_ref[...]) + mm(other_ref[...], wp_ref[...])
    for segment in range(segs):
        rows = slice(segment * part, (segment + 1) * part)
        hid_ref[rows, :] = lat_ref[segment, pl.ds(first, part), :].astype(F32) + delta[rows]
    normed = rms_rows(hid_ref[...]).astype(BF16)
    norm_ref[...] = normed
    query_ref[...] = (mm(normed, wq_ref[...]) * (HD ** (-0.5))).astype(BF16)


def project_blocks(blocks, slots, wk_ref, wv_ref, key_all, value_all):
    for block, slot in zip(blocks, slots):
        size = block.shape[0]
        place = pl.ds(pl.multiple_of(slot * size, size), size)
        key_all[place, :] = mm(block[...], wk_ref[...]).astype(BF16)
        value_all[place, :] = mm(block[...], wv_ref[...]).astype(BF16)


def collect(segment, segs, part, slot_of, offsets, pattern_ref, sources, targets):
    seg_total = pattern_ref.shape[1]
    home = lax.axis_index("pos") * segs + segment
    live = jnp.int32(0)
    for offset in offsets:
        block_step, inner = divmod(segment + offset, segs)
        if block_step not in slot_of:
            continue
        inside = (home + offset >= 0) & (home + offset < seg_total)
        flag = pattern_ref[segment, jnp.clip(home + offset, 0, seg_total - 1)]
        chosen = inside & (flag > 0)
        source = (slot_of[block_step] * segs + inner) * part

        place = pl.ds(pl.multiple_of(live * part, part), part)
        for whole, packed in zip(sources, targets):
            packed[place, :] = whole[source : source + part, :]
        live = live + chosen.astype(jnp.int32)
    return live


def near_kernel(readers, offsets, pattern_ref, wk_ref, wv_ref, *rest):
    queries = rest[:readers]
    own, ahead, behind = rest[readers : readers + 3]
    spread, max_out, total_out, acc = rest[readers + 3 : readers + 7]
    query_buf, key_all, value_all, key_buf, value_buf = rest[readers + 7 :]
    segs, _, local = spread.shape
    lat_rows = query_buf.shape[1]
    part = lat_rows // readers
    heads = local // HD
    reader = lax.axis_index("read")
    core = lax.axis_index("head")

    key_buf[...] = jnp.zeros(key_buf.shape, BF16)
    value_buf[...] = jnp.zeros(value_buf.shape, BF16)
    project_blocks(
        (own, ahead, behind), (0, 1 + core, 2 - core), wk_ref, wv_ref, key_all, value_all
    )
    for step in range(readers):
        first = pl.multiple_of(lax.rem(reader + readers - step, readers) * part, part)
        for segment in range(segs):
            query_buf[segment, pl.ds(first, part), :] = queries[step][
                segment * part : (segment + 1) * part, :
            ]

    for segment in range(segs):
        spread_queries(query_buf[segment], heads, spread.at[segment])
    counts = [
        collect(
            segment, segs, part, {0: 0, -1: 1, 1: 2}, offsets, pattern_ref,
            (key_all, value_all), (key_buf.at[segment], value_buf.at[segment]),
        )
        for segment in range(segs)
    ]

    def weigh(segment, base, before):
        keys = slice(base, base + CHUNK)
        place = base + lax.broadcasted_iota(jnp.int32, (1, CHUNK), 1)
        scores = nt_dot(spread[segment], key_buf[segment, keys])
        scores = jnp.where(place < counts[segment] * part, scores, NEG)
        top = jnp.max(tile_fold(scores, jnp.maximum), axis=1, keepdims=True)
        peak = jnp.broadcast_to(top, max_out.shape[1:])
        if before is not None:
            peak = jnp.maximum(peak, before)
        weights = jnp.exp(scores - jnp.tile(peak, (1, CHUNK // 128)))
        update = mm(weights.astype(BF16), value_buf[segment, keys])
        return peak, tile_fold(weights, jnp.add), update

    for segment in range(segs):
        max_out[segment], total_out[segment], acc[segment] = weigh(segment, 0, None)
    for segment in range(segs):
        for base in range(CHUNK, key_buf.shape[1], CHUNK):

            @pl.when(counts[segment] * part > base)
            def _(segment=segment, base=base):
                before = max_out[segment]
                peak, totals, update = weigh(segment, base, before)
                factor = jnp.exp(before - peak)
                max_out[segment] = peak
                total_out[segment] = total_out[segment] * factor + totals
                acc[segment] = acc[segment] * jnp.tile(factor, (1, local // 128)) + update


def far_kernel(readers, steps, offsets, pattern_ref, wk_ref, wv_ref, *rest):
    spread, max_in, total_in, acc_in = rest[:4]
    blocks = rest[4 : 4 + 2 * len(steps)]
    rest = rest[4 + 2 * len(steps) :]
    own_ref, own_stat_ref = rest[:2]
    sends = rest[2 : 1 + readers]
    key_all, value_all, key_buf, value_buf, max_buf, total_buf, acc, full, stat_full = rest[
        1 + readers :
    ]
    segs, _, local = spread.shape
    heads = local // HD
    part = own_ref.shape[1]
    core = lax.axis_index("head")
    many = key_buf.shape[1]

    key_buf[...] = jnp.zeros(key_buf.shape, BF16)
    value_buf[...] = jnp.zeros(value_buf.shape, BF16)
    slots, slot_of = [], {}
    for index, step in enumerate(steps):
        slots += [2 * index + core, 2 * index + 1 - core]
        slot_of[-step], slot_of[step] = 2 * index, 2 * index + 1
    project_blocks(blocks, slots, wk_ref, wv_ref, key_all, value_all)
    counts = [
        collect(
            segment, segs, part, slot_of, offsets, pattern_ref,
            (key_all, value_all), (key_buf.at[segment], value_buf.at[segment]),
        )
        for segment in range(segs)
    ]

    for segment in range(segs):
        place = lax.broadcasted_iota(jnp.int32, (1, many), 1)
        scores = nt_dot(spread[segment], key_buf[segment])
        scores = jnp.where(place < counts[segment] * part, scores, NEG)
        before = max_in[segment]
        top = jnp.max(tile_fold(scores, jnp.maximum), axis=1, keepdims=True)
        peak = jnp.maximum(before, jnp.broadcast_to(top, before.shape))
        max_buf[segment] = peak
        factor = jnp.exp(before - peak)
        weights = jnp.exp(scores - jnp.tile(peak, (1, many // 128)))
        row_total = jnp.sum(
            total_in[segment] * factor + tile_fold(weights, jnp.add), axis=1, keepdims=True
        )
        total_buf[segment] = jnp.broadcast_to(row_total, before.shape)
        acc[segment] = acc_in[segment] * jnp.tile(factor, (1, local // 128)) + mm(
            weights.astype(BF16), value_buf[segment]
        )
    for segment in range(segs):
        emit(
            segment, max_buf[segment], total_buf[segment], acc.at[segment], heads,
            full.at[segment], stat_full.at[segment], own_ref, own_stat_ref, sends,
        )


def out_kernel(hid_ref, own_ref, other_ref, wo_ref, wp_ref, out_ref):
    segs, part, share = out_ref.shape
    cols = pl.ds(pl.multiple_of(lax.axis_index("head") * share, 128), share)
    result = (
        hid_ref[:, cols] + mm(own_ref[...], wo_ref[:, cols]) + mm(other_ref[...], wp_ref[:, cols])
    )
    for segment in range(segs):
        out_ref[segment] = result[segment * part : (segment + 1) * part].astype(BF16)


def cost(flops, moved, exps=0):
    return pl.CostEstimate(flops=int(flops), bytes_accessed=int(moved), transcendentals=int(exps))


def vmem():
    return pl.BlockSpec(memory_space=pltpu.VMEM)


def smem():
    return pl.BlockSpec(memory_space=pltpu.SMEM)


def call(kernel, inputs, outputs, specs=None, scratch=(), estimate=None, limit=8 << 20):
    return pl.pallas_call(
        kernel,
        out_shape=[jax.ShapeDtypeStruct(shape, kind) for shape, kind in outputs],
        in_specs=specs or [vmem() for _ in inputs],
        out_specs=[vmem() for _ in outputs],
        scratch_shapes=list(scratch),
        cost_estimate=estimate,
        compiler_params=pltpu.CompilerParams(vmem_limit_bytes=limit),
    )(*inputs)


def swap_cores(value):
    return lax.ppermute(value, "head", [(0, 1), (1, 0)])


def to_reader(value, step):
    readers = lax.axis_size("read")
    return lax.ppermute(value, "read", [(i, (i + step) % readers) for i in range(readers)])


def both_ways(value, step):
    count = lax.axis_size("pos")
    ring = [2 * place for place in range(count)]
    ring += [2 * place + 1 for place in reversed(range(count))]
    moves = [(ring[i], ring[(i + step) % len(ring)]) for i in range(len(ring))]
    return lax.ppermute(value, ("pos", "head"), moves)


def layer(
    latents, read_tokens, band_start, coverage, present, pattern, cross_query, cross_key,
    cross_value, cross_out, self_query, self_key, self_value, self_out,
):
    segs, lat_rows, width = latents.shape
    reads, length = read_tokens.shape[1:3]
    local = cross_query.shape[1]
    heads = local // HD
    readers = lax.axis_size("read")
    part = lat_rows // readers
    size = segs * part
    seg_total = pattern.shape[1]
    share = width // lax.axis_size("head")
    spread_rows = heads * lat_rows

    offsets = [0]
    distance = 1
    while distance < seg_total:
        offsets += [distance, -distance]
        distance *= 2
    steps = sorted(
        {abs((seg + off) // segs) for off in offsets for seg in range(segs)} - {0}
    )

    cross_out_other = swap_cores(cross_out)
    self_out_other = swap_cores(self_out)

    part_outputs = [((segs, part, local), F32), ((segs, part, STATS), BF16)] + [
        ((segs, part + STAT_ROWS, local), BF16)
    ] * (readers - 1)
    work = [pltpu.VMEM((segs, lat_rows, local), F32), pltpu.VMEM((segs, lat_rows, STATS), F32)]
    most = reads * length
    tiles = -(-most // CHUNK)
    spare = (segs * tiles + 1) // 2 * 2 + 2
    produced = call(
        functools.partial(cross_kernel, readers),
        (band_start, coverage, present, latents, read_tokens, cross_query, cross_key, cross_value),
        part_outputs,
        specs=[pl.BlockSpec(memory_space=pltpu.HBM)] * 8,
        scratch=[
            pltpu.SMEM(band_start.shape, jnp.int32),
            pltpu.SMEM(coverage.shape, jnp.int32),
            pltpu.SMEM(present.shape, jnp.int32),
            pltpu.SMEM((segs * tiles + 3,), jnp.int32),
            pltpu.SMEM((segs + 1, reads + 1), jnp.int32),
            pltpu.SMEM((segs + 1, reads), jnp.int32),
            pltpu.VMEM(latents.shape, BF16),
            pltpu.VMEM(cross_query.shape, BF16),
            pltpu.VMEM(cross_key.shape, BF16),
            pltpu.VMEM(cross_value.shape, BF16),
            pltpu.VMEM((spare * CHUNK, width), BF16),
            pltpu.VMEM((segs + 1, spread_rows, local), BF16),
            pltpu.VMEM((2, 2 * CHUNK, local), BF16),
            pltpu.VMEM((segs * tiles + 1, spread_rows, CHUNK), F32),
            pltpu.VMEM((spare * CHUNK, local), BF16),
            pltpu.VMEM((segs + 1, spread_rows, 128), F32),
            pltpu.VMEM((segs + 1, spread_rows, 128), F32),
            pltpu.VMEM((segs + 1, spread_rows, local), F32),
        ]
        + work
        + [pltpu.SemaphoreType.DMA((7,)), pltpu.SemaphoreType.DMA((segs,))],
        estimate=cost(
            2 * segs * most * local * (2 * width + 2 * spread_rows),
            2 * segs * most * width,
            segs * most * spread_rows,
        ),
        limit=60 * 1024 * 1024,
    )

    def combine(parts):
        own, own_stat, sends = parts[0], parts[1], parts[2:]
        received = [to_reader(value, step + 1) for step, value in enumerate(sends)]
        kept, level = call(
            own_kernel,
            (own.reshape(size, local), own_stat.reshape(size, STATS)),
            [((size, local), F32), ((size, local), F32)],
            estimate=cost(2 * size * STATS * local, 12 * size * local),
        )
        return call(
            combine_kernel,
            [kept, level] + received,
            [((size, local), BF16)],
            estimate=cost(8 * size * STATS * local, 8 * size * local),
        )[0]

    attended = combine(produced)
    attended_other = swap_cores(attended)
    hidden, normed, query = call(
        hidden_kernel,
        (latents, attended, attended_other, cross_out, cross_out_other, self_query),
        [((size, width), F32), ((size, width), BF16), ((size, local), BF16)],
        estimate=cost(2 * size * width * (width + local), 8 * size * width),
    )
    queries = [query] + [to_reader(query, step) for step in range(1, readers)]
    direct, pair = {}, {}
    for step in steps:
        half = step // 2
        if half in direct and 2 * half == step:
            direct[step] = both_ways(direct[half], half)
        else:
            direct[step] = both_ways(normed, step)
        pair[step] = (direct[step], swap_cores(direct[step]))
    state = [
        ((segs, spread_rows, local), BF16),
        ((segs, spread_rows, 128), F32),
        ((segs, spread_rows, 128), F32),
        ((segs, spread_rows, local), F32),
    ]

    def reach(test):
        return max(
            sum(test(abs((segment + offset) // segs)) for offset in offsets)
            for segment in range(segs)
        )

    near_keys = -(-reach(lambda step: step <= 1) * part // CHUNK) * CHUNK
    far_keys = -(-reach(lambda step: step > 1) * part // 128) * 128
    carried = call(
        functools.partial(near_kernel, readers, tuple(offsets)),
        (pattern, self_key, self_value, *queries, normed, *pair[1]),
        state,
        specs=[smem()] + [vmem()] * (5 + len(queries)),
        scratch=[
            pltpu.VMEM((segs, lat_rows, local), BF16),
            pltpu.VMEM((3 * size, local), BF16),
            pltpu.VMEM((3 * size, local), BF16),
            pltpu.VMEM((segs, near_keys, local), BF16),
            pltpu.VMEM((segs, near_keys, local), BF16),
        ],
        estimate=cost(4 * segs * near_keys * local * spread_rows, 8 * segs * spread_rows * local),
        limit=16 << 20,
    )
    far = [step for step in steps if step > 1]
    far_blocks = [block for step in far for block in pair[step]]
    produced = call(
        functools.partial(far_kernel, readers, tuple(far), tuple(offsets)),
        (pattern, self_key, self_value, *carried, *far_blocks),
        part_outputs,
        specs=[smem()] + [vmem()] * (6 + len(far_blocks)),
        scratch=[
            pltpu.VMEM((len(far_blocks) * size, local), BF16),
            pltpu.VMEM((len(far_blocks) * size, local), BF16),
            pltpu.VMEM((segs, far_keys, local), BF16),
            pltpu.VMEM((segs, far_keys, local), BF16),
            pltpu.VMEM((segs, spread_rows, 128), F32),
            pltpu.VMEM((segs, spread_rows, 128), F32),
            pltpu.VMEM((segs, spread_rows, local), F32),
        ]
        + work,
        estimate=cost(
            4 * segs * far_keys * local * spread_rows, 8 * segs * spread_rows * local
        ),
        limit=16 << 20,
    )
    mixed = combine(produced)
    mixed_other = swap_cores(mixed)
    return call(
        out_kernel,
        (hidden, mixed, mixed_other, self_out, self_out_other),
        [((segs, part, share), BF16)],
        estimate=cost(2 * size * width * share, 8 * size * width),
    )[0]


def solution(mesh):
    placed = (
        P(("grp", "pos"), None, None),
        P(("grp", "pos"), "read", None, None),
        P(("grp", "pos"), "read"),
        P(("grp", "pos"), "read"),
        P(("grp", "pos"), "read"),
        P(("grp", "pos"), None),
        P(None, "head"),
        P(None, "head"),
        P(None, "head"),
        P("head", None),
        P(None, "head"),
        P(None, "head"),
        P(None, "head"),
        P("head", None),
    )
    return jax.shard_map(
        layer,
        mesh=mesh,
        in_specs=placed,
        out_specs=P(("grp", "pos"), "read", "head"),
        check_vma=False,
    )
```

```python
import functools

import jax
import jax.numpy as jnp
from jax import lax
from jax.experimental import pallas as pl
from jax.experimental.pallas import tpu as pltpu
from jax.sharding import PartitionSpec as P


HD = 64
EPSILON = 1e-06
NEG = -1e30
CHUNK = 256
STATS = 128
STAT_ROWS = 16
ROWS = 16
F32 = jnp.float32
BF16 = jnp.bfloat16


def nt_dot(left, right):
    return lax.dot_general(left, right, (((1,), (1,)), ((), ())), preferred_element_type=F32)


def mm(left, right):
    return jnp.dot(left, right, preferred_element_type=F32)


def rms_rows(values):
    return values * lax.rsqrt(jnp.mean(values * values, axis=-1, keepdims=True) + EPSILON)


def spread_queries(query, heads, target):
    rows, width = query.shape
    lane = lax.broadcasted_iota(jnp.int32, (rows, 128), 1)
    for head in range(heads):
        inside = (lane >= HD) if head % 2 else (lane < HD)
        for tile in range(width // 128):
            cols = slice(tile * 128, (tile + 1) * 128)
            kept = jnp.zeros((rows, 128), BF16)
            if tile == head // 2:
                kept = jnp.where(inside, query[:, cols].astype(F32), 0.0).astype(BF16)
            target[head * rows : (head + 1) * rows, cols] = kept


def tile_fold(values, combine):
    folded = values[:, :128]
    for tile in range(1, values.shape[1] // 128):
        folded = combine(folded, values[:, tile * 128 : (tile + 1) * 128])
    return folded


def emit(segment, row_max, row_total, acc, heads, full, stat_full, own_ref, own_stat_ref, sends):
    readers = len(sends) + 1
    rows, width = full.shape
    part = rows // readers
    lane = lax.broadcasted_iota(jnp.int32, (rows, 128), 1)
    lane_head = lax.rem(lane, heads)

    def compact(values):
        packed = values[:rows]
        for head in range(1, heads):
            packed = jnp.where(lane_head == head, values[head * rows : (head + 1) * rows], packed)
        return packed

    divisor = jnp.where(row_total > 0, row_total, 1.0)
    packed_total = compact(row_total)
    level = jnp.where(
        packed_total > 0, compact(row_max) + jnp.log(jnp.where(packed_total > 0, packed_total, 1.0)),
        NEG,
    )
    for tile in range(width // 128):
        low = slice(2 * tile * rows, (2 * tile + 1) * rows)
        high = slice((2 * tile + 1) * rows, (2 * tile + 2) * rows)
        cols = slice(tile * 128, (tile + 1) * 128)
        full[:, cols] = jnp.where(lane < HD, acc[low, cols], acc[high, cols]) / jnp.where(
            lane < HD, divisor[low], divisor[high]
        )
    stats = jnp.zeros((rows, STATS), F32)
    for step in range(3):
        piece = level.astype(BF16).astype(F32)
        stats = jnp.where(lane // heads == step, piece, stats)
        level = level - piece
    stat_full[...] = stats
    flipped = stats.T[:STAT_ROWS]
    reader = lax.axis_index("read")
    for step in range(readers):
        first = pl.multiple_of(lax.rem(reader + step, readers) * part, part)
        if step == 0:
            own_ref[segment] = full[pl.ds(first, part), :]
            own_stat_ref[segment] = stat_full[pl.ds(first, part), :].astype(BF16)
        else:
            sends[step - 1][segment, :part, :] = full[pl.ds(first, part), :].astype(BF16)
            turned = pltpu.roll(flipped, lax.rem(rows - first, rows), 1)
            sends[step - 1][segment, part:, :] = jnp.concatenate(
                [turned, jnp.zeros((STAT_ROWS, width - rows), F32)], axis=1
            ).astype(BF16)


def cross_kernel(
    readers, start_hbm, cov_hbm, present_hbm, lat_hbm, tok_ref, wq_hbm, wk_hbm, wv_hbm, *rest
):
    own_ref, own_stat_ref = rest[:2]
    sends = rest[2 : 1 + readers]
    (start_ref, cov_ref, present_ref, seg_of, low_of, high_of, lat_ref, wq_ref, wk_ref, wv_ref,
     token_buf, spread, key_buf, score_buf, value_buf, max_buf, total_buf, acc, full, stat_full,
     load_sems, sems) = rest[1 + readers :]
    loads = [
        pltpu.make_async_copy(source, target, load_sems.at[index])
        for index, (source, target) in enumerate(
            (
                (start_hbm, start_ref),
                (cov_hbm, cov_ref),
                (present_hbm, present_ref),
                (lat_hbm, lat_ref),
                (wq_hbm, wq_ref),
                (wk_hbm, wk_ref),
                (wv_hbm, wv_ref),
            )
        )
    ]
    for load in loads:
        load.start()
    for load in loads[:3]:
        load.wait()
    segs, lat_rows, width = lat_ref.shape
    reads = tok_ref.shape[1]
    local = wq_ref.shape[1]
    heads = local // HD

    used = jnp.int32(0)
    for segment in range(segs):
        offset = used * CHUNK
        for read in range(reads):
            start = start_ref[segment, read]
            length = cov_ref[segment, read]
            live = present_ref[segment, read] > 0
            first = start & -ROWS
            last = (start + length + ROWS - 1) & -ROWS
            rows = pl.multiple_of(jnp.where(live, last - first, 0), ROWS)
            low_of[segment, read] = offset + start - first
            high_of[segment, read] = offset + jnp.where(live, start - first + length, 0)

            @pl.when(live)
            def _(segment=segment, read=read, offset=offset, first=first, rows=rows):
                pltpu.make_async_copy(
                    tok_ref.at[segment, read, pl.ds(pl.multiple_of(first, ROWS), rows), :],
                    token_buf.at[pl.ds(pl.multiple_of(offset, ROWS), rows), :],
                    sems.at[segment],
                ).start()

            offset = offset + rows
        low_of[segment, reads] = offset - used * CHUNK
        chunks = (offset - used * CHUNK + CHUNK - 1) // CHUNK

        def clear(step, carry, offset=offset):
            token_buf[pl.ds(pl.multiple_of(offset + step * ROWS, ROWS), ROWS), :] = jnp.zeros(
                (ROWS, width), BF16
            )
            return carry

        lax.fori_loop(0, ((used + chunks) * CHUNK - offset) // ROWS, clear, 0)

        def note(step, carry, segment=segment, used=used):
            seg_of[used + step] = segment
            return carry

        lax.fori_loop(0, chunks, note, 0)
        used = used + chunks
    for step in range(3):
        seg_of[used + step] = segs
    for read in range(reads):
        low_of[segs, read] = 0
        high_of[segs, read] = 0

    max_buf[:segs] = jnp.full((segs,) + max_buf.shape[1:], NEG, F32)
    total_buf[:segs] = jnp.zeros((segs,) + total_buf.shape[1:], F32)
    acc[:segs] = jnp.zeros((segs,) + acc.shape[1:], F32)
    for load in loads[3:]:
        load.wait()
    normed = rms_rows(lat_ref[...].reshape(segs * lat_rows, width).astype(F32)).astype(BF16)
    query = (mm(normed, wq_ref[...]) * (HD ** (-0.5))).astype(BF16)
    for segment in range(segs):
        spread_queries(
            query[segment * lat_rows : (segment + 1) * lat_rows], heads, spread.at[segment]
        )

    def landed(segment):
        size = pl.multiple_of(low_of[segment, reads], ROWS)
        whole = token_buf.at[pl.ds(0, size), :]
        pltpu.make_async_copy(whole, whole, sems.at[segment]).wait()

    def projected(pair):
        place = pl.ds(pl.multiple_of(pair * 2 * CHUNK, 2 * CHUNK), 2 * CHUNK)
        tokens = token_buf[place, :]
        key_buf[lax.rem(pair, 2)] = mm(tokens, wk_ref[...]).astype(BF16)
        value_buf[place, :] = mm(tokens, wv_ref[...]).astype(BF16)

    def arrive(chunk, before):
        upcoming = seg_of[chunk]

        @pl.when((upcoming != before) & (upcoming < segs))
        def _():
            landed(upcoming)

    pairs = (used + 1) // 2

    @pl.when(used > 0)
    def _():
        arrive(0, -1)
        arrive(1, seg_of[0])
        projected(jnp.int32(0))

    def first_pass(pair, carry):
        chunk = 2 * pair
        arrive(chunk + 2, seg_of[chunk + 1])
        arrive(chunk + 3, seg_of[chunk + 2])
        keys = key_buf[lax.rem(pair, 2)]
        segments = [seg_of[chunk], seg_of[chunk + 1]]
        for half in range(2):
            segment = segments[half]
            place = (chunk + half) * CHUNK + lax.broadcasted_iota(jnp.int32, (1, CHUNK), 1)
            live = jnp.zeros((1, CHUNK), jnp.bool_)
            for read in range(reads):
                live = live | (
                    (place >= low_of[segment, read]) & (place < high_of[segment, read])
                )
            for block in range(2):
                size = acc.shape[1] // 2
                rows = slice(block * size, (block + 1) * size)
                scores = nt_dot(
                    spread[segment, rows], keys[half * CHUNK : (half + 1) * CHUNK]
                )
                scores = jnp.where(live, scores, NEG)
                score_buf[chunk + half, rows] = scores
                max_buf[segment, rows] = jnp.maximum(
                    max_buf[segment, rows], tile_fold(scores, jnp.maximum)
                )
        projected(pair + 1)
        return carry

    lax.fori_loop(0, pairs, first_pass, 0)
    for segment in range(segs):
        row_max = jnp.max(max_buf[segment], axis=1, keepdims=True)
        max_buf[segment] = jnp.broadcast_to(row_max, max_buf.shape[1:])

    def second_pass(pair, carry):
        for half in range(2):
            chunk = 2 * pair + half
            segment = seg_of[chunk]
            value = value_buf[pl.ds(pl.multiple_of(chunk * CHUNK, CHUNK), CHUNK), :]
            for block in range(2):
                rows = slice(block * acc.shape[1] // 2, (block + 1) * acc.shape[1] // 2)
                weights = jnp.exp(
                    score_buf[chunk, rows] - jnp.tile(max_buf[segment, rows], (1, CHUNK // 128))
                )
                total_buf[segment, rows] += tile_fold(weights, jnp.add)
                acc[segment, rows] += mm(weights.astype(BF16), value)
        return carry

    lax.fori_loop(0, pairs, second_pass, 0)

    for segment in range(segs):
        row_total = jnp.sum(total_buf[segment], axis=1, keepdims=True)
        emit(
            segment, max_buf[segment], jnp.broadcast_to(row_total, total_buf.shape[1:]),
            acc.at[segment], heads, full.at[segment], stat_full.at[segment], own_ref,
            own_stat_ref, sends,
        )


def pick_heads(rows, width):
    heads = width // HD
    place = lax.broadcasted_iota(jnp.int32, (rows, width), 0)
    head = lax.broadcasted_iota(jnp.int32, (rows, width), 1) // HD
    return ((lax.rem(place, heads) == head) & (place < 3 * heads)).astype(F32).astype(BF16)


def own_kernel(own_ref, stat_ref, kept_ref, level_ref):
    kept_ref[...] = own_ref[...]
    level_ref[...] = mm(stat_ref[...], pick_heads(STATS, own_ref.shape[1]))


def combine_kernel(each, *refs):
    out_ref = refs[-1]
    width = out_ref.shape[1]
    pick = pick_heads(STAT_ROWS, width)
    done = 0
    for group in range(0, len(refs) - 1, each):
        own_ref, level_ref = refs[group : group + 2]
        received = refs[group + 2 : group + each]
        segs = received[0].shape[0]
        part = own_ref.shape[0] // segs
        for segment in range(segs):
            rows = slice(segment * part, (segment + 1) * part)
            parts, levels = [own_ref[rows, :]], [level_ref[rows, :]]
            for ref in received:
                parts.append(ref[segment, :part, :].astype(F32))
                stats = ref[segment, part:, :STATS]
                levels.append(
                    lax.dot_general(
                        stats, pick, (((0,), (0,)), ((), ())), preferred_element_type=F32
                    )[:part]
                )
            joint = functools.reduce(jnp.maximum, levels)
            factors = [jnp.exp(level - joint) for level in levels]
            mixed = sum(value * factor for value, factor in zip(parts, factors))
            out_ref[done : done + part, :] = (mixed / sum(factors)).astype(BF16)
            done += part


def hidden_kernel(
    lat_ref, own_ref, other_ref, wo_ref, wp_ref, wq_ref, hid_ref, norm_ref, query_ref
):
    segs, _, _ = lat_ref.shape
    part = own_ref.shape[0] // segs
    first = pl.multiple_of(lax.axis_index("read") * part, part)
    delta = mm(own_ref[...], wo_ref[...]) + mm(other_ref[...], wp_ref[...])
    for segment in range(segs):
        rows = slice(segment * part, (segment + 1) * part)
        hid_ref[rows, :] = lat_ref[segment, pl.ds(first, part), :].astype(F32) + delta[rows]
    normed = rms_rows(hid_ref[...]).astype(BF16)
    norm_ref[...] = normed
    query_ref[...] = (mm(normed, wq_ref[...]) * (HD ** (-0.5))).astype(BF16)


def project_blocks(blocks, slots, wk_ref, wv_ref, key_all, value_all):
    for block, slot in zip(blocks, slots):
        size = block.shape[0]
        place = pl.ds(pl.multiple_of(slot * size, size), size)
        key_all[place, :] = mm(block[...], wk_ref[...]).astype(BF16)
        value_all[place, :] = mm(block[...], wv_ref[...]).astype(BF16)


def collect(segment, segs, part, slot_of, offsets, pattern_ref, sources, targets):
    seg_total = pattern_ref.shape[1]
    home = lax.axis_index("pos") * segs + segment
    live = jnp.int32(0)
    for offset in offsets:
        block_step, inner = divmod(segment + offset, segs)
        if block_step not in slot_of:
            continue
        inside = (home + offset >= 0) & (home + offset < seg_total)
        flag = pattern_ref[segment, jnp.clip(home + offset, 0, seg_total - 1)]
        chosen = inside & (flag > 0)
        source = (slot_of[block_step] * segs + inner) * part

        place = pl.ds(pl.multiple_of(live * part, part), part)
        for whole, packed in zip(sources, targets):
            packed[place, :] = whole[source : source + part, :]
        live = live + chosen.astype(jnp.int32)
    return live


def near_kernel(readers, offsets, pattern_ref, wk_ref, wv_ref, *rest):
    queries = rest[:readers]
    own, ahead, behind = rest[readers : readers + 3]
    spread, max_out, total_out, acc = rest[readers + 3 : readers + 7]
    query_buf, key_all, value_all, key_buf, value_buf = rest[readers + 7 :]
    segs, _, local = spread.shape
    lat_rows = query_buf.shape[1]
    part = lat_rows // readers
    heads = local // HD
    reader = lax.axis_index("read")
    core = lax.axis_index("head")

    key_buf[...] = jnp.zeros(key_buf.shape, BF16)
    value_buf[...] = jnp.zeros(value_buf.shape, BF16)
    project_blocks(
        (own, ahead, behind), (0, 1 + core, 2 - core), wk_ref, wv_ref, key_all, value_all
    )
    for step in range(readers):
        first = pl.multiple_of(lax.rem(reader + readers - step, readers) * part, part)
        for segment in range(segs):
            query_buf[segment, pl.ds(first, part), :] = queries[step][
                segment * part : (segment + 1) * part, :
            ]

    for segment in range(segs):
        spread_queries(query_buf[segment], heads, spread.at[segment])
    counts = [
        collect(
            segment, segs, part, {0: 0, -1: 1, 1: 2}, offsets, pattern_ref,
            (key_all, value_all), (key_buf.at[segment], value_buf.at[segment]),
        )
        for segment in range(segs)
    ]

    def weigh(segment, base, before):
        keys = slice(base, base + CHUNK)
        place = base + lax.broadcasted_iota(jnp.int32, (1, CHUNK), 1)
        scores = nt_dot(spread[segment], key_buf[segment, keys])
        scores = jnp.where(place < counts[segment] * part, scores, NEG)
        top = jnp.max(tile_fold(scores, jnp.maximum), axis=1, keepdims=True)
        peak = jnp.broadcast_to(top, max_out.shape[1:])
        if before is not None:
            peak = jnp.maximum(peak, before)
        weights = jnp.exp(scores - jnp.tile(peak, (1, CHUNK // 128)))
        update = mm(weights.astype(BF16), value_buf[segment, keys])
        return peak, tile_fold(weights, jnp.add), update

    for segment in range(segs):
        max_out[segment], total_out[segment], acc[segment] = weigh(segment, 0, None)
    for segment in range(segs):
        for base in range(CHUNK, key_buf.shape[1], CHUNK):

            @pl.when(counts[segment] * part > base)
            def _(segment=segment, base=base):
                before = max_out[segment]
                peak, totals, update = weigh(segment, base, before)
                factor = jnp.exp(before - peak)
                max_out[segment] = peak
                total_out[segment] = total_out[segment] * factor + totals
                acc[segment] = acc[segment] * jnp.tile(factor, (1, local // 128)) + update


def far_kernel(readers, steps, offsets, base, pattern_ref, *rest):
    spread, max_in, total_in, acc_in = rest[:4]
    rest = rest[4:]
    projects = base == 0
    if projects:
        wk_ref, wv_ref = rest[:2]
        blocks = rest[2 : 2 + 2 * len(steps)]
        rest = rest[2 + 2 * len(steps) :]
    else:
        key_all, value_all = rest[:2]
        rest = rest[2:]
    own_ref, own_stat_ref = rest[:2]
    sends = rest[2 : 1 + readers]
    rest = rest[1 + readers :]
    if projects:
        key_all, value_all = rest[:2]
        rest = rest[2:]
    key_buf, value_buf, max_buf, total_buf, acc, full, stat_full = rest
    segs, _, local = spread.shape
    heads = local // HD
    part = own_ref.shape[1]
    core = lax.axis_index("head")
    many = key_buf.shape[1]

    key_buf[...] = jnp.zeros(key_buf.shape, BF16)
    value_buf[...] = jnp.zeros(value_buf.shape, BF16)
    slots, slot_of = [], {}
    for index, step in enumerate(steps):
        slots += [2 * index + core, 2 * index + 1 - core]
        slot_of[-step], slot_of[step] = 2 * index, 2 * index + 1
    if projects:
        project_blocks(blocks, slots, wk_ref, wv_ref, key_all, value_all)
    held = own_ref.shape[0]
    counts = [
        collect(
            base + segment, segs, part, slot_of, offsets, pattern_ref,
            (key_all, value_all), (key_buf.at[segment], value_buf.at[segment]),
        )
        for segment in range(held)
    ]

    for segment in range(held):
        place = lax.broadcasted_iota(jnp.int32, (1, many), 1)
        scores = nt_dot(spread[base + segment], key_buf[segment])
        scores = jnp.where(place < counts[segment] * part, scores, NEG)
        before = max_in[base + segment]
        top = jnp.max(tile_fold(scores, jnp.maximum), axis=1, keepdims=True)
        peak = jnp.maximum(before, jnp.broadcast_to(top, before.shape))
        max_buf[segment] = peak
        factor = jnp.exp(before - peak)
        weights = jnp.exp(scores - jnp.tile(peak, (1, many // 128)))
        row_total = jnp.sum(
            total_in[base + segment] * factor + tile_fold(weights, jnp.add), axis=1, keepdims=True
        )
        total_buf[segment] = jnp.broadcast_to(row_total, before.shape)
        acc[segment] = acc_in[base + segment] * jnp.tile(factor, (1, local // 128)) + mm(
            weights.astype(BF16), value_buf[segment]
        )
    for segment in range(held):
        emit(
            segment, max_buf[segment], total_buf[segment], acc.at[segment], heads,
            full.at[segment], stat_full.at[segment], own_ref, own_stat_ref, sends,
        )


def out_kernel(hid_ref, own_ref, other_ref, wo_ref, wp_ref, out_ref):
    segs, part, share = out_ref.shape
    cols = pl.ds(pl.multiple_of(lax.axis_index("head") * share, 128), share)
    result = (
        hid_ref[:, cols] + mm(own_ref[...], wo_ref[:, cols]) + mm(other_ref[...], wp_ref[:, cols])
    )
    for segment in range(segs):
        out_ref[segment] = result[segment * part : (segment + 1) * part].astype(BF16)


def cost(flops, moved, exps=0):
    return pl.CostEstimate(flops=int(flops), bytes_accessed=int(moved), transcendentals=int(exps))


def vmem():
    return pl.BlockSpec(memory_space=pltpu.VMEM)


def smem():
    return pl.BlockSpec(memory_space=pltpu.SMEM)


def call(kernel, inputs, outputs, specs=None, scratch=(), estimate=None, limit=8 << 20):
    return pl.pallas_call(
        kernel,
        out_shape=[jax.ShapeDtypeStruct(shape, kind) for shape, kind in outputs],
        in_specs=specs or [vmem() for _ in inputs],
        out_specs=[vmem() for _ in outputs],
        scratch_shapes=list(scratch),
        cost_estimate=estimate,
        compiler_params=pltpu.CompilerParams(vmem_limit_bytes=limit),
    )(*inputs)


def swap_cores(value):
    return lax.ppermute(value, "head", [(0, 1), (1, 0)])


def to_reader(value, step):
    readers = lax.axis_size("read")
    return lax.ppermute(value, "read", [(i, (i + step) % readers) for i in range(readers)])


def both_ways(value, step):
    count = lax.axis_size("pos")
    ring = [2 * place for place in range(count)]
    ring += [2 * place + 1 for place in reversed(range(count))]
    moves = [(ring[i], ring[(i + step) % len(ring)]) for i in range(len(ring))]
    return lax.ppermute(value, ("pos", "head"), moves)


def layer(
    latents, read_tokens, band_start, coverage, present, pattern, cross_query, cross_key,
    cross_value, cross_out, self_query, self_key, self_value, self_out,
):
    segs, lat_rows, width = latents.shape
    reads, length = read_tokens.shape[1:3]
    local = cross_query.shape[1]
    heads = local // HD
    readers = lax.axis_size("read")
    part = lat_rows // readers
    size = segs * part
    seg_total = pattern.shape[1]
    share = width // lax.axis_size("head")
    spread_rows = heads * lat_rows

    offsets = [0]
    distance = 1
    while distance < seg_total:
        offsets += [distance, -distance]
        distance *= 2
    steps = sorted(
        {abs((seg + off) // segs) for off in offsets for seg in range(segs)} - {0}
    )

    cross_out_other = swap_cores(cross_out)
    self_out_other = swap_cores(self_out)


    def part_outputs(held):
        return [((held, part, local), F32), ((held, part, STATS), BF16)] + [
            ((held, part + STAT_ROWS, local), BF16)
        ] * (readers - 1)

    work = [pltpu.VMEM((segs, lat_rows, local), F32), pltpu.VMEM((segs, lat_rows, STATS), F32)]
    most = reads * length
    tiles = -(-most // CHUNK)
    spare = (segs * tiles + 1) // 2 * 2 + 2
    produced = call(
        functools.partial(cross_kernel, readers),
        (band_start, coverage, present, latents, read_tokens, cross_query, cross_key, cross_value),
        part_outputs(segs),
        specs=[pl.BlockSpec(memory_space=pltpu.HBM)] * 8,
        scratch=[
            pltpu.SMEM(band_start.shape, jnp.int32),
            pltpu.SMEM(coverage.shape, jnp.int32),
            pltpu.SMEM(present.shape, jnp.int32),
            pltpu.SMEM((segs * tiles + 3,), jnp.int32),
            pltpu.SMEM((segs + 1, reads + 1), jnp.int32),
            pltpu.SMEM((segs + 1, reads), jnp.int32),
            pltpu.VMEM(latents.shape, BF16),
            pltpu.VMEM(cross_query.shape, BF16),
            pltpu.VMEM(cross_key.shape, BF16),
            pltpu.VMEM(cross_value.shape, BF16),
            pltpu.VMEM((spare * CHUNK, width), BF16),
            pltpu.VMEM((segs + 1, spread_rows, local), BF16),
            pltpu.VMEM((2, 2 * CHUNK, local), BF16),
            pltpu.VMEM((segs * tiles + 1, spread_rows, CHUNK), F32),
            pltpu.VMEM((spare * CHUNK, local), BF16),
            pltpu.VMEM((segs + 1, spread_rows, 128), F32),
            pltpu.VMEM((segs + 1, spread_rows, 128), F32),
            pltpu.VMEM((segs + 1, spread_rows, local), F32),
        ]
        + work
        + [pltpu.SemaphoreType.DMA((7,)), pltpu.SemaphoreType.DMA((segs,))],
        estimate=cost(
            2 * segs * most * local * (2 * width + 2 * spread_rows),
            2 * segs * most * width,
            segs * most * spread_rows,
        ),
        limit=60 * 1024 * 1024,
    )

    def combine(groups):
        inputs = []
        for parts in groups:
            own, own_stat, sends = parts[0], parts[1], parts[2:]
            rows = own.shape[0] * part
            received = [to_reader(value, step + 1) for step, value in enumerate(sends)]
            kept, level = call(
                own_kernel,
                (own.reshape(rows, local), own_stat.reshape(rows, STATS)),
                [((rows, local), F32), ((rows, local), F32)],
                estimate=cost(2 * rows * STATS * local, 12 * rows * local),
            )
            inputs += [kept, level] + received
        return call(
            functools.partial(combine_kernel, 1 + readers),
            inputs,
            [((size, local), BF16)],
            estimate=cost(8 * size * STATS * local, 8 * size * local),
        )[0]

    attended = combine([produced])
    attended_other = swap_cores(attended)
    hidden, normed, query = call(
        hidden_kernel,
        (latents, attended, attended_other, cross_out, cross_out_other, self_query),
        [((size, width), F32), ((size, width), BF16), ((size, local), BF16)],
        estimate=cost(2 * size * width * (width + local), 8 * size * width),
    )
    queries = [query] + [to_reader(query, step) for step in range(1, readers)]
    direct, pair = {}, {}
    for step in steps:
        half = step // 2
        if half in direct and 2 * half == step:
            direct[step] = both_ways(direct[half], half)
        else:
            direct[step] = both_ways(normed, step)
        pair[step] = (direct[step], swap_cores(direct[step]))
    state = [
        ((segs, spread_rows, local), BF16),
        ((segs, spread_rows, 128), F32),
        ((segs, spread_rows, 128), F32),
        ((segs, spread_rows, local), F32),
    ]

    def reach(test):
        return max(
            sum(test(abs((segment + offset) // segs)) for offset in offsets)
            for segment in range(segs)
        )

    near_keys = -(-reach(lambda step: step <= 1) * part // CHUNK) * CHUNK
    far_keys = -(-reach(lambda step: step > 1) * part // 128) * 128
    carried = call(
        functools.partial(near_kernel, readers, tuple(offsets)),
        (pattern, self_key, self_value, *queries, normed, *pair[1]),
        state,
        specs=[smem()] + [vmem()] * (5 + len(queries)),
        scratch=[
            pltpu.VMEM((segs, lat_rows, local), BF16),
            pltpu.VMEM((3 * size, local), BF16),
            pltpu.VMEM((3 * size, local), BF16),
            pltpu.VMEM((segs, near_keys, local), BF16),
            pltpu.VMEM((segs, near_keys, local), BF16),
        ],
        estimate=cost(4 * segs * near_keys * local * spread_rows, 8 * segs * spread_rows * local),
        limit=16 << 20,
    )
    far = [step for step in steps if step > 1]
    far_blocks = [block for step in far for block in pair[step]]
    keys_shape = (len(far_blocks) * size, local)
    groups, projected = [], None
    half = segs // 2
    for index, (base, held) in enumerate(((0, half), (half, segs - half))):
        inputs = (pattern, *carried)
        inputs += (self_key, self_value, *far_blocks) if index == 0 else projected
        produced = call(
            functools.partial(far_kernel, readers, tuple(far), tuple(offsets), base),
            inputs,
            part_outputs(held) + [(keys_shape, BF16)] * (2 if index == 0 else 0),
            specs=[smem()] + [vmem()] * (len(inputs) - 1),
            scratch=[
                pltpu.VMEM((held, far_keys, local), BF16),
                pltpu.VMEM((held, far_keys, local), BF16),
                pltpu.VMEM((held, spread_rows, 128), F32),
                pltpu.VMEM((held, spread_rows, 128), F32),
                pltpu.VMEM((held, spread_rows, local), F32),
                pltpu.VMEM((held, lat_rows, local), F32),
                pltpu.VMEM((held, lat_rows, STATS), F32),
            ],
            estimate=cost(
                4 * held * far_keys * local * spread_rows, 8 * held * spread_rows * local
            ),
            limit=16 << 20,
        )
        if index == 0:
            projected = tuple(produced[1 + readers :])
        groups.append(produced[: 1 + readers])
    mixed = combine(groups)
    mixed_other = swap_cores(mixed)
    return call(
        out_kernel,
        (hidden, mixed, mixed_other, self_out, self_out_other),
        [((segs, part, share), BF16)],
        estimate=cost(2 * size * width * share, 8 * size * width),
    )[0]


def solution(mesh):
    placed = (
        P(("grp", "pos"), None, None),
        P(("grp", "pos"), "read", None, None),
        P(("grp", "pos"), "read"),
        P(("grp", "pos"), "read"),
        P(("grp", "pos"), "read"),
        P(("grp", "pos"), None),
        P(None, "head"),
        P(None, "head"),
        P(None, "head"),
        P("head", None),
        P(None, "head"),
        P(None, "head"),
        P(None, "head"),
        P("head", None),
    )
    return jax.shard_map(
        layer,
        mesh=mesh,
        in_specs=placed,
        out_specs=P(("grp", "pos"), "read", "head"),
        check_vma=False,
    )
```
